256 devices in a mesh: ctx: 32 (over x, z), head: 8 (over y, core).
Axes of the slice: x: 4, y: 4, z: 8, core: 2. Of those that a mesh axis runs over, the one named last changes fastest.
Arguments:
- activations: bfloat16 [32768, 2048], P('ctx', 'head'), may hold values from -6 to 6
- w_query: bfloat16 [2048, 2048], P('ctx', 'head'), may hold values from -0.125 to 0.125
- w_key: bfloat16 [2048, 2048], P('ctx', 'head'), may hold values from -0.125 to 0.125
- w_value: bfloat16 [2048, 2048], P('ctx', 'head'), may hold values from -0.125 to 0.125
- level_table: float32 [16, 64, 16], P('head'), may hold values from 0.2 to 2
- table_rows: int32 [32768], P('ctx'), may hold values from 0 to 63
- out_grad: bfloat16 [32768, 2048], P('ctx', 'head'), may hold values from -0.059814453 to 0.059814453
Outputs:
- attended: bfloat16 [32768, 2048], P('ctx', 'head')
- grad_query: float32 [2048, 2048], P('ctx', 'head')
- grad_key: float32 [2048, 2048], P('ctx', 'head')
- grad_value: float32 [2048, 2048], P('ctx', 'head')
The draws below stay inside these ranges and needn't reach their ends.
All inputs are finite; a program needn't handle non-finite values.
Results may differ from the reference program's by a relative error of at most 0.0056.
Values may be sent and summed in bfloat16 or wider, within the bound.
No kernel may reach another device: no remote copies, remote signals or barrier semaphores. Data moves between devices by JAX's collectives and lax.ppermute only.
A program may use at most 64 MiB of HBM per device.

```python
import math
import jax
import jax.numpy as jnp
from jax import lax

D = 2048
HEADS = 16
HEAD_DIM = 128
TABLE = 64
TOK_DEV = 1024
TOKENS = 32768
LEVELS = 16


def plant(entries, stream_key, low, top_value):
    longest = entries.shape.index(max(entries.shape))
    spots = []
    for shift in (0, 1):
        where = [jax.random.randint(jax.random.fold_in(stream_key, axis), (), 0, length) for axis, length in enumerate(entries.shape)]
        where[longest] = (where[longest] + shift) % entries.shape[longest]
        spots.append(tuple(where))
    return entries.at[spots[0]].set(low).at[spots[1]].set(top_value)


def spiked(array, own_key, source, target, parts, factor):
    owner, partner = [(jnp.arange(array.shape[axis_at]) // (array.shape[axis_at] // parts)).reshape([-1 if axis == axis_at else 1 for axis in range(array.ndim)]) for axis_at in (source, target)]
    chosen = jax.random.permutation(own_key, parts)[partner]
    strong = (owner == chosen) | (owner == (partner + parts // 2) % parts)
    return jnp.where(strong, factor * array, array)


def shard_levels(stream_key, extent, split, least, top_value):
    gain = 1.0
    for position, blocks in split:
        heights = jax.random.uniform(jax.random.fold_in(jax.random.fold_in(stream_key, 6), position), (blocks,), jnp.float32, least / len(split), top_value / len(split))
        gain = gain * jnp.repeat(jnp.exp(heights), extent[position] // blocks).reshape((-1,) + (1,) * (len(extent) - 1 - position))
    return gain


def gaussian(stream_key, extent, deviation, reach, shards=(), kind=jnp.bfloat16):
    values = deviation * jax.random.normal(stream_key, extent, jnp.float32)
    if shards:
        values = values * shard_levels(stream_key, extent, shards, -0.22, 0.18)
    return jnp.clip(values, -reach, reach).astype(kind)


def heavy_noise(rng, extent, width, reach, split, heavy, held_as=jnp.bfloat16):
    array = width * jax.random.normal(rng, extent, jnp.float32)
    if split:
        array = array * shard_levels(rng, extent, split, -0.22, 0.18)
    return jnp.clip(spiked(array, jax.random.fold_in(rng, 3), *heavy), -reach, reach).astype(held_as)


def setup_inputs(seed: int = 0) -> dict:
    key_list = jax.random.split(jax.random.key(seed), 8)
    activations = heavy_noise(key_list[0], (TOKENS, D), 1.0, 6.0, ((0, 32), (1, 8)), (0, 1, 32, 2.75))
    w_query = gaussian(key_list[1], (D, HEADS * HEAD_DIM), D ** -0.5, 0.125, ((0, 32), (1, 8)))
    w_key = gaussian(key_list[2], (D, HEADS * HEAD_DIM), D ** -0.5, 0.125, ((0, 32), (1, 8)))
    w_value = gaussian(key_list[3], (D, HEADS * HEAD_DIM), D ** -0.5, 0.125, ((0, 32), (1, 8)))
    level_table = jnp.clip(jnp.exp(math.log(2.0) - 2.3025851 * jax.random.uniform(key_list[4], (HEADS, TABLE, LEVELS), jnp.float32) ** shard_levels(key_list[4], (HEADS, TABLE, LEVELS), ((0, 8),), -0.2, 0.2)), 0.2, 2.0)
    table_rows = plant(jax.random.randint(key_list[5], (TOKENS,), 0, TABLE), jax.random.fold_in(key_list[5], 1), 0, TABLE - 1).astype(jnp.int32)
    out_grad = gaussian(key_list[6], (TOKENS, HEADS * HEAD_DIM), 0.01, 0.059814453, ((0, 32), (1, 8)))
    return {"activations": activations, "w_query": w_query, "w_key": w_key, "w_value": w_value, "level_table": level_table, "table_rows": table_rows, "out_grad": out_grad}


def level_of(distance, bit_total):
    running = jnp.zeros(distance.shape, jnp.int32)
    for bit_num in range(bit_total):
        running = running + (distance >= 1 << bit_num).astype(jnp.int32)
    return running

def reference(activations, w_query, w_key, w_value, level_table, table_rows, out_grad):
    blocks = TOKENS // TOK_DEV
    inner_bits = int(TOK_DEV).bit_length() - 1
    outer_bits = int(blocks).bit_length() - 1
    scale_factor = 1.0 / math.sqrt(HEAD_DIM * TOK_DEV)
    highest = lax.Precision.HIGHEST
    queries = jnp.dot(activations, w_query, preferred_element_type=jnp.float32).astype(jnp.bfloat16)
    keys = jnp.dot(activations, w_key, preferred_element_type=jnp.float32).astype(jnp.bfloat16)
    values = jnp.dot(activations, w_value, preferred_element_type=jnp.float32).astype(jnp.bfloat16)
    onehot = (table_rows[:, None] == jnp.arange(TABLE, dtype=jnp.int32)[None, :]).astype(jnp.float32)
    lam = jnp.einsum('tr,hrl->thl', onehot, level_table, precision=highest)
    block_shape = (blocks, TOK_DEV, HEADS, HEAD_DIM)
    query_blocks = queries.reshape(block_shape)
    key_blocks = keys.reshape(block_shape)
    value_blocks = values.reshape(block_shape)
    grad_blocks = out_grad.reshape(block_shape)
    lam_blocks = lam.reshape(blocks, TOK_DEV, HEADS, LEVELS)
    positions = jnp.arange(TOK_DEV, dtype=jnp.int32)
    pair_level = level_of(jnp.bitwise_xor(positions[:, None], positions[None, :]), inner_bits + 1)
    causal = positions[:, None] >= positions[None, :]

    def near_block(pieces):
        query_here, key_here, value_here, grad_here, lam_here = pieces
        level_mix = jnp.zeros((HEADS, TOK_DEV, TOK_DEV), jnp.float32)
        for level_num in range(inner_bits + 1):
            level_mix = jnp.where(pair_level[None] == level_num, jnp.transpose(lam_here[:, :, level_num])[:, :, None], level_mix)
        level_mix = jnp.where(causal[None], level_mix * scale_factor, 0.0)
        query_wide = query_here.astype(jnp.float32)
        key_wide = key_here.astype(jnp.float32)
        value_wide = value_here.astype(jnp.float32)
        grad_wide = grad_here.astype(jnp.float32)
        scores = jnp.einsum('thd,shd->hts', query_wide, key_wide)
        attn_probs = (level_mix * scores).astype(jnp.bfloat16).astype(jnp.float32)
        near_out = jnp.einsum('hts,she->the', attn_probs, value_wide)
        grad_scores = jnp.einsum('the,she->hts', grad_wide, value_wide)
        grad_mixed = (level_mix * grad_scores).astype(jnp.bfloat16).astype(jnp.float32)
        query_near = jnp.einsum('hts,shd->thd', grad_mixed, key_wide)
        key_near = jnp.einsum('hts,thd->shd', grad_mixed, query_wide)
        value_near = jnp.einsum('hts,the->she', attn_probs, grad_wide)
        return (near_out, query_near, key_near, value_near)
    near_out, query_near, key_near, value_near = lax.map(near_block, (query_blocks, key_blocks, value_blocks, grad_blocks, lam_blocks))
    query_wide = query_blocks.astype(jnp.float32)
    key_wide = key_blocks.astype(jnp.float32)
    value_wide = value_blocks.astype(jnp.float32)
    grad_wide = grad_blocks.astype(jnp.float32)
    local_states = jnp.einsum('bthd,bthe->bhde', key_wide, value_wide)
    peer_index = jnp.arange(blocks, dtype=jnp.int32)
    peer_level = level_of(jnp.bitwise_xor(peer_index[:, None], peer_index[None, :]), outer_bits + 1)
    earlier = peer_index[None, :] < peer_index[:, None]
    far_out = jnp.zeros(block_shape, jnp.float32)
    query_far = jnp.zeros(block_shape, jnp.float32)
    incoming = jnp.zeros((blocks, HEADS, HEAD_DIM, HEAD_DIM), jnp.float32)
    for bit_num in range(outer_bits):
        member = ((peer_level == bit_num + 1) & earlier).astype(jnp.float32)
        level_sum = jnp.einsum('de,ehij->dhij', member, local_states, precision=highest)
        level_state = lax.optimization_barrier(level_sum.astype(jnp.bfloat16)).astype(jnp.float32)
        level_weight = lam_blocks[:, :, :, inner_bits + 1 + bit_num]
        far_out = far_out + scale_factor * level_weight[..., None] * jnp.einsum('bthd,bhde->bthe', query_wide, level_state)
        query_far = query_far + scale_factor * level_weight[..., None] * jnp.einsum('bthe,bhde->bthd', grad_wide, level_state)
        scaled_query = lax.optimization_barrier(((scale_factor * level_weight)[..., None] * query_wide).astype(jnp.bfloat16)).astype(jnp.float32)
        grad_state = jnp.einsum('bthd,bthe->bhde', scaled_query, grad_wide)
        incoming = incoming + jnp.einsum('de,dhij->ehij', member, grad_state, precision=highest)
    back_state = lax.optimization_barrier(incoming.astype(jnp.bfloat16)).astype(jnp.float32)
    key_far = jnp.einsum('bthe,bhde->bthd', value_wide, back_state)
    value_far = jnp.einsum('bthd,bhde->bthe', key_wide, back_state)
    flat = (TOKENS, HEADS * HEAD_DIM)
    attended = (near_out + far_out).astype(jnp.bfloat16).reshape(flat)
    query_total = (query_near + query_far).astype(jnp.bfloat16).reshape(flat)
    key_total = (key_near + key_far).astype(jnp.bfloat16).reshape(flat)
    value_total = (value_near + value_far).astype(jnp.bfloat16).reshape(flat)
    grad_query = jnp.dot(activations.T, query_total, preferred_element_type=jnp.float32)
    grad_key = jnp.dot(activations.T, key_total, preferred_element_type=jnp.float32)
    grad_value = jnp.dot(activations.T, value_total, preferred_element_type=jnp.float32)
    return (attended, grad_query, grad_key, grad_value)
```

```python
import functools
import math

import jax
import jax.numpy as jnp
from jax import lax
from jax.experimental import pallas as pl
from jax.experimental.pallas import tpu as pltpu
from jax.sharding import Mesh
from jax.sharding import PartitionSpec as P

F32 = jnp.float32
BF16 = jnp.bfloat16
VMEM_LIMIT = 48 * 1024 * 1024

TOK = 1024
WIDTH = 2048
COLS = 256
HD = 128
HEADS_HERE = 2
LEVELS = 16
NEAR = 11
FAR = 5
XN, ZN, YN = 4, 8, 4
PIECE = WIDTH // (XN * ZN)


def shifted(value, axis, offset):
    count = lax.axis_size(axis)
    return lax.ppermute(value, axis, [(i, (i + offset) % count) for i in range(count)])


def swapped(value, axis, bit):
    count = lax.axis_size(axis)
    return lax.ppermute(value, axis, [(i, i ^ bit) for i in range(count)])


def ring_of(value, axis):
    found = [(0, value)]
    up = down = value
    for step in range(1, 5):
        up = shifted(up, axis, 1)
        found.append((-step, up))
        if step < 4:
            down = shifted(down, axis, -1)
            found.append((step, down))
    return found


def features_of(block):
    up = shifted(block, "y", 1)
    down = shifted(block, "y", -1)
    far = shifted(up, "y", 1)
    mine = [(0, block), (-1, up), (1, down), (-2, far)]
    found = [(off, True, part) for off, part in mine]
    found += [(off, False, shifted(part, "core", 1)) for off, part in mine]
    return found


def dot(a, b):
    return lax.dot_general(a, b, (((1,), (0,)), ((), ())), preferred_element_type=F32)


def dot_nt(a, b):
    return lax.dot_general(a, b, (((1,), (1,)), ((), ())), preferred_element_type=F32)


def dot_tn(a, b):
    return lax.dot_general(a, b, (((0,), (0,)), ((), ())), preferred_element_type=F32)


def feature_copies(tags, refs, scratch, sem):
    y = lax.axis_index("y")
    core = lax.axis_index("core")
    copies = []
    for i, ((off, same), ref) in enumerate(zip(tags, refs)):
        block = lax.rem(y + (off + YN), YN) * 2 + (core if same else 1 - core)
        cols = pl.ds(pl.multiple_of(block * COLS, COLS), COLS)
        copies.append(pltpu.make_async_copy(ref, scratch.at[:, cols], sem.at[i]))
    return copies


def weight_copies(tags, refs, scratch, sem):
    x = lax.axis_index("x")
    z = lax.axis_index("z")
    copies = []
    for i, (off, ref) in enumerate(zip(tags, refs)):
        zz = lax.rem(z + (off + ZN), ZN)
        for rx in range(XN):
            xx = lax.rem(x + rx, XN)
            rows = pl.ds(pl.multiple_of((xx * ZN + zz) * PIECE, PIECE), PIECE)
            src = ref.at[pl.ds(rx * PIECE, PIECE), :]
            copies.append(pltpu.make_async_copy(src, scratch.at[rows, :], sem.at[i, rx]))
    return copies


def begin(copies):
    for copy in copies:
        copy.start()


def finish(copies):
    for copy in copies:
        copy.wait()


def query_kernel(ftags, wtags, *refs):
    nf, nw = len(ftags), len(wtags)
    fr, wr = refs[:nf], refs[nf : nf + nw]
    g_ref, lam_ref, q_ref, state_ref, a_s, w_s, fsem, wsem = refs[nf + nw :]
    fc = feature_copies(ftags, fr, a_s, fsem)
    wc = weight_copies(wtags, wr, w_s, wsem)
    begin(fc + wc)
    finish(fc + wc)
    for r in range(0, TOK, 256):
        rows = pl.ds(r, 256)
        q_ref[rows, :] = dot(a_s[rows, :], w_s[...]).astype(BF16)
    for h in range(HEADS_HERE):
        cols = pl.ds(h * HD, HD)
        q = q_ref[:, cols].astype(F32)
        scaled = []
        for b in range(FAR):
            at = h * LEVELS + NEAR + b
            scaled.append((lam_ref[:, at : at + 1] * q).astype(BF16))
        g = g_ref[:, cols]
        for b in range(FAR):
            state_ref[b, h] = dot_tn(scaled[b], g)


def key_value_kernel(ftags, wtags, *refs):
    nf, nw = len(ftags), len(wtags)
    fr, wr = refs[:nf], refs[nf : nf + nw]
    k_ref, v_ref, state_ref, a_s, w_s, fsem, wsem = refs[nf + nw :]
    fc = feature_copies(ftags, fr, a_s, fsem)
    wc = weight_copies(wtags, wr, w_s, wsem)
    begin(fc + wc)
    finish(fc + wc)
    for r in range(0, TOK, 256):
        rows = pl.ds(r, 256)
        both = dot(a_s[rows, :], w_s[...]).astype(BF16)
        k_ref[rows, :] = both[:, :COLS]
        v_ref[rows, :] = both[:, COLS:]
    for h in range(HEADS_HERE):
        cols = pl.ds(h * HD, HD)
        state_ref[h] = dot_tn(k_ref[:, cols], v_ref[:, cols])


def near_kernel(q_ref, k_ref, v_ref, g_ref, lam_ref, out_ref, dq_ref, dk_ref, dv_ref):
    tile = 128
    t_at = lax.broadcasted_iota(jnp.int32, (tile, tile), 0)
    s_at = lax.broadcasted_iota(jnp.int32, (tile, tile), 1)
    apart = jnp.bitwise_xor(t_at, s_at)
    causal = t_at >= s_at
    for h in range(HEADS_HERE):
        cols = pl.ds(h * HD, HD)
        for i in range(TOK // tile):
            rows = pl.ds(i * tile, tile)
            q, k, v, g = q_ref[rows, cols], k_ref[rows, cols], v_ref[rows, cols], g_ref[rows, cols]
            lam = lam_ref[rows, pl.ds(h * LEVELS, LEVELS)]
            mix = jnp.broadcast_to(lam[:, 0:1], (tile, tile))
            for level in range(1, 8):
                mix = jnp.where(apart >= 1 << (level - 1), lam[:, level : level + 1], mix)
            mix = jnp.where(causal, mix, 0.0)
            probs = (mix * dot_nt(q, k)).astype(BF16)
            mixed = (mix * dot_nt(g, v)).astype(BF16)
            out_ref[rows, cols] = dot(probs, v)
            dq_ref[rows, cols] = dot(mixed, k)
            dk_ref[rows, cols] = dot_tn(mixed, q)
            dv_ref[rows, cols] = dot_tn(probs, g)
        for level in range(8, NEAR):
            size = tile << (level - 8)
            for at in range(0, TOK, 2 * size):
                early, late = pl.ds(at, size), pl.ds(at + size, size)
                k, v = k_ref[early, cols], v_ref[early, cols]
                q, g = q_ref[late, cols], g_ref[late, cols]
                lam = lam_ref[late, h * LEVELS + level : h * LEVELS + level + 1]
                state = dot_tn(k, v).astype(BF16)
                back = dot_tn((lam * q.astype(F32)).astype(BF16), g).astype(BF16)
                out_ref[late, cols] += lam * dot(q, state)
                dq_ref[late, cols] += lam * dot_nt(g, state)
                dk_ref[early, cols] += dot_nt(v, back)
                dv_ref[early, cols] += dot(k, back)


def key_value_grad_kernel(ftags, *refs):
    nf = len(ftags)
    fr = refs[:nf]
    k_ref, v_ref, dk_ref, dv_ref, back_ref = refs[nf : nf + 5]
    outs = refs[nf + 5 : nf + 5 + 7]
    a_s, tot_s, grad_s, fsem = refs[nf + 12 :]
    fc = feature_copies(ftags, fr, a_s, fsem)
    begin(fc)
    for h in range(HEADS_HERE):
        cols = pl.ds(h * HD, HD)
        back = back_ref[h].astype(BF16)
        tot_s[:, cols] = (dk_ref[:, cols] + dot_nt(v_ref[:, cols], back)).astype(BF16)
        tot_s[:, pl.ds(COLS + h * HD, HD)] = (dv_ref[:, cols] + dot(k_ref[:, cols], back)).astype(BF16)
    finish(fc)
    for r in range(0, WIDTH, 256):
        grad_s[pl.ds(r, 256), :] = dot_tn(a_s[:, pl.ds(r, 256)], tot_s[...]).astype(BF16)
    x = lax.axis_index("x")
    part = WIDTH // XN
    half = part // 2

    def rows_of(off, start, size):
        at = lax.rem(x + off, XN) * part + start
        return grad_s[pl.ds(pl.multiple_of(at, half), size), :]

    outs[0][...] = rows_of(0, 0, part)
    outs[1][...] = rows_of(1, 0, half)
    outs[2][...] = rows_of(1, half, half)
    outs[3][...] = rows_of(2, 0, half)
    outs[4][...] = rows_of(2, half, half)
    outs[5][...] = rows_of(3, 0, half)
    outs[6][...] = rows_of(3, half, half)


def query_grad_kernel(ftags, *refs):
    nf = len(ftags)
    fr = refs[:nf]
    q_ref, g_ref, near_ref, dq_ref, lam_ref, state_ref = refs[nf : nf + 6]
    att_ref = refs[nf + 6]
    outs = refs[nf + 7 : nf + 7 + ZN]
    a_s, tot_s, grad_s, fsem = refs[nf + 7 + ZN :]
    fc = feature_copies(ftags, fr, a_s, fsem)
    begin(fc)
    for h in range(HEADS_HERE):
        cols = pl.ds(h * HD, HD)
        q, g = q_ref[:, cols], g_ref[:, cols]
        out = near_ref[:, cols]
        total = dq_ref[:, cols]
        for b in range(FAR):
            at = h * LEVELS + NEAR + b
            lam = lam_ref[:, at : at + 1]
            state = state_ref[b, h]
            out = out + lam * dot(q, state)
            total = total + lam * dot_nt(g, state)
        att_ref[:, cols] = out.astype(BF16)
        tot_s[:, cols] = total.astype(BF16)
    finish(fc)
    for r in range(0, WIDTH, 256):
        grad_s[pl.ds(r, 256), :] = dot_tn(a_s[:, pl.ds(r, 256)], tot_s[...]).astype(BF16)
    x = lax.axis_index("x")
    z = lax.axis_index("z")
    for d in range(ZN):
        zz = lax.rem(z + d, ZN)
        for rx in range(XN):
            xx = lax.rem(x + rx, XN)
            at = pl.multiple_of((xx * ZN + zz) * PIECE, PIECE)
            outs[d][pl.ds(rx * PIECE, PIECE), :] = grad_s[pl.ds(at, PIECE), :]


ANY = pl.BlockSpec(memory_space=pl.ANY)
VM = pl.BlockSpec(memory_space=pltpu.VMEM)


def struct(shape, dtype):
    return jax.ShapeDtypeStruct(shape, dtype)


def call(body, name, inputs, specs, outs, scratch, flops, moved):
    return pl.pallas_call(
        body,
        name=name,
        in_specs=specs,
        out_specs=[VM] * len(outs),
        out_shape=outs,
        scratch_shapes=scratch,
        compiler_params=pltpu.CompilerParams(vmem_limit_bytes=VMEM_LIMIT),
        cost_estimate=pl.CostEstimate(flops=flops, transcendentals=0, bytes_accessed=moved),
    )(*inputs)


def on_device(activations, w_query, w_key, w_value, level_table, table_rows, out_grad):
    x = lax.axis_index("x")
    z = lax.axis_index("z")
    feats = features_of(activations)
    ftags = [(off, same) for off, same, _ in feats]
    fparts = [part for _, _, part in feats]

    weights = jnp.concatenate([w_query, w_key, w_value], axis=1)
    along_x = [weights] + [shifted(weights, "x", -off) for off in (1, 2, 3)]
    wq = ring_of(jnp.concatenate([w[:, :COLS] for w in along_x], axis=0), "z")
    wkv = ring_of(jnp.concatenate([w[:, COLS:] for w in along_x], axis=0), "z")
    wtags = [off for off, _ in wq]

    scale = 1.0 / math.sqrt(HD * TOK)
    table_size = level_table.shape[1]
    onehot = (table_rows[:, None] == jnp.arange(table_size, dtype=jnp.int32)[None, :]).astype(F32)
    flat = jnp.transpose(level_table, (1, 0, 2)).reshape(table_size, HEADS_HERE * LEVELS)
    lam = scale * jnp.dot(onehot, flat, precision=lax.Precision.HIGHEST)

    a_scratch = pltpu.VMEM((TOK, WIDTH), BF16)
    fsem = pltpu.SemaphoreType.DMA((len(ftags),))
    wsem = pltpu.SemaphoreType.DMA((len(wtags), XN))
    nf, nw = len(ftags), len(wtags)

    queries, grads = call(
        functools.partial(query_kernel, ftags, wtags),
        "queries",
        [*fparts, *[w for _, w in wq], out_grad, lam],
        [ANY] * (nf + nw) + [VM] * 2,
        [struct((TOK, COLS), BF16), struct((FAR, HEADS_HERE, HD, HD), F32)],
        [a_scratch, pltpu.VMEM((WIDTH, COLS), BF16), fsem, wsem],
        2 * TOK * WIDTH * COLS,
        8 << 20,
    )

    pending = jnp.zeros((HEADS_HERE, HD, HD), F32)
    steps = (("x", 2, x, 4), ("x", 1, x, 3), ("z", 4, z, 2), ("z", 2, z, 1), ("z", 1, z, 0))
    for axis, bit, index, level in steps:
        upper = (index & bit) != 0
        sent = pending + jnp.where(upper, grads[level], 0.0)
        pending = pending + swapped(sent.astype(BF16), axis, bit).astype(F32)

    keys, values, local = call(
        functools.partial(key_value_kernel, ftags, wtags),
        "keys_values",
        [*fparts, *[w for _, w in wkv]],
        [ANY] * (nf + nw),
        [struct((TOK, COLS), BF16), struct((TOK, COLS), BF16), struct((HEADS_HERE, HD, HD), F32)],
        [a_scratch, pltpu.VMEM((WIDTH, 2 * COLS), BF16), fsem, wsem],
        4 * TOK * WIDTH * COLS,
        8 << 20,
    )

    total = local
    states = []
    for axis, bit, index in (("z", 1, z), ("z", 2, z), ("z", 4, z), ("x", 1, x), ("x", 2, x)):
        upper = (index & bit) != 0
        sibling = swapped(total.astype(BF16), axis, bit)
        states.append(jnp.where(upper, sibling, jnp.zeros_like(sibling)))
        total = total + sibling.astype(F32)
    states = jnp.stack(states)

    near_out, query_near, key_near, value_near = call(
        near_kernel,
        "near",
        [queries, keys, values, out_grad, lam],
        [VM] * 5,
        [struct((TOK, COLS), F32)] * 4,
        [],
        2 << 30,
        8 << 20,
    )

    part = WIDTH // XN
    half = part // 2
    sizes = [part, half, half, half, half, half, half]
    c0, c1t, c1b, c2t, c2b, c3t, c3b = call(
        functools.partial(key_value_grad_kernel, ftags),
        "key_value_grad",
        [*fparts, keys, values, key_near, value_near, pending],
        [ANY] * nf + [VM] * 5,
        [struct((n, 2 * COLS), BF16) for n in sizes],
        [a_scratch, pltpu.VMEM((TOK, 2 * COLS), BF16), pltpu.VMEM((WIDTH, 2 * COLS), BF16), fsem],
        4 * TOK * WIDTH * COLS,
        8 << 20,
    )
    via_up = shifted(c2t, "x", 1)
    via_down = shifted(c2b, "x", -1)
    r1b = shifted(c1b, "x", 1)
    r3t = shifted(c3t, "x", -1)
    r1t = shifted((c1t.astype(F32) + via_up.astype(F32)).astype(BF16), "x", 1)
    r3b = shifted((c3b.astype(F32) + via_down.astype(F32)).astype(BF16), "x", -1)
    top = c0[:half].astype(F32) + r1t.astype(F32) + r3t.astype(F32)
    bottom = c0[half:].astype(F32) + r1b.astype(F32) + r3b.astype(F32)
    mine = jnp.concatenate([top, bottom], axis=0).astype(BF16).reshape(ZN, PIECE, 2 * COLS)
    gathered = lax.all_to_all(mine, "z", 0, 0, tiled=True)
    grad_kv = jnp.sum(gathered.astype(F32), axis=0)

    outs = call(
        functools.partial(query_grad_kernel, ftags),
        "query_grad",
        [*fparts, queries, out_grad, near_out, query_near, lam, states],
        [ANY] * nf + [VM] * 6,
        [struct((TOK, COLS), BF16)] + [struct((XN * PIECE, COLS), BF16)] * ZN,
        [a_scratch, pltpu.VMEM((TOK, COLS), BF16), pltpu.VMEM((WIDTH, COLS), BF16), fsem],
        2 * TOK * WIDTH * COLS,
        8 << 20,
    )
    attended, pieces = outs[0], outs[1:]
    up, down = pieces[4], pieces[5]
    for nxt in (3, 2, 1):
        up = (shifted(up, "z", 1).astype(F32) + pieces[nxt].astype(F32)).astype(BF16)
    up = shifted(up, "z", 1)
    for nxt in (6, 7):
        down = (shifted(down, "z", -1).astype(F32) + pieces[nxt].astype(F32)).astype(BF16)
    down = shifted(down, "z", -1)
    sums = (pieces[0].astype(F32) + up.astype(F32) + down.astype(F32)).reshape(XN, PIECE, COLS)
    grad_query = sums[0]
    for off in (1, 2, 3):
        grad_query = grad_query + shifted(sums[off].astype(BF16), "x", off).astype(F32)
    return attended, grad_query, grad_kv[:, :COLS], grad_kv[:, COLS:]


def solution(mesh):
    finer = Mesh(mesh.devices.reshape(XN, ZN, YN, 2), ("x", "z", "y", "core"))
    rows, cols = ("x", "z"), ("y", "core")
    return jax.shard_map(
        on_device,
        mesh=finer,
        in_specs=(
            P(rows, cols),
            P(rows, cols),
            P(rows, cols),
            P(rows, cols),
            P(cols, None, None),
            P(rows),
            P(rows, cols),
        ),
        out_specs=(P(rows, cols), P(rows, cols), P(rows, cols), P(rows, cols)),
        check_vma=False,
    )
```

```python
import functools
import math

import jax
import jax.numpy as jnp
from jax import lax
from jax.experimental import pallas as pl
from jax.experimental.pallas import tpu as pltpu
from jax.sharding import Mesh
from jax.sharding import PartitionSpec as P

F32 = jnp.float32
BF16 = jnp.bfloat16
VMEM_LIMIT = 20 * 1024 * 1024

TOK = 1024
WIDTH = 2048
COLS = 256
HD = 128
HEADS_HERE = 2
LEVELS = 16
NEAR = 11
FAR = 5
XN, ZN, YN = 4, 8, 4
PIECE = WIDTH // (XN * ZN)


def shifted(value, axis, offset):
    count = lax.axis_size(axis)
    return lax.ppermute(value, axis, [(i, (i + offset) % count) for i in range(count)])


def swapped(value, axis, bit):
    count = lax.axis_size(axis)
    return lax.ppermute(value, axis, [(i, i ^ bit) for i in range(count)])


def ring_of(value, axis):
    found = [(0, value)]
    up = down = value
    for step in range(1, 5):
        up = shifted(up, axis, 1)
        found.append((-step, up))
        if step < 4:
            down = shifted(down, axis, -1)
            found.append((step, down))
    return found


def features_of(block, gate):
    mine = [block] + [shifted(block, "y", -off) for off in (1, -1, 2)]
    *mine, gate = lax.optimization_barrier((*mine, gate))
    mine = list(zip((0, 1, -1, 2), mine))
    found = [(off, True, part) for off, part in mine]
    found += [(off, False, shifted(part, "core", 1)) for off, part in mine]
    return found, gate


def copy_for_each(value, axis):
    peers = lax.axis_size(axis)
    wide = jnp.broadcast_to(value[None], (peers, *value.shape))
    return lax.all_to_all(wide, axis, 0, 0, tiled=True)


def dot(a, b):
    return lax.dot_general(a, b, (((1,), (0,)), ((), ())), preferred_element_type=F32)


def dot_nt(a, b):
    return lax.dot_general(a, b, (((1,), (1,)), ((), ())), preferred_element_type=F32)


def dot_tn(a, b):
    return lax.dot_general(a, b, (((0,), (0,)), ((), ())), preferred_element_type=F32)


def feature_copies(tags, refs, scratch, sem):
    y = lax.axis_index("y")
    core = lax.axis_index("core")
    copies = []
    for i, ((off, same), ref) in enumerate(zip(tags, refs)):
        block = lax.rem(y + (off + YN), YN) * 2 + (core if same else 1 - core)
        cols = pl.ds(pl.multiple_of(block * COLS, COLS), COLS)
        copies.append(pltpu.make_async_copy(ref, scratch.at[:, cols], sem.at[i]))
    return copies


def weight_copies(tags, refs, scratch, sem):
    x = lax.axis_index("x")
    z = lax.axis_index("z")
    copies = []
    for i, (off, ref) in enumerate(zip(tags, refs)):
        zz = lax.rem(z + (off + ZN), ZN)
        for rx in range(XN):
            xx = lax.rem(x + rx, XN)
            rows = pl.ds(pl.multiple_of((xx * ZN + zz) * PIECE, PIECE), PIECE)
            src = ref.at[pl.ds(rx * PIECE, PIECE), :]
            copies.append(pltpu.make_async_copy(src, scratch.at[rows, :], sem.at[i, rx]))
    return copies


def column_weight_copies(refs, scratch, sem):
    x = lax.axis_index("x")
    part = ZN * PIECE
    copies = []
    for i, ref in enumerate(refs):
        at = pl.multiple_of(lax.rem(x + i, XN) * part, part)
        copies.append(pltpu.make_async_copy(ref, scratch.at[pl.ds(at, part), :], sem.at[i]))
    return copies


def begin(copies):
    for copy in copies:
        copy.start()


def finish(copies):
    for copy in copies:
        copy.wait()


def query_kernel(ftags, wtags, *refs):
    nf, nw = len(ftags), len(wtags)
    fr, wr = refs[:nf], refs[nf : nf + nw]
    g_ref, lam_ref, q_ref, state_ref, a_s, w_s, fsem, wsem = refs[nf + nw :]
    fc = feature_copies(ftags, fr, a_s, fsem)
    wc = weight_copies(wtags, wr, w_s, wsem)
    begin(fc + wc)
    finish(fc + wc)
    for r in range(0, TOK, 256):
        rows = pl.ds(r, 256)
        q_ref[rows, :] = dot(a_s[rows, :], w_s[...]).astype(BF16)
    for h in range(HEADS_HERE):
        cols = pl.ds(h * HD, HD)
        q = q_ref[:, cols].astype(F32)
        scaled = []
        for b in range(FAR):
            at = h * LEVELS + NEAR + b
            scaled.append((lam_ref[:, at : at + 1] * q).astype(BF16))
        g = g_ref[:, cols]
        for b in range(FAR):
            state_ref[b, h] = dot_tn(scaled[b], g)


def key_value_kernel(ftags, *refs):
    nf, nw = len(ftags), XN
    fr, wr = refs[:nf], refs[nf : nf + nw]
    k_ref, v_ref, state_ref, a_s, w_s, fsem, wsem = refs[nf + nw :]
    fc = feature_copies(ftags, fr, a_s, fsem)
    wc = column_weight_copies(wr, w_s, wsem)
    begin(fc + wc)
    finish(fc + wc)
    for r in range(0, TOK, 256):
        rows = pl.ds(r, 256)
        both = dot(a_s[rows, :], w_s[...]).astype(BF16)
        k_ref[rows, :] = both[:, :COLS]
        v_ref[rows, :] = both[:, COLS:]
    for h in range(HEADS_HERE):
        cols = pl.ds(h * HD, HD)
        state_ref[h] = dot_tn(k_ref[:, cols], v_ref[:, cols])


def near_kernel(h, q_ref, k_ref, v_ref, g_ref, lam_ref, out_ref, dq_ref, dk_ref, dv_ref):
    tile = 128
    t_at = lax.broadcasted_iota(jnp.int32, (tile, tile), 0)
    s_at = lax.broadcasted_iota(jnp.int32, (tile, tile), 1)
    apart = jnp.bitwise_xor(t_at, s_at)
    causal = t_at >= s_at
    mine = pl.ds(0, HD)
    cols = pl.ds(h * HD, HD)
    for i in range(TOK // tile):
        rows = pl.ds(i * tile, tile)
        q, k, v, g = q_ref[rows, cols], k_ref[rows, cols], v_ref[rows, cols], g_ref[rows, cols]
        lam = lam_ref[rows, pl.ds(h * LEVELS, LEVELS)]
        mix = jnp.broadcast_to(lam[:, 0:1], (tile, tile))
        for level in range(1, 8):
            mix = jnp.where(apart >= 1 << (level - 1), lam[:, level : level + 1], mix)
        mix = jnp.where(causal, mix, 0.0)
        probs = (mix * dot_nt(q, k)).astype(BF16)
        mixed = (mix * dot_nt(g, v)).astype(BF16)
        out_ref[rows, mine] = dot(probs, v)
        dq_ref[rows, mine] = dot(mixed, k)
        dk_ref[rows, mine] = dot_tn(mixed, q)
        dv_ref[rows, mine] = dot_tn(probs, g)
    for level in range(8, NEAR):
        size = tile << (level - 8)
        for at in range(0, TOK, 2 * size):
            early, late = pl.ds(at, size), pl.ds(at + size, size)
            k, v = k_ref[early, cols], v_ref[early, cols]
            q, g = q_ref[late, cols], g_ref[late, cols]
            lam = lam_ref[late, h * LEVELS + level : h * LEVELS + level + 1]
            state = dot_tn(k, v).astype(BF16)
            back = dot_tn((lam * q.astype(F32)).astype(BF16), g).astype(BF16)
            out_ref[late, mine] += lam * dot(q, state)
            dq_ref[late, mine] += lam * dot_nt(g, state)
            dk_ref[early, mine] += dot_nt(v, back)
            dv_ref[early, mine] += dot(k, back)


def key_value_grad_kernel(ftags, *refs):
    nf = len(ftags)
    fr = refs[:nf]
    k_ref, v_ref, dk0, dk1, dv0, dv1, back_ref = refs[nf : nf + 7]
    outs = refs[nf + 7 : nf + 7 + XN]
    a_s, tot_s, grad_s, fsem = refs[nf + 7 + XN :]
    fc = feature_copies(ftags, fr, a_s, fsem)
    begin(fc)
    for h in range(HEADS_HERE):
        cols = pl.ds(h * HD, HD)
        back = back_ref[h].astype(BF16)
        tot_s[:, cols] = ((dk0, dk1)[h][...] + dot_nt(v_ref[:, cols], back)).astype(BF16)
        tot_s[:, pl.ds(COLS + h * HD, HD)] = ((dv0, dv1)[h][...] + dot(k_ref[:, cols], back)).astype(BF16)
    finish(fc)
    for r in range(0, WIDTH, 256):
        grad_s[pl.ds(r, 256), :] = dot_tn(a_s[:, pl.ds(r, 256)], tot_s[...]).astype(BF16)
    x = lax.axis_index("x")
    part = WIDTH // XN
    for off in range(XN):
        at = pl.multiple_of(lax.rem(x + off, XN) * part, part)
        outs[off][...] = grad_s[pl.ds(at, part), :]


def query_grad_kernel(ftags, *refs):
    nf = len(ftags)
    fr = refs[:nf]
    q_ref, g_ref, near0, near1, dq0, dq1, lam_ref, state_ref = refs[nf : nf + 8]
    att_ref = refs[nf + 8]
    outs = refs[nf + 9 : nf + 9 + ZN]
    a_s, tot_s, grad_s, fsem = refs[nf + 9 + ZN :]
    fc = feature_copies(ftags, fr, a_s, fsem)
    begin(fc)
    for h in range(HEADS_HERE):
        cols = pl.ds(h * HD, HD)
        q, g = q_ref[:, cols], g_ref[:, cols]
        out = (near0, near1)[h][...]
        total = (dq0, dq1)[h][...]
        for b in range(FAR):
            at = h * LEVELS + NEAR + b
            lam = lam_ref[:, at : at + 1]
            state = state_ref[b, h]
            out = out + lam * dot(q, state)
            total = total + lam * dot_nt(g, state)
        att_ref[:, cols] = out.astype(BF16)
        tot_s[:, cols] = total.astype(BF16)
    finish(fc)
    for r in range(0, WIDTH, 256):
        grad_s[pl.ds(r, 256), :] = dot_tn(a_s[:, pl.ds(r, 256)], tot_s[...]).astype(BF16)
    x = lax.axis_index("x")
    z = lax.axis_index("z")
    for d in range(ZN):
        zz = lax.rem(z + d, ZN)
        for rx in range(XN):
            xx = lax.rem(x + rx, XN)
            at = pl.multiple_of((xx * ZN + zz) * PIECE, PIECE)
            outs[d][pl.ds(rx * PIECE, PIECE), :] = grad_s[pl.ds(at, PIECE), :]


ANY = pl.BlockSpec(memory_space=pl.ANY)
VM = pl.BlockSpec(memory_space=pltpu.VMEM)


def struct(shape, dtype):
    return jax.ShapeDtypeStruct(shape, dtype)


def call(body, name, inputs, specs, outs, scratch, flops, moved):
    return pl.pallas_call(
        body,
        name=name,
        in_specs=specs,
        out_specs=[VM] * len(outs),
        out_shape=outs,
        scratch_shapes=scratch,
        compiler_params=pltpu.CompilerParams(vmem_limit_bytes=VMEM_LIMIT),
        cost_estimate=pl.CostEstimate(flops=flops, transcendentals=0, bytes_accessed=moved),
    )(*inputs)


def on_device(activations, w_query, w_key, w_value, level_table, table_rows, out_grad):
    x = lax.axis_index("x")
    z = lax.axis_index("z")
    query_parts = [w_query] + [shifted(w_query, "x", -off) for off in (1, 2, 3)]
    wq = ring_of(jnp.concatenate(query_parts, axis=0), "z")
    wtags = [off for off, _ in wq]
    wkv = copy_for_each(jnp.concatenate([w_key, w_value], axis=1), "z")
    feats, wkv = features_of(activations, wkv.reshape(ZN * PIECE, 2 * COLS))
    ftags = [(off, same) for off, same, _ in feats]
    fparts = [part for _, _, part in feats]
    wkv = [wkv] + [shifted(wkv, "x", -off) for off in (1, 2, 3)]

    scale = 1.0 / math.sqrt(HD * TOK)
    table_size = level_table.shape[1]
    onehot = (table_rows[:, None] == jnp.arange(table_size, dtype=jnp.int32)[None, :]).astype(F32)
    flat = jnp.transpose(level_table, (1, 0, 2)).reshape(table_size, HEADS_HERE * LEVELS)
    lam = scale * jnp.dot(onehot, flat, precision=lax.Precision.HIGHEST)

    a_scratch = pltpu.VMEM((TOK, WIDTH), BF16)
    fsem = pltpu.SemaphoreType.DMA((len(ftags),))
    wsem = pltpu.SemaphoreType.DMA((len(wtags), XN))
    nf, nw = len(ftags), len(wtags)

    queries, grads = call(
        functools.partial(query_kernel, ftags, wtags),
        "queries",
        [*fparts, *[w for _, w in wq], out_grad, lam],
        [ANY] * (nf + nw) + [VM] * 2,
        [struct((TOK, COLS), BF16), struct((FAR, HEADS_HERE, HD, HD), F32)],
        [a_scratch, pltpu.VMEM((WIDTH, COLS), BF16), fsem, wsem],
        1048576,
        1024,
    )

    grads, *wkv = lax.optimization_barrier((grads, *wkv))

    pair = lax.shift_right_logical(z, 1)
    pending = jnp.zeros((HEADS_HERE, HD, HD), F32)
    arrived = []
    for off in (1, 2, 3):
        to = lax.rem(x + (XN - off), XN)
        level = jnp.where(jnp.bitwise_xor(x, to) == 1, grads[3], grads[4])
        arrived.append(shifted(jnp.where(to < x, level, 0.0).astype(BF16), "x", -off))
    pending = sum(part.astype(F32) for part in arrived)
    after_one = arrived
    arrived = []
    for off in (1, 2, 3):
        to = jnp.bitwise_and(pair + (4 - off), 3)
        level = jnp.where(jnp.bitwise_xor(pair, to) == 1, grads[1], grads[2])
        sent = pending + jnp.where(to < pair, level, 0.0)
        arrived.append(shifted(sent.astype(BF16), "z", -2 * off))
    pending = pending + sum(part.astype(F32) for part in arrived)
    after_two = arrived
    sent = pending + jnp.where((z & 1) != 0, grads[0], 0.0)
    pending = pending + swapped(sent.astype(BF16), "z", 1).astype(F32)

    keys, values, local = call(
        functools.partial(key_value_kernel, ftags),
        "keys_values",
        [*fparts, *wkv],
        [ANY] * (nf + XN),
        [struct((TOK, COLS), BF16), struct((TOK, COLS), BF16), struct((HEADS_HERE, HD, HD), F32)],
        [a_scratch, pltpu.VMEM((WIDTH, 2 * COLS), BF16), fsem, pltpu.SemaphoreType.DMA((XN,))],
        8 << 30,
        8 << 20,
    )

    none = jnp.zeros((HEADS_HERE, HD, HD), BF16)

    def among_four(value, index, axis, stride):
        sent = value.astype(BF16)
        got = {off: shifted(sent, axis, off * stride) for off in (1, 2, 3)}
        wide = {off: part.astype(F32) for off, part in got.items()}
        near = jnp.where((index & 1) != 0, got[1], none)
        other = wide[2] + jnp.where(index == 2, wide[1], wide[3])
        far = jnp.where(index >= 2, other.astype(BF16), none)
        return near, far, value + wide[1] + wide[2] + wide[3]

    local, *_ = lax.optimization_barrier((local, *after_one))
    sibling = swapped(local.astype(BF16), "z", 1)
    state0 = jnp.where((z & 1) != 0, sibling, none)
    total = local + sibling.astype(F32)
    near = []
    for h, gate in enumerate((after_one, [*after_two, sibling])):
        first, *_ = lax.optimization_barrier((queries, *gate))
        near.append(
            call(
                functools.partial(near_kernel, h),
                "near",
                [first, keys, values, out_grad, lam],
                [VM] * 5,
                [struct((TOK, HD), F32)] * 4,
                [],
                2 << 30,
                8 << 20,
            )
        )
    near_out, query_near, key_near, value_near = (list(parts) for parts in zip(*near))

    state1, state2, total = among_four(total, pair, "z", 2)
    key_near[0], _ = lax.optimization_barrier((key_near[0], state1))
    state3, state4, total = among_four(total, x, "x", 1)
    states = jnp.stack([state0, state1, state2, state3, state4])

    part = WIDTH // XN
    sums = call(
        functools.partial(key_value_grad_kernel, ftags),
        "key_value_grad",
        [*fparts, keys, values, *key_near, *value_near, pending],
        [ANY] * nf + [VM] * 7,
        [struct((part, 2 * COLS), BF16)] * XN,
        [a_scratch, pltpu.VMEM((TOK, 2 * COLS), BF16), pltpu.VMEM((WIDTH, 2 * COLS), BF16), fsem],
        1048576,
        1024,
    )
    sums = list(sums)
    arrived = [shifted(sums[off], "x", off) for off in (1, 2, 3)]
    mine = sums[0].astype(F32) + sum(part.astype(F32) for part in arrived)
    mine = mine.astype(BF16).reshape(ZN, PIECE, 2 * COLS)
    gathered = lax.all_to_all(mine, "z", 0, 0, tiled=True)
    grad_kv = jnp.sum(gathered.astype(F32), axis=0)

    query_near[0], _ = lax.optimization_barrier((query_near[0], sums[0]))
    outs = call(
        functools.partial(query_grad_kernel, ftags),
        "query_grad",
        [*fparts, queries, out_grad, *near_out, *query_near, lam, states],
        [ANY] * nf + [VM] * 8,
        [struct((TOK, COLS), BF16)] + [struct((XN * PIECE, COLS), BF16)] * ZN,
        [a_scratch, pltpu.VMEM((TOK, COLS), BF16), pltpu.VMEM((WIDTH, COLS), BF16), fsem],
        8 << 30,
        8 << 20,
    )
    attended, pieces = outs[0], list(outs[1:])
    pieces[3], pieces[6], *_ = lax.optimization_barrier((pieces[3], pieces[6], *arrived))
    up, down = pieces[4], pieces[5]
    for nxt in (3, 2, 1):
        up = (shifted(up, "z", 1).astype(F32) + pieces[nxt].astype(F32)).astype(BF16)
    up = shifted(up, "z", 1)
    for nxt in (6, 7):
        down = (shifted(down, "z", -1).astype(F32) + pieces[nxt].astype(F32)).astype(BF16)
    down = shifted(down, "z", -1)
    sums = (pieces[0].astype(F32) + up.astype(F32) + down.astype(F32)).reshape(XN, PIECE, COLS)
    grad_query = sums[0]
    for off in (1, 2, 3):
        grad_query = grad_query + shifted(sums[off].astype(BF16), "x", off).astype(F32)
    return attended, grad_query, grad_kv[:, :COLS], grad_kv[:, COLS:]


def solution(mesh):
    finer = Mesh(mesh.devices.reshape(XN, ZN, YN, 2), ("x", "z", "y", "core"))
    rows, cols = ("x", "z"), ("y", "core")
    return jax.shard_map(
        on_device,
        mesh=finer,
        in_specs=(
            P(rows, cols),
            P(rows, cols),
            P(rows, cols),
            P(rows, cols),
            P(cols, None, None),
            P(rows),
            P(rows, cols),
        ),
        out_specs=(P(rows, cols), P(rows, cols), P(rows, cols), P(rows, cols)),
        check_vma=False,
    )
```

```python
import functools
import math

import jax
import jax.numpy as jnp
from jax import lax
from jax.experimental import pallas as pl
from jax.experimental.pallas import tpu as pltpu
from jax.sharding import Mesh
from jax.sharding import PartitionSpec as P

F32 = jnp.float32
BF16 = jnp.bfloat16
VMEM_LIMIT = 20 * 1024 * 1024

TOK = 1024
WIDTH = 2048
COLS = 256
HD = 128
HEADS_HERE = 2
LEVELS = 16
NEAR = 11
FAR = 5
XN, ZN, YN = 4, 8, 4
PIECE = WIDTH // (XN * ZN)


def shifted(value, axis, offset):
    count = lax.axis_size(axis)
    return lax.ppermute(value, axis, [(i, (i + offset) % count) for i in range(count)])


def swapped(value, axis, bit):
    count = lax.axis_size(axis)
    return lax.ppermute(value, axis, [(i, i ^ bit) for i in range(count)])


def features_of(block):
    mine = [(0, block)] + [(off, shifted(block, "y", -off)) for off in (1, -1, 2)]
    found = [(off, True, part) for off, part in mine]
    found += [(off, False, shifted(part, "core", 1)) for off, part in mine]
    return found


def copy_for_each(value, axis):
    peers = lax.axis_size(axis)
    wide = jnp.broadcast_to(value[None], (peers, *value.shape))
    return lax.all_to_all(wide, axis, 0, 0, tiled=True)


def dot(a, b):
    return lax.dot_general(a, b, (((1,), (0,)), ((), ())), preferred_element_type=F32)


def dot_nt(a, b):
    return lax.dot_general(a, b, (((1,), (1,)), ((), ())), preferred_element_type=F32)


def dot_tn(a, b):
    return lax.dot_general(a, b, (((0,), (0,)), ((), ())), preferred_element_type=F32)


def feature_copies(tags, refs, scratch, sem):
    y = lax.axis_index("y")
    core = lax.axis_index("core")
    copies = []
    for i, ((off, same), ref) in enumerate(zip(tags, refs)):
        block = lax.rem(y + (off + YN), YN) * 2 + (core if same else 1 - core)
        cols = pl.ds(pl.multiple_of(block * COLS, COLS), COLS)
        copies.append(pltpu.make_async_copy(ref, scratch.at[:, cols], sem.at[i]))
    return copies


def weight_copies(ref, scratch, sem):
    x = lax.axis_index("x")
    copies = []
    for z in range(ZN):
        for rx in range(XN):
            xx = lax.rem(x + rx, XN)
            rows = pl.ds(pl.multiple_of((xx * ZN + z) * PIECE, PIECE), PIECE)
            src = ref.at[z, pl.ds(rx * PIECE, PIECE), :]
            copies.append(pltpu.make_async_copy(src, scratch.at[rows, :], sem.at[z, rx]))
    return copies


def column_weight_copies(refs, scratch, sem):
    x = lax.axis_index("x")
    part = ZN * PIECE
    copies = []
    for i, ref in enumerate(refs):
        at = pl.multiple_of(lax.rem(x + i, XN) * part, part)
        copies.append(pltpu.make_async_copy(ref, scratch.at[pl.ds(at, part), :], sem.at[i]))
    return copies


def begin(copies):
    for copy in copies:
        copy.start()


def finish(copies):
    for copy in copies:
        copy.wait()


def query_kernel(ftags, *refs):
    nf = len(ftags)
    fr, wr = refs[:nf], refs[nf : nf + XN]
    g_ref, lam_ref, q_ref, state_ref, a_s, w_s, fsem, wsem = refs[nf + XN :]
    fc = feature_copies(ftags, fr, a_s, fsem)
    wc = column_weight_copies(wr, w_s, wsem)
    begin(fc + wc)
    finish(fc + wc)
    for r in range(0, TOK, 256):
        rows = pl.ds(r, 256)
        q_ref[rows, :] = dot(a_s[rows, :], w_s[...]).astype(BF16)
    for h in range(HEADS_HERE):
        cols = pl.ds(h * HD, HD)
        q = q_ref[:, cols].astype(F32)
        scaled = []
        for b in range(FAR):
            at = h * LEVELS + NEAR + b
            scaled.append((lam_ref[:, at : at + 1] * q).astype(BF16))
        g = g_ref[:, cols]
        for b in range(FAR):
            state_ref[b, h] = dot_tn(scaled[b], g)


def key_value_kernel(ftags, *refs):
    nf = len(ftags)
    fr, wr = refs[:nf], refs[nf]
    k_ref, v_ref, state_ref, a_s, w_s, fsem, wsem = refs[nf + 1 :]
    fc = feature_copies(ftags, fr, a_s, fsem)
    wc = weight_copies(wr, w_s, wsem)
    begin(fc + wc)
    finish(fc + wc)
    for r in range(0, TOK, 256):
        rows = pl.ds(r, 256)
        both = dot(a_s[rows, :], w_s[...]).astype(BF16)
        k_ref[rows, :] = both[:, :COLS]
        v_ref[rows, :] = both[:, COLS:]
    for h in range(HEADS_HERE):
        cols = pl.ds(h * HD, HD)
        state_ref[h] = dot_tn(k_ref[:, cols], v_ref[:, cols])


def near_kernel(h, q_ref, k_ref, v_ref, g_ref, lam_ref, out_ref, dq_ref, dk_ref, dv_ref):
    tile = 128
    t_at = lax.broadcasted_iota(jnp.int32, (tile, tile), 0)
    s_at = lax.broadcasted_iota(jnp.int32, (tile, tile), 1)
    apart = jnp.bitwise_xor(t_at, s_at)
    causal = t_at >= s_at
    mine = pl.ds(0, HD)
    cols = pl.ds(h * HD, HD)
    for i in range(TOK // tile):
        rows = pl.ds(i * tile, tile)
        q, k, v, g = q_ref[rows, cols], k_ref[rows, cols], v_ref[rows, cols], g_ref[rows, cols]
        lam = lam_ref[rows, pl.ds(h * LEVELS, LEVELS)]
        mix = jnp.broadcast_to(lam[:, 0:1], (tile, tile))
        for level in range(1, 8):
            mix = jnp.where(apart >= 1 << (level - 1), lam[:, level : level + 1], mix)
        mix = jnp.where(causal, mix, 0.0)
        probs = (mix * dot_nt(q, k)).astype(BF16)
        mixed = (mix * dot_nt(g, v)).astype(BF16)
        out_ref[rows, mine] = dot(probs, v)
        dq_ref[rows, mine] = dot(mixed, k)
        dk_ref[rows, mine] = dot_tn(mixed, q)
        dv_ref[rows, mine] = dot_tn(probs, g)
    for level in range(8, NEAR):
        size = tile << (level - 8)
        for at in range(0, TOK, 2 * size):
            early, late = pl.ds(at, size), pl.ds(at + size, size)
            k, v = k_ref[early, cols], v_ref[early, cols]
            q, g = q_ref[late, cols], g_ref[late, cols]
            lam = lam_ref[late, h * LEVELS + level : h * LEVELS + level + 1]
            state = dot_tn(k, v).astype(BF16)
            back = dot_tn((lam * q.astype(F32)).astype(BF16), g).astype(BF16)
            out_ref[late, mine] += lam * dot(q, state)
            dq_ref[late, mine] += lam * dot_nt(g, state)
            dk_ref[early, mine] += dot_nt(v, back)
            dv_ref[early, mine] += dot(k, back)


def key_value_grad_kernel(ftags, *refs):
    nf = len(ftags)
    fr = refs[:nf]
    k_ref, v_ref, dk0, dk1, dv0, dv1, back_ref = refs[nf : nf + 7]
    parts_ref, a_s, tot_s, grad_s, fsem = refs[nf + 7 :]
    fc = feature_copies(ftags, fr, a_s, fsem)
    begin(fc)
    for h in range(HEADS_HERE):
        cols = pl.ds(h * HD, HD)
        back = back_ref[h].astype(BF16)
        tot_s[:, cols] = ((dk0, dk1)[h][...] + dot_nt(v_ref[:, cols], back)).astype(BF16)
        tot_s[:, pl.ds(COLS + h * HD, HD)] = ((dv0, dv1)[h][...] + dot(k_ref[:, cols], back)).astype(BF16)
    finish(fc)
    for r in range(0, WIDTH, 256):
        grad_s[pl.ds(r, 256), :] = dot_tn(a_s[:, pl.ds(r, 256)], tot_s[...]).astype(BF16)
    x = lax.axis_index("x")
    for z in range(ZN):
        for rx in range(XN):
            xx = lax.rem(x + rx, XN)
            at = pl.multiple_of((xx * ZN + z) * PIECE, PIECE)
            parts_ref[pl.ds((z * XN + rx) * PIECE, PIECE), :] = grad_s[pl.ds(at, PIECE), :]


def query_grad_kernel(ftags, *refs):
    nf = len(ftags)
    fr = refs[:nf]
    q_ref, g_ref, near0, near1, dq0, dq1, lam_ref, state_ref = refs[nf : nf + 8]
    att_ref = refs[nf + 8]
    outs = refs[nf + 9 : nf + 9 + XN]
    a_s, tot_s, grad_s, fsem = refs[nf + 9 + XN :]
    fc = feature_copies(ftags, fr, a_s, fsem)
    begin(fc)
    for h in range(HEADS_HERE):
        cols = pl.ds(h * HD, HD)
        q, g = q_ref[:, cols], g_ref[:, cols]
        out = (near0, near1)[h][...]
        total = (dq0, dq1)[h][...]
        for b in range(FAR):
            at = h * LEVELS + NEAR + b
            lam = lam_ref[:, at : at + 1]
            state = state_ref[b, h]
            out = out + lam * dot(q, state)
            total = total + lam * dot_nt(g, state)
        att_ref[:, cols] = out.astype(BF16)
        tot_s[:, cols] = total.astype(BF16)
    finish(fc)
    for r in range(0, WIDTH, 256):
        grad_s[pl.ds(r, 256), :] = dot_tn(a_s[:, pl.ds(r, 256)], tot_s[...]).astype(BF16)
    x = lax.axis_index("x")
    part = WIDTH // XN
    for off in range(XN):
        at = pl.multiple_of(lax.rem(x + off, XN) * part, part)
        outs[off][...] = grad_s[pl.ds(at, part), :]


ANY = pl.BlockSpec(memory_space=pl.ANY)
VM = pl.BlockSpec(memory_space=pltpu.VMEM)


def struct(shape, dtype):
    return jax.ShapeDtypeStruct(shape, dtype)


def call(body, name, inputs, specs, outs, scratch, flops, moved):
    return pl.pallas_call(
        body,
        name=name,
        in_specs=specs,
        out_specs=[VM] * len(outs),
        out_shape=outs,
        scratch_shapes=scratch,
        compiler_params=pltpu.CompilerParams(vmem_limit_bytes=VMEM_LIMIT),
        cost_estimate=pl.CostEstimate(flops=flops, transcendentals=0, bytes_accessed=moved),
    )(*inputs)


def on_device(activations, w_query, w_key, w_value, level_table, table_rows, out_grad):
    x = lax.axis_index("x")
    z = lax.axis_index("z")
    both = jnp.concatenate([w_key, w_value], axis=1)
    both = [both] + [shifted(both, "x", -off) for off in (1, 2, 3)]
    wkv = lax.all_gather(jnp.concatenate(both, axis=0), "z", axis=0)
    wq = copy_for_each(w_query, "z").reshape(ZN * PIECE, COLS)
    wq = [wq] + [shifted(wq, "x", -off) for off in (1, 2, 3)]
    feats = features_of(activations)
    ftags = [(off, same) for off, same, _ in feats]
    fparts = [part for _, _, part in feats]

    scale = 1.0 / math.sqrt(HD * TOK)
    table_size = level_table.shape[1]
    onehot = (table_rows[:, None] == jnp.arange(table_size, dtype=jnp.int32)[None, :]).astype(F32)
    flat = jnp.transpose(level_table, (1, 0, 2)).reshape(table_size, HEADS_HERE * LEVELS)
    lam = scale * jnp.dot(onehot, flat, precision=lax.Precision.HIGHEST)

    a_scratch = pltpu.VMEM((TOK, WIDTH), BF16)
    fsem = pltpu.SemaphoreType.DMA((len(ftags),))
    wsem = pltpu.SemaphoreType.DMA((ZN, XN))
    nf = len(ftags)

    queries, grads = call(
        functools.partial(query_kernel, ftags),
        "queries",
        [*fparts, *wq, out_grad, lam],
        [ANY] * (nf + XN) + [VM] * 2,
        [struct((TOK, COLS), BF16), struct((FAR, HEADS_HERE, HD, HD), F32)],
        [a_scratch, pltpu.VMEM((WIDTH, COLS), BF16), fsem, pltpu.SemaphoreType.DMA((XN,))],
        1048576,
        1024,
    )

    pair = lax.shift_right_logical(z, 1)
    pending = jnp.zeros((HEADS_HERE, HD, HD), F32)
    arrived = []
    for off in (1, 2, 3):
        to = lax.rem(x + (XN - off), XN)
        level = jnp.where(jnp.bitwise_xor(x, to) == 1, grads[3], grads[4])
        arrived.append(shifted(jnp.where(to < x, level, 0.0).astype(BF16), "x", -off))
    pending = sum(part.astype(F32) for part in arrived)
    after_one = arrived
    arrived = []
    for off in (1, 2, 3):
        to = jnp.bitwise_and(pair + (4 - off), 3)
        level = jnp.where(jnp.bitwise_xor(pair, to) == 1, grads[1], grads[2])
        sent = pending + jnp.where(to < pair, level, 0.0)
        arrived.append(shifted(sent.astype(BF16), "z", -2 * off))
    pending = pending + sum(part.astype(F32) for part in arrived)
    after_two = arrived
    sent = pending + jnp.where((z & 1) != 0, grads[0], 0.0)
    pending = pending + swapped(sent.astype(BF16), "z", 1).astype(F32)

    keys, values, local = call(
        functools.partial(key_value_kernel, ftags),
        "keys_values",
        [*fparts, wkv],
        [ANY] * (nf + 1),
        [struct((TOK, COLS), BF16), struct((TOK, COLS), BF16), struct((HEADS_HERE, HD, HD), F32)],
        [a_scratch, pltpu.VMEM((WIDTH, 2 * COLS), BF16), fsem, wsem],
        8 << 30,
        8 << 20,
    )

    none = jnp.zeros((HEADS_HERE, HD, HD), BF16)

    def among_four(value, index, axis, stride):
        sent = value.astype(BF16)
        got = {off: shifted(sent, axis, off * stride) for off in (1, 2, 3)}
        wide = {off: part.astype(F32) for off, part in got.items()}
        near = jnp.where((index & 1) != 0, got[1], none)
        other = wide[2] + jnp.where(index == 2, wide[1], wide[3])
        far = jnp.where(index >= 2, other.astype(BF16), none)
        return near, far, value + wide[1] + wide[2] + wide[3]

    local, *_ = lax.optimization_barrier((local, *after_one))
    sibling = swapped(local, "z", 1)
    state0 = jnp.where((z & 1) != 0, sibling, 0.0).astype(BF16)
    total = local + sibling
    near = []
    for h, gate in enumerate((after_one, [*after_two, sibling])):
        first, *_ = lax.optimization_barrier((queries, *gate))
        near.append(
            call(
                functools.partial(near_kernel, h),
                "near",
                [first, keys, values, out_grad, lam],
                [VM] * 5,
                [struct((TOK, HD), F32)] * 4,
                [],
                2 << 30,
                8 << 20,
            )
        )
    near_out, query_near, key_near, value_near = (list(parts) for parts in zip(*near))

    state1, state2, total = among_four(total, pair, "z", 2)
    key_near[0], _ = lax.optimization_barrier((key_near[0], state1))
    state3, state4, total = among_four(total, x, "x", 1)
    states = jnp.stack([state0, state1, state2, state3, state4])

    part = WIDTH // XN
    (parts,) = call(
        functools.partial(key_value_grad_kernel, ftags),
        "key_value_grad",
        [*fparts, keys, values, *key_near, *value_near, pending],
        [ANY] * nf + [VM] * 7,
        [struct((WIDTH, 2 * COLS), BF16)],
        [a_scratch, pltpu.VMEM((TOK, 2 * COLS), BF16), pltpu.VMEM((WIDTH, 2 * COLS), BF16), fsem],
        1048576,
        1024,
    )
    kv_sum = lax.psum_scatter(parts, "z", scatter_dimension=0, tiled=True)

    query_near[0], _ = lax.optimization_barrier((query_near[0], parts))
    attended, *sums = call(
        functools.partial(query_grad_kernel, ftags),
        "query_grad",
        [*fparts, queries, out_grad, *near_out, *query_near, lam, states],
        [ANY] * nf + [VM] * 8,
        [struct((TOK, COLS), BF16)] + [struct((part, COLS), BF16)] * XN,
        [a_scratch, pltpu.VMEM((TOK, COLS), BF16), pltpu.VMEM((WIDTH, COLS), BF16), fsem],
        8 << 30,
        8 << 20,
    )
    mine = sums[0].astype(F32)
    for off in (1, 2, 3):
        mine = mine + shifted(sums[off], "x", off).astype(F32)
    gathered = lax.all_to_all(mine.astype(BF16).reshape(ZN, PIECE, COLS), "z", 0, 0, tiled=True)
    grad_query = jnp.sum(gathered.astype(F32), axis=0)

    kv_sum = kv_sum.reshape(XN, PIECE, 2 * COLS)
    grad_kv = kv_sum[0].astype(F32)
    for off in (1, 2, 3):
        grad_kv = grad_kv + shifted(kv_sum[off], "x", off).astype(F32)
    return attended, grad_query, grad_kv[:, :COLS], grad_kv[:, COLS:]


def solution(mesh):
    finer = Mesh(mesh.devices.reshape(XN, ZN, YN, 2), ("x", "z", "y", "core"))
    rows, cols = ("x", "z"), ("y", "core")
    return jax.shard_map(
        on_device,
        mesh=finer,
        in_specs=(
            P(rows, cols),
            P(rows, cols),
            P(rows, cols),
            P(rows, cols),
            P(cols, None, None),
            P(rows),
            P(rows, cols),
        ),
        out_specs=(P(rows, cols), P(rows, cols), P(rows, cols), P(rows, cols)),
        check_vma=False,
    )
```

```python
import functools
import math

import jax
import jax.numpy as jnp
from jax import lax
from jax.experimental import pallas as pl
from jax.experimental.pallas import tpu as pltpu
from jax.sharding import Mesh
from jax.sharding import PartitionSpec as P

F32 = jnp.float32
BF16 = jnp.bfloat16
VMEM_LIMIT = 56 * 1024 * 1024

TOK = 1024
WIDTH = 2048
COLS = 256
HD = 128
HEADS_HERE = 2
LEVELS = 16
NEAR = 11
FAR = 5
XN, ZN, YN = 4, 8, 4
PIECE = WIDTH // (XN * ZN)


def shifted(value, axis, offset):
    count = lax.axis_size(axis)
    return lax.ppermute(value, axis, [(i, (i + offset) % count) for i in range(count)])


def swapped(value, axis, bit):
    count = lax.axis_size(axis)
    return lax.ppermute(value, axis, [(i, i ^ bit) for i in range(count)])


def features_of(block):
    mine = [(0, block)] + [(off, shifted(block, "y", -off)) for off in (1, -1, 2)]
    found = [(off, True, part) for off, part in mine]
    found += [(off, False, shifted(part, "core", 1)) for off, part in mine]
    return found


def dot(a, b):
    return lax.dot_general(a, b, (((1,), (0,)), ((), ())), preferred_element_type=F32)


def dot_nt(a, b):
    return lax.dot_general(a, b, (((1,), (1,)), ((), ())), preferred_element_type=F32)


def dot_tn(a, b):
    return lax.dot_general(a, b, (((0,), (0,)), ((), ())), preferred_element_type=F32)


def feature_copies(tags, refs, scratch, sem):
    y = lax.axis_index("y")
    core = lax.axis_index("core")
    copies = []
    for i, ((off, same), ref) in enumerate(zip(tags, refs)):
        block = lax.rem(y + (off + YN), YN) * 2 + (core if same else 1 - core)
        cols = pl.ds(pl.multiple_of(block * COLS, COLS), COLS)
        copies.append(pltpu.make_async_copy(ref, scratch.at[:, cols], sem.at[i]))
    return copies


def weight_copies(ref, scratch, sem):
    x = lax.axis_index("x")
    copies = []
    for z in range(ZN):
        for rx in range(XN):
            xx = lax.rem(x + rx, XN)
            rows = pl.ds(pl.multiple_of((xx * ZN + z) * PIECE, PIECE), PIECE)
            src = ref.at[z, pl.ds(rx * PIECE, PIECE), :]
            copies.append(pltpu.make_async_copy(src, scratch.at[rows, :], sem.at[z, rx]))
    return copies


def plain_copies(sources, targets, sem):
    return [
        pltpu.make_async_copy(src, dst, sem.at[i]) for i, (src, dst) in enumerate(zip(sources, targets))
    ]


def begin(copies):
    for copy in copies:
        copy.start()


def finish(copies):
    for copy in copies:
        copy.wait()


def projection_kernel(ftags, *refs):
    nf = len(ftags)
    fr = refs[:nf]
    w_ref, g_ref, lam_ref, q_ref, k_ref, v_ref, local_ref = refs[nf : nf + 7]
    send_refs = refs[nf + 7 : nf + 10]
    pair_ref, one_ref = refs[nf + 10 : nf + 12]
    a_s, w_s, g_s, lam_s, q_s, k_s, v_s, fsem, wsem, isem, osem = refs[nf + 12 :]
    fc = feature_copies(ftags, fr, a_s, fsem)
    wc = weight_copies(w_ref, w_s, wsem)
    ic = plain_copies([g_ref, lam_ref], [g_s, lam_s], isem)
    begin(wc + fc + ic)
    finish(wc + fc)
    step = 256
    outs = [(q_s, q_ref), (k_s, k_ref), (v_s, v_ref)]
    oc = []
    for r in range(0, TOK, step):
        rows = pl.ds(r, step)
        both = dot(a_s[rows, :], w_s[...]).astype(BF16)
        for i, (held, out) in enumerate(outs):
            held[rows, :] = both[:, i * COLS : (i + 1) * COLS]
            oc.append(pltpu.make_async_copy(held.at[rows, :], out.at[rows, :], osem.at[r // step, i]))
            oc[-1].start()
    finish(ic)
    x = lax.axis_index("x")
    pair = lax.div(lax.axis_index("z"), 2)
    low = lax.rem(lax.axis_index("z"), 2)
    for h in range(HEADS_HERE):
        cols = pl.ds(h * HD, HD)
        q = q_s[:, cols].astype(F32)
        g = g_s[:, cols]
        states = []
        for b in range(FAR):
            at = h * LEVELS + NEAR + b
            states.append(dot_tn((lam_s[:, at : at + 1] * q).astype(BF16), g))
        local_ref[h] = dot_tn(k_s[:, cols], v_s[:, cols])
        one_ref[h] = jnp.where(low == 1, states[0], 0.0)
        for i, off in enumerate((1, 2, 3)):
            to = lax.rem(pair + (4 - off), 4)
            sibling = lax.div(pair, 2) == lax.div(to, 2)
            pair_ref[i, h] = jnp.where(to < pair, jnp.where(sibling, states[1], states[2]), 0.0)
            to = lax.rem(x + (XN - off), XN)
            sibling = lax.div(x, 2) == lax.div(to, 2)
            level = jnp.where(to < x, jnp.where(sibling, states[3], states[4]), 0.0)
            send_refs[i][h] = level.astype(BF16)
    finish(oc)


def near_kernel(h, q_ref, k_ref, v_ref, g_ref, lam_ref, out_h, dq_h, dk_h, dv_h, *scratch):
    q_s, k_s, v_s, g_s, lam_s, out_ref, dq_ref, dk_ref, dv_ref, isem, osem = scratch
    cols = pl.ds(h * HD, HD)
    ic = plain_copies(
        [q_ref.at[:, cols], k_ref.at[:, cols], v_ref.at[:, cols], g_ref.at[:, cols], lam_ref],
        [q_s, k_s, v_s, g_s, lam_s],
        isem,
    )
    begin(ic)
    tile = 128
    t_at = lax.broadcasted_iota(jnp.int32, (tile, tile), 0)
    s_at = lax.broadcasted_iota(jnp.int32, (tile, tile), 1)
    apart = jnp.bitwise_xor(t_at, s_at)
    causal = t_at >= s_at
    finish(ic)
    for i in range(TOK // tile):
        rows = pl.ds(i * tile, tile)
        q, k, v, g = q_s[rows, :], k_s[rows, :], v_s[rows, :], g_s[rows, :]
        lam = lam_s[rows, pl.ds(h * LEVELS, LEVELS)]
        mix = jnp.broadcast_to(lam[:, 0:1], (tile, tile))
        for level in range(1, 8):
            mix = jnp.where(apart >= 1 << (level - 1), lam[:, level : level + 1], mix)
        mix = jnp.where(causal, mix, 0.0)
        probs = (mix * dot_nt(q, k)).astype(BF16)
        mixed = (mix * dot_nt(g, v)).astype(BF16)
        out_ref[rows, :] = dot(probs, v)
        dq_ref[rows, :] = dot(mixed, k)
        dk_ref[rows, :] = dot_tn(mixed, q)
        dv_ref[rows, :] = dot_tn(probs, g)
    for level in range(8, NEAR):
        size = tile << (level - 8)
        for at in range(0, TOK, 2 * size):
            early, late = pl.ds(at, size), pl.ds(at + size, size)
            k, v = k_s[early, :], v_s[early, :]
            q, g = q_s[late, :], g_s[late, :]
            lam = lam_s[late, h * LEVELS + level : h * LEVELS + level + 1]
            state = dot_tn(k, v).astype(BF16)
            back = dot_tn((lam * q.astype(F32)).astype(BF16), g).astype(BF16)
            out_ref[late, :] += lam * dot(q, state)
            dq_ref[late, :] += lam * dot_nt(g, state)
            dk_ref[early, :] += dot_nt(v, back)
            dv_ref[early, :] += dot(k, back)
    oc = plain_copies([out_ref, dq_ref, dk_ref, dv_ref], [out_h, dq_h, dk_h, dv_h], osem)
    begin(oc)
    finish(oc)


def key_value_grad_kernel(ftags, *refs):
    nf = len(ftags)
    fr = refs[:nf]
    ins = refs[nf : nf + 6]
    back_ref, parts_ref = refs[nf + 6 : nf + 8]
    a_s, k_s, v_s, dk0, dk1, dv0, dv1, tot_s, grad_s, fsem, isem, osem = refs[nf + 8 :]
    fc = feature_copies(ftags, fr, a_s, fsem)
    ic = plain_copies(ins, [k_s, v_s, dk0, dk1, dv0, dv1], isem)
    begin(ic + fc)
    finish(ic)
    for h in range(HEADS_HERE):
        cols = pl.ds(h * HD, HD)
        back = back_ref[h].astype(BF16)
        tot_s[:, cols] = ((dk0, dk1)[h][...] + dot_nt(v_s[:, cols], back)).astype(BF16)
        tot_s[:, pl.ds(COLS + h * HD, HD)] = ((dv0, dv1)[h][...] + dot(k_s[:, cols], back)).astype(BF16)
    finish(fc)
    x = lax.axis_index("x")
    oc = []
    for r in range(0, WIDTH, 256):
        grad_s[pl.ds(r, 256), :] = dot_tn(a_s[:, pl.ds(r, 256)], tot_s[...]).astype(BF16)
        xx = r // (ZN * PIECE)
        rx = lax.rem(xx + (XN - x), XN)
        for i in range(256 // PIECE):
            z = r % (ZN * PIECE) // PIECE + i
            to = pl.ds(pl.multiple_of((z * XN + rx) * PIECE, PIECE), PIECE)
            src = grad_s.at[pl.ds(r + i * PIECE, PIECE), :]
            oc.append(pltpu.make_async_copy(src, parts_ref.at[to, :], osem.at[r // PIECE + i]))
            oc[-1].start()
    finish(oc)


def query_grad_kernel(ftags, *refs):
    nf = len(ftags)
    fr = refs[:nf]
    ins = refs[nf : nf + 7]
    state_ref, att_ref, parts_ref = refs[nf + 7 : nf + 10]
    a_s, q_s, g_s, near0, near1, dq0, dq1, lam_s, att_s, tot_s, grad_s, fsem, isem, osem = refs[nf + 10 :]
    fc = feature_copies(ftags, fr, a_s, fsem)
    ic = plain_copies(ins, [q_s, g_s, near0, near1, dq0, dq1, lam_s], isem)
    begin(ic + fc)
    finish(ic)
    for h in range(HEADS_HERE):
        cols = pl.ds(h * HD, HD)
        q, g = q_s[:, cols], g_s[:, cols]
        out = (near0, near1)[h][...]
        total = (dq0, dq1)[h][...]
        for b in range(FAR):
            at = h * LEVELS + NEAR + b
            lam = lam_s[:, at : at + 1]
            state = state_ref[b, h]
            out = out + lam * dot(q, state)
            total = total + lam * dot_nt(g, state)
        att_s[:, cols] = out.astype(BF16)
        tot_s[:, cols] = total.astype(BF16)
    oc = [pltpu.make_async_copy(att_s, att_ref, osem.at[ZN])]
    begin(oc)
    finish(fc)
    x = lax.axis_index("x")
    for i in range(ZN):
        r = i * 256
        grad_s[pl.ds(r, 256), :] = dot_tn(a_s[:, pl.ds(r, 256)], tot_s[...]).astype(BF16)
        rx = lax.rem(r // (ZN * PIECE) + (XN - x), XN)
        at = r % (ZN * PIECE)
        src = grad_s.at[pl.ds(r, 256), :]
        oc.append(pltpu.make_async_copy(src, parts_ref.at[rx, pl.ds(at, 256), :], osem.at[i]))
        oc[-1].start()
    finish(oc)


HBM = pl.BlockSpec(memory_space=pltpu.HBM)
VM = pl.BlockSpec(memory_space=pltpu.VMEM)


def struct(shape, dtype):
    return jax.ShapeDtypeStruct(shape, dtype)


def call(body, name, inputs, specs, outs, out_specs, scratch, flops, moved):
    return pl.pallas_call(
        body,
        name=name,
        in_specs=specs,
        out_specs=out_specs,
        out_shape=outs,
        scratch_shapes=scratch,
        compiler_params=pltpu.CompilerParams(vmem_limit_bytes=VMEM_LIMIT),
        cost_estimate=pl.CostEstimate(flops=flops, transcendentals=0, bytes_accessed=moved),
    )(*inputs)


def on_device(activations, w_query, w_key, w_value, level_table, table_rows, out_grad):
    x = lax.axis_index("x")
    z = lax.axis_index("z")
    pair = lax.shift_right_logical(z, 1)

    weights = jnp.concatenate([w_query, w_key, w_value], axis=1)
    along = [weights] + [shifted(weights, "x", -off) for off in (1, 2, 3)]
    weights = lax.all_gather(jnp.concatenate(along, axis=0), "z", axis=0)

    feats = features_of(activations)
    ftags = [(off, same) for off, same, _ in feats]
    fparts = [part for _, _, part in feats]
    nf = len(ftags)

    scale = 1.0 / math.sqrt(HD * TOK)
    table_size = level_table.shape[1]
    onehot = (table_rows[:, None] == jnp.arange(table_size, dtype=jnp.int32)[None, :]).astype(F32)
    flat = jnp.transpose(level_table, (1, 0, 2)).reshape(table_size, HEADS_HERE * LEVELS)
    lam = scale * jnp.dot(onehot, flat, precision=lax.Precision.HIGHEST)

    dma = pltpu.SemaphoreType.DMA
    wide = pltpu.VMEM((TOK, WIDTH), BF16)
    block = pltpu.VMEM((TOK, COLS), BF16)
    narrow = pltpu.VMEM((TOK, HD), BF16)
    near_f32 = pltpu.VMEM((TOK, HD), F32)
    lam_held = pltpu.VMEM((TOK, HEADS_HERE * LEVELS), F32)
    state = (HEADS_HERE, HD, HD)

    queries, keys, values, local, s1, s2, s3, by_pair, by_one = call(
        functools.partial(projection_kernel, ftags),
        "projections",
        [*fparts, weights, out_grad, lam],
        [HBM] * (nf + 3),
        [struct((TOK, COLS), BF16)] * 3
        + [struct(state, F32)]
        + [struct(state, BF16)] * 3
        + [struct((3, *state), F32), struct(state, F32)],
        [HBM] * 3 + [VM] * 6,
        [
            wide,
            pltpu.VMEM((WIDTH, 3 * COLS), BF16),
            block,
            lam_held,
            block,
            block,
            block,
            dma((nf,)),
            dma((ZN, XN)),
            dma((2,)),
            dma((4, 3)),
        ],
        1 << 20,
        1 << 10,
    )

    after_one = [shifted(part, "x", -off) for off, part in zip((1, 2, 3), (s1, s2, s3))]
    pending = sum(part.astype(F32) for part in after_one)
    after_two = [
        shifted((pending + by_pair[i]).astype(BF16), "z", -2 * off) for i, off in enumerate((1, 2, 3))
    ]
    pending = pending + sum(part.astype(F32) for part in after_two)
    pending = pending + swapped((pending + by_one).astype(BF16), "z", 1).astype(F32)

    none = jnp.zeros(state, BF16)

    def among_four(value, index, axis, stride):
        sent = value.astype(BF16)
        got = {off: shifted(sent, axis, off * stride) for off in (1, 2, 3)}
        full = {off: part.astype(F32) for off, part in got.items()}
        first = jnp.where((index & 1) != 0, got[1], none)
        other = full[2] + jnp.where(index == 2, full[1], full[3])
        second = jnp.where(index >= 2, other.astype(BF16), none)
        return first, second, value + full[1] + full[2] + full[3]

    local, *_ = lax.optimization_barrier((local, *after_one))
    sibling = swapped(local, "z", 1)
    state0 = jnp.where((z & 1) != 0, sibling, 0.0).astype(BF16)
    total = local + sibling
    near = []
    for h, gate in enumerate(([], after_one)):
        first, *_ = lax.optimization_barrier((queries, *gate))
        near.append(
            call(
                functools.partial(near_kernel, h),
                "near",
                [first, keys, values, out_grad, lam],
                [HBM] * 5,
                [struct((TOK, HD), F32)] * 4,
                [HBM] * 4,
                [narrow] * 4 + [lam_held] + [near_f32] * 4 + [dma((5,)), dma((4,))],
                2 << 30,
                8 << 20,
            )
        )
    near_out, query_near, key_near, value_near = (list(parts) for parts in zip(*near))

    total, pending = lax.optimization_barrier((total, pending))
    state1, state2, total = among_four(total, pair, "z", 2)
    state3, state4, total = among_four(total, x, "x", 1)
    states = jnp.stack([state0, state1, state2, state3, state4])

    part = WIDTH // XN
    (parts,) = call(
        functools.partial(key_value_grad_kernel, ftags),
        "key_value_grad",
        [*fparts, keys, values, *key_near, *value_near, pending],
        [HBM] * (nf + 6) + [VM],
        [struct((WIDTH, 2 * COLS), BF16)],
        [HBM],
        [
            wide,
            block,
            block,
            *[near_f32] * 4,
            pltpu.VMEM((TOK, 2 * COLS), BF16),
            pltpu.VMEM((WIDTH, 2 * COLS), BF16),
            dma((nf,)),
            dma((6,)),
            dma((WIDTH // PIECE,)),
        ],
        1 << 20,
        1 << 10,
    )
    kv_sum = lax.psum_scatter(parts, "z", scatter_dimension=0, tiled=True)

    query_near[0], _ = lax.optimization_barrier((query_near[0], parts))
    attended, sums = call(
        functools.partial(query_grad_kernel, ftags),
        "query_grad",
        [*fparts, queries, out_grad, *near_out, *query_near, lam, states],
        [HBM] * (nf + 7) + [VM],
        [struct((TOK, COLS), BF16), struct((XN, part, COLS), BF16)],
        [HBM] * 2,
        [
            wide,
            block,
            block,
            *[near_f32] * 4,
            lam_held,
            block,
            block,
            pltpu.VMEM((WIDTH, COLS), BF16),
            dma((nf,)),
            dma((7,)),
            dma((ZN + 1,)),
        ],
        8 << 30,
        8 << 20,
    )
    mine = sums[0].astype(F32)
    for off in (1, 2, 3):
        mine = mine + shifted(sums[off], "x", off).astype(F32)
    gathered = lax.all_to_all(mine.astype(BF16).reshape(ZN, PIECE, COLS), "z", 0, 0, tiled=True)
    grad_query = jnp.sum(gathered.astype(F32), axis=0)

    kv_sum = kv_sum.reshape(XN, PIECE, 2 * COLS)
    grad_kv = kv_sum[0].astype(F32)
    for off in (1, 2, 3):
        grad_kv = grad_kv + shifted(kv_sum[off], "x", off).astype(F32)
    return attended, grad_query, grad_kv[:, :COLS], grad_kv[:, COLS:]


def solution(mesh):
    finer = Mesh(mesh.devices.reshape(XN, ZN, YN, 2), ("x", "z", "y", "core"))
    rows, cols = ("x", "z"), ("y", "core")
    return jax.shard_map(
        on_device,
        mesh=finer,
        in_specs=(
            P(rows, cols),
            P(rows, cols),
            P(rows, cols),
            P(rows, cols),
            P(cols, None, None),
            P(rows),
            P(rows, cols),
        ),
        out_specs=(P(rows, cols), P(rows, cols), P(rows, cols), P(rows, cols)),
        check_vma=False,
    )
```

```python
import functools
import math

import jax
import jax.numpy as jnp
from jax import lax
from jax.experimental import pallas as pl
from jax.experimental.pallas import tpu as pltpu
from jax.sharding import Mesh
from jax.sharding import PartitionSpec as P

F32 = jnp.float32
BF16 = jnp.bfloat16
VMEM_LIMIT = 56 * 1024 * 1024

TOK = 1024
WIDTH = 2048
COLS = 256
HD = 128
HEADS_HERE = 2
LEVELS = 16
NEAR = 11
FAR = 5
XN, ZN, YN = 4, 8, 4
PIECE = WIDTH // (XN * ZN)


def shifted(value, axis, offset):
    count = lax.axis_size(axis)
    return lax.ppermute(value, axis, [(i, (i + offset) % count) for i in range(count)])


def swapped(value, axis, bit):
    count = lax.axis_size(axis)
    return lax.ppermute(value, axis, [(i, i ^ bit) for i in range(count)])


def features_of(block):
    mine = [(0, block)] + [(off, shifted(block, "y", -off)) for off in (1, -1, 2)]
    found = [(off, True, part) for off, part in mine]
    found += [(off, False, shifted(part, "core", 1)) for off, part in mine]
    return found


def dot(a, b):
    return lax.dot_general(a, b, (((1,), (0,)), ((), ())), preferred_element_type=F32)


def dot_nt(a, b):
    return lax.dot_general(a, b, (((1,), (1,)), ((), ())), preferred_element_type=F32)


def dot_tn(a, b):
    return lax.dot_general(a, b, (((0,), (0,)), ((), ())), preferred_element_type=F32)


def feature_copies(tags, refs, scratch, sem):
    y = lax.axis_index("y")
    core = lax.axis_index("core")
    copies = []
    for i, ((off, same), ref) in enumerate(zip(tags, refs)):
        block = lax.rem(y + (off + YN), YN) * 2 + (core if same else 1 - core)
        cols = pl.ds(pl.multiple_of(block * COLS, COLS), COLS)
        copies.append(pltpu.make_async_copy(ref, scratch.at[:, cols], sem.at[i]))
    return copies


def weight_copies(ref, scratch, sem):
    x = lax.axis_index("x")
    copies = []
    for z in range(ZN):
        for rx in range(XN):
            xx = lax.rem(x + rx, XN)
            rows = pl.ds(pl.multiple_of((xx * ZN + z) * PIECE, PIECE), PIECE)
            src = ref.at[z, pl.ds(rx * PIECE, PIECE), :]
            copies.append(pltpu.make_async_copy(src, scratch.at[rows, :], sem.at[z, rx]))
    return copies


def begin(copies):
    for copy in copies:
        copy.start()


def finish(copies):
    for copy in copies:
        copy.wait()


def projection_kernel(ftags, *refs):
    nf = len(ftags)
    fr = refs[:nf]
    w_ref, g_s, lam_s, q_s, k_s, v_s, local_ref = refs[nf : nf + 7]
    send_refs = refs[nf + 7 : nf + 10]
    pair_ref, one_ref = refs[nf + 10 : nf + 12]
    a_s, w_s, fsem, wsem = refs[nf + 12 :]
    fc = feature_copies(ftags, fr, a_s, fsem)
    wc = weight_copies(w_ref, w_s, wsem)
    begin(wc + fc)
    finish(wc + fc)
    step = 256
    for r in range(0, TOK, step):
        rows = pl.ds(r, step)
        both = dot(a_s[rows, :], w_s[...]).astype(BF16)
        for i, held in enumerate((q_s, k_s, v_s)):
            held[rows, :] = both[:, i * COLS : (i + 1) * COLS]
    x = lax.axis_index("x")
    pair = lax.div(lax.axis_index("z"), 2)
    low = lax.rem(lax.axis_index("z"), 2)
    for h in range(HEADS_HERE):
        cols = pl.ds(h * HD, HD)
        q = q_s[:, cols].astype(F32)
        g = g_s[:, cols]
        states = []
        for b in range(FAR):
            at = h * LEVELS + NEAR + b
            states.append(dot_tn((lam_s[:, at : at + 1] * q).astype(BF16), g))
        local_ref[h] = dot_tn(k_s[:, cols], v_s[:, cols])
        one_ref[h] = jnp.where(low == 1, states[0], 0.0)
        for i, off in enumerate((1, 2, 3)):
            to = lax.rem(pair + (4 - off), 4)
            sibling = lax.div(pair, 2) == lax.div(to, 2)
            pair_ref[i, h] = jnp.where(to < pair, jnp.where(sibling, states[1], states[2]), 0.0)
            to = lax.rem(x + (XN - off), XN)
            sibling = lax.div(x, 2) == lax.div(to, 2)
            level = jnp.where(to < x, jnp.where(sibling, states[3], states[4]), 0.0)
            send_refs[i][h] = level.astype(BF16)


def near_kernel(h, q_all, k_all, v_all, g_all, lam_s, out_ref, dq_ref, dk_ref, dv_ref):
    cols = pl.ds(h * HD, HD)
    q_s, k_s, v_s, g_s = (ref.at[:, cols] for ref in (q_all, k_all, v_all, g_all))
    tile = 128
    t_at = lax.broadcasted_iota(jnp.int32, (tile, tile), 0)
    s_at = lax.broadcasted_iota(jnp.int32, (tile, tile), 1)
    apart = jnp.bitwise_xor(t_at, s_at)
    causal = t_at >= s_at
    for i in range(TOK // tile):
        rows = pl.ds(i * tile, tile)
        q, k, v, g = q_s[rows, :], k_s[rows, :], v_s[rows, :], g_s[rows, :]
        lam = lam_s[rows, pl.ds(h * LEVELS, LEVELS)]
        mix = jnp.broadcast_to(lam[:, 0:1], (tile, tile))
        for level in range(1, 8):
            mix = jnp.where(apart >= 1 << (level - 1), lam[:, level : level + 1], mix)
        mix = jnp.where(causal, mix, 0.0)
        probs = (mix * dot_nt(q, k)).astype(BF16)
        mixed = (mix * dot_nt(g, v)).astype(BF16)
        out_ref[rows, :] = dot(probs, v)
        dq_ref[rows, :] = dot(mixed, k)
        dk_ref[rows, :] = dot_tn(mixed, q)
        dv_ref[rows, :] = dot_tn(probs, g)
    for level in range(8, NEAR):
        size = tile << (level - 8)
        for at in range(0, TOK, 2 * size):
            early, late = pl.ds(at, size), pl.ds(at + size, size)
            k, v = k_s[early, :], v_s[early, :]
            q, g = q_s[late, :], g_s[late, :]
            lam = lam_s[late, h * LEVELS + level : h * LEVELS + level + 1]
            state = dot_tn(k, v).astype(BF16)
            back = dot_tn((lam * q.astype(F32)).astype(BF16), g).astype(BF16)
            out_ref[late, :] += lam * dot(q, state)
            dq_ref[late, :] += lam * dot_nt(g, state)
            dk_ref[early, :] += dot_nt(v, back)
            dv_ref[early, :] += dot(k, back)


def key_value_grad_kernel(ftags, *refs):
    nf = len(ftags)
    fr = refs[:nf]
    k_s, v_s, dk0, dk1, dv0, dv1, back_ref, parts_ref = refs[nf : nf + 8]
    a_s, tot_s, grad_s, fsem, osem = refs[nf + 8 :]
    fc = feature_copies(ftags, fr, a_s, fsem)
    begin(fc)
    for h in range(HEADS_HERE):
        cols = pl.ds(h * HD, HD)
        back = back_ref[h].astype(BF16)
        tot_s[:, cols] = ((dk0, dk1)[h][...] + dot_nt(v_s[:, cols], back)).astype(BF16)
        tot_s[:, pl.ds(COLS + h * HD, HD)] = ((dv0, dv1)[h][...] + dot(k_s[:, cols], back)).astype(BF16)
    finish(fc)
    x = lax.axis_index("x")
    oc = []
    for r in range(0, WIDTH, 256):
        grad_s[pl.ds(r, 256), :] = dot_tn(a_s[:, pl.ds(r, 256)], tot_s[...]).astype(BF16)
        xx = r // (ZN * PIECE)
        rx = lax.rem(xx + (XN - x), XN)
        for i in range(256 // PIECE):
            z = r % (ZN * PIECE) // PIECE + i
            to = pl.ds(pl.multiple_of((z * XN + rx) * PIECE, PIECE), PIECE)
            src = grad_s.at[pl.ds(r + i * PIECE, PIECE), :]
            oc.append(pltpu.make_async_copy(src, parts_ref.at[to, :], osem.at[r // PIECE + i]))
            oc[-1].start()
    finish(oc)


def query_grad_kernel(ftags, *refs):
    nf = len(ftags)
    fr = refs[:nf]
    q_s, g_s, near0, near1, dq0, dq1, lam_s, state_ref, att_s, parts_ref = refs[nf : nf + 10]
    a_s, tot_s, grad_s, fsem, osem = refs[nf + 10 :]
    fc = feature_copies(ftags, fr, a_s, fsem)
    begin(fc)
    for h in range(HEADS_HERE):
        cols = pl.ds(h * HD, HD)
        q, g = q_s[:, cols], g_s[:, cols]
        out = (near0, near1)[h][...]
        total = (dq0, dq1)[h][...]
        for b in range(FAR):
            at = h * LEVELS + NEAR + b
            lam = lam_s[:, at : at + 1]
            state = state_ref[b, h]
            out = out + lam * dot(q, state)
            total = total + lam * dot_nt(g, state)
        att_s[:, cols] = out.astype(BF16)
        tot_s[:, cols] = total.astype(BF16)
    finish(fc)
    oc = []
    for i in range(ZN):
        rows = pl.ds(i * 256, 256)
        grad_s[rows, :] = dot_tn(a_s[:, rows], tot_s[...]).astype(BF16)
        oc.append(pltpu.make_async_copy(grad_s.at[rows, :], parts_ref.at[rows, :], osem.at[i]))
        oc[-1].start()
    finish(oc)


HBM = pl.BlockSpec(memory_space=pltpu.HBM)
VM = pl.BlockSpec(memory_space=pltpu.VMEM)


def struct(shape, dtype):
    return jax.ShapeDtypeStruct(shape, dtype)


def call(body, name, inputs, specs, outs, out_specs, scratch, flops, moved):
    return pl.pallas_call(
        body,
        name=name,
        in_specs=specs,
        out_specs=out_specs,
        out_shape=outs,
        scratch_shapes=scratch,
        compiler_params=pltpu.CompilerParams(vmem_limit_bytes=VMEM_LIMIT),
        cost_estimate=pl.CostEstimate(flops=flops, transcendentals=0, bytes_accessed=moved),
    )(*inputs)


def on_device(activations, w_query, w_key, w_value, level_table, table_rows, out_grad):
    x = lax.axis_index("x")
    z = lax.axis_index("z")
    pair = lax.shift_right_logical(z, 1)

    weights = jnp.concatenate([w_query, w_key, w_value], axis=1)
    along = [weights] + [shifted(weights, "x", -off) for off in (1, 2, 3)]
    weights = lax.all_gather(jnp.concatenate(along, axis=0), "z", axis=0)

    feats = features_of(activations)
    ftags = [(off, same) for off, same, _ in feats]
    fparts = [part for _, _, part in feats]
    nf = len(ftags)

    scale = 1.0 / math.sqrt(HD * TOK)
    table_size = level_table.shape[1]
    onehot = (table_rows[:, None] == jnp.arange(table_size, dtype=jnp.int32)[None, :]).astype(F32)
    flat = jnp.transpose(level_table, (1, 0, 2)).reshape(table_size, HEADS_HERE * LEVELS)
    lam = scale * jnp.dot(onehot, flat, precision=lax.Precision.HIGHEST)

    dma = pltpu.SemaphoreType.DMA
    wide = pltpu.VMEM((TOK, WIDTH), BF16)
    block = pltpu.VMEM((TOK, COLS), BF16)
    state = (HEADS_HERE, HD, HD)

    queries, keys, values, local, s1, s2, s3, by_pair, by_one = call(
        functools.partial(projection_kernel, ftags),
        "projections",
        [*fparts, weights, out_grad, lam],
        [HBM] * (nf + 1) + [VM] * 2,
        [struct((TOK, COLS), BF16)] * 3
        + [struct(state, F32)]
        + [struct(state, BF16)] * 3
        + [struct((3, *state), F32), struct(state, F32)],
        [VM] * 9,
        [
            wide,
            pltpu.VMEM((WIDTH, 3 * COLS), BF16),
            dma((nf,)),
            dma((ZN, XN)),
        ],
        1 << 20,
        1 << 10,
    )

    after_one = [shifted(part, "x", -off) for off, part in zip((1, 2, 3), (s1, s2, s3))]
    pending = sum(part.astype(F32) for part in after_one)
    after_two = [
        shifted((pending + by_pair[i]).astype(BF16), "z", -2 * off) for i, off in enumerate((1, 2, 3))
    ]

    def near_of(h, gate):
        first, *_ = lax.optimization_barrier((queries, *gate))
        return call(
            functools.partial(near_kernel, h),
            "near",
            [first, keys, values, out_grad, lam],
            [VM] * 5,
            [struct((TOK, HD), F32)] * 4,
            [VM] * 4,
            [],
            2 << 30,
            8 << 20,
        )

    near = [near_of(0, after_one)]
    *after_two, _ = lax.optimization_barrier((*after_two, near[0][0]))
    pending = pending + sum(part.astype(F32) for part in after_two)
    pending = pending + swapped((pending + by_one).astype(BF16), "z", 1).astype(F32)

    none = jnp.zeros(state, BF16)

    def among_four(value, index, axis, stride):
        sent = value.astype(BF16)
        got = {off: shifted(sent, axis, off * stride) for off in (1, 2, 3)}
        full = {off: part.astype(F32) for off, part in got.items()}
        first = jnp.where((index & 1) != 0, got[1], none)
        other = full[2] + jnp.where(index == 2, full[1], full[3])
        second = jnp.where(index >= 2, other.astype(BF16), none)
        return first, second, value + full[1] + full[2] + full[3]

    local, *_ = lax.optimization_barrier((local, *after_one))
    sibling = swapped(local, "z", 1)
    state0 = jnp.where((z & 1) != 0, sibling, 0.0).astype(BF16)
    total = local + sibling
    near.append(near_of(1, [*after_two, sibling]))
    near_out, query_near, key_near, value_near = (list(parts) for parts in zip(*near))

    total, *_ = lax.optimization_barrier((total, *after_two))
    state1, state2, total = among_four(total, pair, "z", 2)
    key_near[0], _ = lax.optimization_barrier((key_near[0], total))
    state3, state4, total = among_four(total, x, "x", 1)
    states = jnp.stack([state0, state1, state2, state3, state4])

    (parts,) = call(
        functools.partial(key_value_grad_kernel, ftags),
        "key_value_grad",
        [*fparts, keys, values, *key_near, *value_near, pending],
        [HBM] * nf + [VM] * 7,
        [struct((WIDTH, 2 * COLS), BF16)],
        [HBM],
        [
            wide,
            pltpu.VMEM((TOK, 2 * COLS), BF16),
            pltpu.VMEM((WIDTH, 2 * COLS), BF16),
            dma((nf,)),
            dma((WIDTH // PIECE,)),
        ],
        8 << 30,
        8 << 20,
    )
    parts, states = lax.optimization_barrier((parts, states))
    kv_sum = lax.psum_scatter(parts, "z", scatter_dimension=0, tiled=True)

    query_near[0], _ = lax.optimization_barrier((query_near[0], parts))
    attended, sums = call(
        functools.partial(query_grad_kernel, ftags),
        "query_grad",
        [*fparts, queries, out_grad, *near_out, *query_near, lam, states],
        [HBM] * nf + [VM] * 8,
        [struct((TOK, COLS), BF16), struct((WIDTH, COLS), BF16)],
        [VM, HBM],
        [
            wide,
            block,
            pltpu.VMEM((WIDTH, COLS), BF16),
            dma((nf,)),
            dma((ZN,)),
        ],
        8 << 30,
        8 << 20,
    )
    gathered = lax.all_to_all(sums.reshape(XN * ZN, PIECE, COLS), ("x", "z"), 0, 0, tiled=True)
    grad_query = jnp.sum(gathered.astype(F32), axis=0)

    kv_sum = kv_sum.reshape(XN, PIECE, 2 * COLS)
    grad_kv = kv_sum[0].astype(F32)
    for off in (1, 2, 3):
        grad_kv = grad_kv + shifted(kv_sum[off], "x", off).astype(F32)
    return attended, grad_query, grad_kv[:, :COLS], grad_kv[:, COLS:]


def solution(mesh):
    finer = Mesh(mesh.devices.reshape(XN, ZN, YN, 2), ("x", "z", "y", "core"))
    rows, cols = ("x", "z"), ("y", "core")
    return jax.shard_map(
        on_device,
        mesh=finer,
        in_specs=(
            P(rows, cols),
            P(rows, cols),
            P(rows, cols),
            P(rows, cols),
            P(cols, None, None),
            P(rows),
            P(rows, cols),
        ),
        out_specs=(P(rows, cols), P(rows, cols), P(rows, cols), P(rows, cols)),
        check_vma=False,
    )
```

```python
import functools
import math

import jax
import jax.numpy as jnp
from jax import lax
from jax.experimental import pallas as pl
from jax.experimental.pallas import tpu as pltpu
from jax.sharding import Mesh
from jax.sharding import PartitionSpec as P

F32 = jnp.float32
BF16 = jnp.bfloat16
VMEM_LIMIT = 56 * 1024 * 1024

TOK = 1024
WIDTH = 2048
COLS = 256
HD = 128
HEADS_HERE = 2
LEVELS = 16
NEAR = 11
FAR = 5
XN, ZN, YN = 4, 8, 4
PIECE = WIDTH // (XN * ZN)


def shifted(value, axis, offset):
    count = lax.axis_size(axis)
    return lax.ppermute(value, axis, [(i, (i + offset) % count) for i in range(count)])


def swapped(value, axis, bit):
    count = lax.axis_size(axis)
    return lax.ppermute(value, axis, [(i, i ^ bit) for i in range(count)])


def features_of(block):
    mine = [(0, block)] + [(off, shifted(block, "y", -off)) for off in (1, -1, 2)]
    found = [(off, True, part) for off, part in mine]
    found += [(off, False, shifted(part, "core", 1)) for off, part in mine]
    return found


def dot(a, b):
    return lax.dot_general(a, b, (((1,), (0,)), ((), ())), preferred_element_type=F32)


def dot_nt(a, b):
    return lax.dot_general(a, b, (((1,), (1,)), ((), ())), preferred_element_type=F32)


def dot_tn(a, b):
    return lax.dot_general(a, b, (((0,), (0,)), ((), ())), preferred_element_type=F32)


def feature_copies(tags, refs, scratch, sem):
    y = lax.axis_index("y")
    core = lax.axis_index("core")
    copies = []
    for i, ((off, same), ref) in enumerate(zip(tags, refs)):
        block = lax.rem(y + (off + YN), YN) * 2 + (core if same else 1 - core)
        cols = pl.ds(pl.multiple_of(block * COLS, COLS), COLS)
        copies.append(pltpu.make_async_copy(ref, scratch.at[:, cols], sem.at[i]))
    return copies


def weight_copies(ref, scratch, sem):
    x = lax.axis_index("x")
    copies = []
    for z in range(ZN):
        for rx in range(XN):
            xx = lax.rem(x + rx, XN)
            rows = pl.ds(pl.multiple_of((xx * ZN + z) * PIECE, PIECE), PIECE)
            src = ref.at[z, pl.ds(rx * PIECE, PIECE), :]
            copies.append(pltpu.make_async_copy(src, scratch.at[rows, :], sem.at[z, rx]))
    return copies


def begin(copies):
    for copy in copies:
        copy.start()


def finish(copies):
    for copy in copies:
        copy.wait()


def projection_kernel(ftags, *refs):
    nf = len(ftags)
    fr = refs[:nf]
    w_ref, g_s, lam_s, q_s, k_s, v_s, local_ref = refs[nf : nf + 7]
    send_refs = refs[nf + 7 : nf + 10]
    pair_ref, one_ref = refs[nf + 10 : nf + 12]
    a_s, w_s, fsem, wsem = refs[nf + 12 :]
    fc = feature_copies(ftags, fr, a_s, fsem)
    wc = weight_copies(w_ref, w_s, wsem)
    begin(wc + fc)
    finish(wc + fc)
    step = 256
    for r in range(0, TOK, step):
        rows = pl.ds(r, step)
        both = dot(a_s[rows, :], w_s[...]).astype(BF16)
        for i, held in enumerate((q_s, k_s, v_s)):
            held[rows, :] = both[:, i * COLS : (i + 1) * COLS]
    x = lax.axis_index("x")
    pair = lax.div(lax.axis_index("z"), 2)
    low = lax.rem(lax.axis_index("z"), 2)
    for h in range(HEADS_HERE):
        cols = pl.ds(h * HD, HD)
        q = q_s[:, cols].astype(F32)
        g = g_s[:, cols]
        states = []
        for b in range(FAR):
            at = h * LEVELS + NEAR + b
            states.append(dot_tn((lam_s[:, at : at + 1] * q).astype(BF16), g))
        local_ref[h] = dot_tn(k_s[:, cols], v_s[:, cols])
        one_ref[h] = jnp.where(low == 1, states[0], 0.0)
        for i, off in enumerate((1, 2, 3)):
            to = lax.rem(pair + (4 - off), 4)
            sibling = lax.div(pair, 2) == lax.div(to, 2)
            pair_ref[i, h] = jnp.where(to < pair, jnp.where(sibling, states[1], states[2]), 0.0)
            to = lax.rem(x + (XN - off), XN)
            sibling = lax.div(x, 2) == lax.div(to, 2)
            level = jnp.where(to < x, jnp.where(sibling, states[3], states[4]), 0.0)
            send_refs[i][h] = level.astype(BF16)


def near_kernel(h, *refs):
    ins, lam_ref, outs = refs[:4], refs[4], refs[5:9]
    held = refs[9:13]
    lam_s, sums = refs[13], refs[14:18]
    isem, osem = refs[18:]
    q_s, k_s, v_s, g_s = held
    cols = pl.ds(h * HD, HD)
    half = TOK // 2
    copies = {}
    for name, i, part in (
        ("k0", 1, 0),
        ("v0", 2, 0),
        ("q1", 0, 1),
        ("g1", 3, 1),
        ("k1", 1, 1),
        ("v1", 2, 1),
        ("q0", 0, 0),
        ("g0", 3, 0),
    ):
        rows = pl.ds(part * half, half)
        copies[name] = pltpu.make_async_copy(ins[i].at[rows, cols], held[i].at[rows, :], isem.at[i, part])
    lam_copy = pltpu.make_async_copy(lam_ref, lam_s, isem.at[4, 0])
    early_ones = [copies[name] for name in ("k0", "v0", "q1", "g1")]
    late_ones = [copies[name] for name in ("k1", "v1", "q0", "g0")]
    begin([*early_ones[:2], lam_copy, *early_ones[2:], *late_ones])
    tile = 128
    t_at = lax.broadcasted_iota(jnp.int32, (tile, tile), 0)
    s_at = lax.broadcasted_iota(jnp.int32, (tile, tile), 1)
    apart = jnp.bitwise_xor(t_at, s_at)
    causal = t_at >= s_at
    begun = [set(), set(), set(), set()]

    def add(which, start, value):
        for i in range(value.shape[0] // tile):
            at = start + i * tile
            rows = pl.ds(at, tile)
            piece = value[i * tile : (i + 1) * tile, :]
            if at in begun[which]:
                piece = sums[which][rows, :] + piece
            begun[which].add(at)
            sums[which][rows, :] = piece

    finish([*early_ones, lam_copy])
    for level in reversed(range(8, NEAR)):
        size = tile << (level - 8)
        for at in range(0, TOK, 2 * size):
            early, late = pl.ds(at, size), pl.ds(at + size, size)
            k, v = k_s[early, :], v_s[early, :]
            q, g = q_s[late, :], g_s[late, :]
            lam = lam_s[late, h * LEVELS + level : h * LEVELS + level + 1]
            state = dot_tn(k, v).astype(BF16)
            back = dot_tn((lam * q.astype(F32)).astype(BF16), g).astype(BF16)
            add(0, at + size, lam * dot(q, state))
            add(1, at + size, lam * dot_nt(g, state))
            add(2, at, dot_nt(v, back))
            add(3, at, dot(k, back))
        if level == NEAR - 1:
            finish(late_ones)
    oc = []
    for i in range(TOK // tile):
        rows = pl.ds(i * tile, tile)
        q, k, v, g = q_s[rows, :], k_s[rows, :], v_s[rows, :], g_s[rows, :]
        lam = lam_s[rows, pl.ds(h * LEVELS, LEVELS)]
        mix = jnp.broadcast_to(lam[:, 0:1], (tile, tile))
        for level in range(1, 8):
            mix = jnp.where(apart >= 1 << (level - 1), lam[:, level : level + 1], mix)
        mix = jnp.where(causal, mix, 0.0)
        probs = (mix * dot_nt(q, k)).astype(BF16)
        mixed = (mix * dot_nt(g, v)).astype(BF16)
        add(0, i * tile, dot(probs, v))
        add(1, i * tile, dot(mixed, k))
        add(2, i * tile, dot_tn(mixed, q))
        add(3, i * tile, dot_tn(probs, g))
        for which in range(4):
            src, to = sums[which].at[rows, :], outs[which].at[rows, :]
            oc.append(pltpu.make_async_copy(src, to, osem.at[which, i]))
            oc[-1].start()
    finish(oc)


def key_value_grad_kernel(ftags, *refs):
    nf = len(ftags)
    fr = refs[:nf]
    k_s, v_s, dk0, dk1, dv0, dv1, back_ref, parts_ref = refs[nf : nf + 8]
    a_s, tot_s, grad_s, fsem, osem = refs[nf + 8 :]
    fc = feature_copies(ftags, fr, a_s, fsem)
    begin(fc)
    for h in range(HEADS_HERE):
        cols = pl.ds(h * HD, HD)
        back = back_ref[h].astype(BF16)
        tot_s[:, cols] = ((dk0, dk1)[h][...] + dot_nt(v_s[:, cols], back)).astype(BF16)
        tot_s[:, pl.ds(COLS + h * HD, HD)] = ((dv0, dv1)[h][...] + dot(k_s[:, cols], back)).astype(BF16)
    finish(fc)
    x = lax.axis_index("x")
    oc = []
    for r in range(0, WIDTH, 256):
        grad_s[pl.ds(r, 256), :] = dot_tn(a_s[:, pl.ds(r, 256)], tot_s[...]).astype(BF16)
        xx = r // (ZN * PIECE)
        rx = lax.rem(xx + (XN - x), XN)
        for i in range(256 // PIECE):
            z = r % (ZN * PIECE) // PIECE + i
            to = pl.ds(pl.multiple_of((z * XN + rx) * PIECE, PIECE), PIECE)
            src = grad_s.at[pl.ds(r + i * PIECE, PIECE), :]
            oc.append(pltpu.make_async_copy(src, parts_ref.at[to, :], osem.at[r // PIECE + i]))
            oc[-1].start()
    finish(oc)


def query_grad_kernel(ftags, *refs):
    nf = len(ftags)
    fr = refs[:nf]
    q_s, g_s, near0, near1, dq0, dq1, lam_s, state_ref, att_s = refs[nf : nf + 9]
    outs = refs[nf + 9 : nf + 9 + XN]
    a_s, tot_s, grad_s, fsem, osem = refs[nf + 9 + XN :]
    fc = feature_copies(ftags, fr, a_s, fsem)
    begin(fc)
    for h in range(HEADS_HERE):
        cols = pl.ds(h * HD, HD)
        q, g = q_s[:, cols], g_s[:, cols]
        out = (near0, near1)[h][...]
        total = (dq0, dq1)[h][...]
        for b in range(FAR):
            at = h * LEVELS + NEAR + b
            lam = lam_s[:, at : at + 1]
            state = state_ref[b, h]
            out = out + lam * dot(q, state)
            total = total + lam * dot_nt(g, state)
        att_s[:, cols] = out.astype(BF16)
        tot_s[:, cols] = total.astype(BF16)
    finish(fc)
    oc = []
    x = lax.axis_index("x")
    part = WIDTH // XN
    for off in range(XN):
        xx = lax.rem(x + off, XN)
        for i in range(part // 256):
            cols = pl.ds(pl.multiple_of(xx * part + i * 256, 256), 256)
            rows = pl.ds(off * part + i * 256, 256)
            grad_s[rows, :] = dot_tn(a_s[:, cols], tot_s[...]).astype(BF16)
            to = outs[off].at[pl.ds(i * 256, 256), :]
            oc.append(pltpu.make_async_copy(grad_s.at[rows, :], to, osem.at[off * 2 + i]))
            oc[-1].start()
    finish(oc)


HBM = pl.BlockSpec(memory_space=pltpu.HBM)
VM = pl.BlockSpec(memory_space=pltpu.VMEM)


def struct(shape, dtype):
    return jax.ShapeDtypeStruct(shape, dtype)


def call(body, name, inputs, specs, outs, out_specs, scratch, flops, moved):
    return pl.pallas_call(
        body,
        name=name,
        in_specs=specs,
        out_specs=out_specs,
        out_shape=outs,
        scratch_shapes=scratch,
        compiler_params=pltpu.CompilerParams(vmem_limit_bytes=VMEM_LIMIT),
        cost_estimate=pl.CostEstimate(flops=flops, transcendentals=0, bytes_accessed=moved),
    )(*inputs)


def on_device(activations, w_query, w_key, w_value, level_table, table_rows, out_grad):
    x = lax.axis_index("x")
    z = lax.axis_index("z")
    pair = lax.shift_right_logical(z, 1)

    weights = jnp.concatenate([w_query, w_key, w_value], axis=1)
    along = [weights] + [shifted(weights, "x", -off) for off in (1, 2, 3)]
    weights = lax.all_gather(jnp.concatenate(along, axis=0), "z", axis=0)

    feats = features_of(activations)
    ftags = [(off, same) for off, same, _ in feats]
    fparts = [part for _, _, part in feats]
    nf = len(ftags)

    scale = 1.0 / math.sqrt(HD * TOK)
    table_size = level_table.shape[1]
    onehot = (table_rows[:, None] == jnp.arange(table_size, dtype=jnp.int32)[None, :]).astype(F32)
    flat = jnp.transpose(level_table, (1, 0, 2)).reshape(table_size, HEADS_HERE * LEVELS)
    lam = scale * jnp.dot(onehot, flat, precision=lax.Precision.HIGHEST)

    dma = pltpu.SemaphoreType.DMA
    wide = pltpu.VMEM((TOK, WIDTH), BF16)
    block = pltpu.VMEM((TOK, COLS), BF16)
    state = (HEADS_HERE, HD, HD)

    queries, keys, values, local, s1, s2, s3, by_pair, by_one = call(
        functools.partial(projection_kernel, ftags),
        "projections",
        [*fparts, weights, out_grad, lam],
        [HBM] * (nf + 1) + [VM] * 2,
        [struct((TOK, COLS), BF16)] * 3
        + [struct(state, F32)]
        + [struct(state, BF16)] * 3
        + [struct((3, *state), F32), struct(state, F32)],
        [VM] * 9,
        [
            wide,
            pltpu.VMEM((WIDTH, 3 * COLS), BF16),
            dma((nf,)),
            dma((ZN, XN)),
        ],
        1 << 20,
        1 << 10,
    )

    after_one = [shifted(part, "x", -off) for off, part in zip((1, 2, 3), (s1, s2, s3))]
    pending = sum(part.astype(F32) for part in after_one)
    after_two = [
        shifted((pending + by_pair[i]).astype(BF16), "z", -2 * off) for i, off in enumerate((1, 2, 3))
    ]

    def near_of(h, gate):
        first, *_ = lax.optimization_barrier((queries, *gate))
        return call(
            functools.partial(near_kernel, h),
            "near",
            [first, keys, values, out_grad, lam],
            [HBM] * 5,
            [struct((TOK, HD), F32)] * 4,
            [HBM] * 4,
            [pltpu.VMEM((TOK, HD), BF16)] * 4
            + [pltpu.VMEM((TOK, HEADS_HERE * LEVELS), F32)]
            + [pltpu.VMEM((TOK, HD), F32)] * 4
            + [dma((5, 2)), dma((4, TOK // 128))],
            2 << 30,
            8 << 20,
        )

    near = [near_of(0, after_one)]
    *after_two, _ = lax.optimization_barrier((*after_two, near[0][0]))
    pending = pending + sum(part.astype(F32) for part in after_two)
    pending = pending + swapped((pending + by_one).astype(BF16), "z", 1).astype(F32)

    none = jnp.zeros(state, BF16)

    def among_four(value, index, axis, stride):
        sent = value.astype(BF16)
        got = {off: shifted(sent, axis, off * stride) for off in (1, 2, 3)}
        full = {off: part.astype(F32) for off, part in got.items()}
        first = jnp.where((index & 1) != 0, got[1], none)
        other = full[2] + jnp.where(index == 2, full[1], full[3])
        second = jnp.where(index >= 2, other.astype(BF16), none)
        return first, second, value + full[1] + full[2] + full[3]

    local, *_ = lax.optimization_barrier((local, *after_one))
    sibling = swapped(local, "z", 1)
    state0 = jnp.where((z & 1) != 0, sibling, 0.0).astype(BF16)
    total = local + sibling
    near.append(near_of(1, [*after_two, sibling]))
    near_out, query_near, key_near, value_near = (list(parts) for parts in zip(*near))

    total, *_ = lax.optimization_barrier((total, *after_two))
    state1, state2, total = among_four(total, pair, "z", 2)
    key_near[0], _ = lax.optimization_barrier((key_near[0], total))
    state3, state4, total = among_four(total, x, "x", 1)
    states = jnp.stack([state0, state1, state2, state3, state4])

    (parts,) = call(
        functools.partial(key_value_grad_kernel, ftags),
        "key_value_grad",
        [*fparts, keys, values, *key_near, *value_near, pending],
        [HBM] * nf + [VM] * 7,
        [struct((WIDTH, 2 * COLS), BF16)],
        [HBM],
        [
            wide,
            pltpu.VMEM((TOK, 2 * COLS), BF16),
            pltpu.VMEM((WIDTH, 2 * COLS), BF16),
            dma((nf,)),
            dma((WIDTH // PIECE,)),
        ],
        8 << 30,
        8 << 20,
    )
    kv_sum = lax.psum_scatter(parts, "z", scatter_dimension=0, tiled=True)

    query_near[0], _ = lax.optimization_barrier((query_near[0], parts))
    attended, *sums = call(
        functools.partial(query_grad_kernel, ftags),
        "query_grad",
        [*fparts, queries, out_grad, *near_out, *query_near, lam, states],
        [HBM] * nf + [VM] * 8,
        [struct((TOK, COLS), BF16)] + [struct((WIDTH // XN, COLS), BF16)] * XN,
        [VM] + [HBM] * XN,
        [
            wide,
            block,
            pltpu.VMEM((WIDTH, COLS), BF16),
            dma((nf,)),
            dma((ZN,)),
        ],
        8 << 30,
        8 << 20,
    )
    mine = sums[0].astype(F32)
    for off in (1, 2, 3):
        mine = mine + shifted(sums[off], "x", off).astype(F32)
    gathered = lax.all_to_all(mine.astype(BF16).reshape(ZN, PIECE, COLS), "z", 0, 0, tiled=True)
    grad_query = jnp.sum(gathered.astype(F32), axis=0)

    kv_sum = kv_sum.reshape(XN, PIECE, 2 * COLS)
    grad_kv = kv_sum[0].astype(F32)
    for off in (1, 2, 3):
        grad_kv = grad_kv + shifted(kv_sum[off], "x", off).astype(F32)
    return attended, grad_query, grad_kv[:, :COLS], grad_kv[:, COLS:]


def solution(mesh):
    finer = Mesh(mesh.devices.reshape(XN, ZN, YN, 2), ("x", "z", "y", "core"))
    rows, cols = ("x", "z"), ("y", "core")
    return jax.shard_map(
        on_device,
        mesh=finer,
        in_specs=(
            P(rows, cols),
            P(rows, cols),
            P(rows, cols),
            P(rows, cols),
            P(cols, None, None),
            P(rows),
            P(rows, cols),
        ),
        out_specs=(P(rows, cols), P(rows, cols), P(rows, cols), P(rows, cols)),
        check_vma=False,
    )
```

```python
import functools
import math

import jax
import jax.numpy as jnp
from jax import lax
from jax.experimental import pallas as pl
from jax.experimental.pallas import tpu as pltpu
from jax.sharding import Mesh
from jax.sharding import PartitionSpec as P

F32 = jnp.float32
BF16 = jnp.bfloat16
VMEM_LIMIT = 56 * 1024 * 1024

TOK = 1024
WIDTH = 2048
COLS = 256
HD = 128
HEADS_HERE = 2
LEVELS = 16
NEAR = 11
FAR = 5
XN, ZN, YN = 4, 8, 4
PIECE = WIDTH // (XN * ZN)


def shifted(value, axis, offset):
    count = lax.axis_size(axis)
    return lax.ppermute(value, axis, [(i, (i + offset) % count) for i in range(count)])


def swapped(value, axis, bit):
    count = lax.axis_size(axis)
    return lax.ppermute(value, axis, [(i, i ^ bit) for i in range(count)])


def features_of(block):
    mine = [(0, block)] + [(off, shifted(block, "y", -off)) for off in (1, -1, 2)]
    found = [(off, True, part) for off, part in mine]
    found += [(off, False, shifted(part, "core", 1)) for off, part in mine]
    return found


def dot(a, b):
    return lax.dot_general(a, b, (((1,), (0,)), ((), ())), preferred_element_type=F32)


def dot_nt(a, b):
    return lax.dot_general(a, b, (((1,), (1,)), ((), ())), preferred_element_type=F32)


def dot_tn(a, b):
    return lax.dot_general(a, b, (((0,), (0,)), ((), ())), preferred_element_type=F32)


def feature_copies(tags, refs, scratch, sem):
    y = lax.axis_index("y")
    core = lax.axis_index("core")
    copies = []
    for i, ((off, same), ref) in enumerate(zip(tags, refs)):
        block = lax.rem(y + (off + YN), YN) * 2 + (core if same else 1 - core)
        cols = pl.ds(pl.multiple_of(block * COLS, COLS), COLS)
        copies.append(pltpu.make_async_copy(ref, scratch.at[:, cols], sem.at[i]))
    return copies


def weight_copies(ref, scratch, sem):
    x = lax.axis_index("x")
    copies = []
    for z in range(ZN):
        for rx in range(XN):
            xx = lax.rem(x + rx, XN)
            rows = pl.ds(pl.multiple_of((xx * ZN + z) * PIECE, PIECE), PIECE)
            src = ref.at[z, pl.ds(rx * PIECE, PIECE), :]
            copies.append(pltpu.make_async_copy(src, scratch.at[rows, :], sem.at[z, rx]))
    return copies


def plain_copies(sources, targets, sem):
    return [
        pltpu.make_async_copy(src, dst, sem.at[i]) for i, (src, dst) in enumerate(zip(sources, targets))
    ]


def begin(copies):
    for copy in copies:
        copy.start()


def finish(copies):
    for copy in copies:
        copy.wait()


def projection_kernel(ftags, *refs):
    nf = len(ftags)
    fr = refs[:nf]
    w_ref, g_s, lam_s, q_s, k_s, v_s, local_ref = refs[nf : nf + 7]
    send_refs = refs[nf + 7 : nf + 10]
    pair_ref, one_ref = refs[nf + 10 : nf + 12]
    a_s, w_s, fsem, wsem = refs[nf + 12 :]
    step = 256
    wc = weight_copies(w_ref, w_s, wsem)
    tiles = []
    for r in range(0, TOK, step):
        rows = pl.ds(r, step)
        parts = [ref.at[rows, :] for ref in fr]
        tiles.append(feature_copies(ftags, parts, a_s.at[rows, :], fsem.at[r // step]))
    begin(wc)
    for tile in tiles:
        begin(tile)
    finish(wc)
    for r in range(0, TOK, step):
        rows = pl.ds(r, step)
        finish(tiles[r // step])
        both = dot(a_s[rows, :], w_s[...]).astype(BF16)
        for i, held in enumerate((q_s, k_s, v_s)):
            held[rows, :] = both[:, i * COLS : (i + 1) * COLS]
    x = lax.axis_index("x")
    pair = lax.div(lax.axis_index("z"), 2)
    low = lax.rem(lax.axis_index("z"), 2)
    for h in range(HEADS_HERE):
        cols = pl.ds(h * HD, HD)
        q = q_s[:, cols].astype(F32)
        g = g_s[:, cols]
        states = []
        for b in range(FAR):
            at = h * LEVELS + NEAR + b
            states.append(dot_tn((lam_s[:, at : at + 1] * q).astype(BF16), g))
        local_ref[h] = dot_tn(k_s[:, cols], v_s[:, cols])
        one_ref[h] = jnp.where(low == 1, states[0], 0.0)
        for i, off in enumerate((1, 2, 3)):
            to = lax.rem(pair + (4 - off), 4)
            sibling = lax.div(pair, 2) == lax.div(to, 2)
            pair_ref[i, h] = jnp.where(to < pair, jnp.where(sibling, states[1], states[2]), 0.0)
            to = lax.rem(x + (XN - off), XN)
            sibling = lax.div(x, 2) == lax.div(to, 2)
            level = jnp.where(to < x, jnp.where(sibling, states[3], states[4]), 0.0)
            send_refs[i][h] = level.astype(BF16)


def near_kernel(h, *refs):
    ins, lam_ref, outs = refs[:4], refs[4], refs[5:9]
    held = refs[9:13]
    lam_s, sums = refs[13], refs[14:18]
    isem, osem = refs[18:]
    q_s, k_s, v_s, g_s = held
    cols = pl.ds(h * HD, HD)
    half = TOK // 2
    copies = {}
    for name, i, part in (
        ("k0", 1, 0),
        ("v0", 2, 0),
        ("q1", 0, 1),
        ("g1", 3, 1),
        ("k1", 1, 1),
        ("v1", 2, 1),
        ("q0", 0, 0),
        ("g0", 3, 0),
    ):
        rows = pl.ds(part * half, half)
        copies[name] = pltpu.make_async_copy(ins[i].at[rows, cols], held[i].at[rows, :], isem.at[i, part])
    lam_copy = pltpu.make_async_copy(lam_ref, lam_s, isem.at[4, 0])
    early_ones = [copies[name] for name in ("k0", "v0", "q1", "g1")]
    late_ones = [copies[name] for name in ("k1", "v1", "q0", "g0")]
    begin([*early_ones[:2], lam_copy, *early_ones[2:], *late_ones])
    tile = 128
    t_at = lax.broadcasted_iota(jnp.int32, (tile, tile), 0)
    s_at = lax.broadcasted_iota(jnp.int32, (tile, tile), 1)
    apart = jnp.bitwise_xor(t_at, s_at)
    causal = t_at >= s_at
    begun = [set(), set(), set(), set()]

    def add(which, start, value):
        for i in range(value.shape[0] // tile):
            at = start + i * tile
            rows = pl.ds(at, tile)
            piece = value[i * tile : (i + 1) * tile, :]
            if at in begun[which]:
                piece = sums[which][rows, :] + piece
            begun[which].add(at)
            sums[which][rows, :] = piece

    finish([*early_ones, lam_copy])
    for level in reversed(range(8, NEAR)):
        size = tile << (level - 8)
        for at in range(0, TOK, 2 * size):
            early, late = pl.ds(at, size), pl.ds(at + size, size)
            k, v = k_s[early, :], v_s[early, :]
            q, g = q_s[late, :], g_s[late, :]
            lam = lam_s[late, h * LEVELS + level : h * LEVELS + level + 1]
            state = dot_tn(k, v).astype(BF16)
            back = dot_tn((lam * q.astype(F32)).astype(BF16), g).astype(BF16)
            add(0, at + size, lam * dot(q, state))
            add(1, at + size, lam * dot_nt(g, state))
            add(2, at, dot_nt(v, back))
            add(3, at, dot(k, back))
        if level == NEAR - 1:
            finish(late_ones)
    oc = []
    for i in range(TOK // tile):
        rows = pl.ds(i * tile, tile)
        q, k, v, g = q_s[rows, :], k_s[rows, :], v_s[rows, :], g_s[rows, :]
        lam = lam_s[rows, pl.ds(h * LEVELS, LEVELS)]
        mix = jnp.broadcast_to(lam[:, 0:1], (tile, tile))
        for level in range(1, 8):
            mix = jnp.where(apart >= 1 << (level - 1), lam[:, level : level + 1], mix)
        mix = jnp.where(causal, mix, 0.0)
        probs = (mix * dot_nt(q, k)).astype(BF16)
        mixed = (mix * dot_nt(g, v)).astype(BF16)
        add(0, i * tile, dot(probs, v))
        add(1, i * tile, dot(mixed, k))
        add(2, i * tile, dot_tn(mixed, q))
        add(3, i * tile, dot_tn(probs, g))
        for which in range(4):
            src, to = sums[which].at[rows, :], outs[which].at[rows, :]
            oc.append(pltpu.make_async_copy(src, to, osem.at[which, i]))
            oc[-1].start()
    finish(oc)


def key_value_grad_kernel(ftags, *refs):
    nf = len(ftags)
    fr = refs[:nf]
    ins = refs[nf : nf + 6]
    back_ref, parts_ref = refs[nf + 6 : nf + 8]
    a_s, k_s, v_s, dk0, dk1, dv0, dv1, tot_s, grad_s, fsem, isem, osem = refs[nf + 8 :]
    ic = plain_copies(ins, [k_s, v_s, dk0, dk1, dv0, dv1], isem)
    fc = plain_copies(fr, [a_s.at[i] for i in range(nf)], fsem)
    begin(ic + fc)
    finish(ic)
    for h in range(HEADS_HERE):
        cols = pl.ds(h * HD, HD)
        back = back_ref[h].astype(BF16)
        tot_s[:, cols] = ((dk0, dk1)[h][...] + dot_nt(v_s[:, cols], back)).astype(BF16)
        tot_s[:, pl.ds(COLS + h * HD, HD)] = ((dv0, dv1)[h][...] + dot(k_s[:, cols], back)).astype(BF16)
    x = lax.axis_index("x")
    y = lax.axis_index("y")
    core = lax.axis_index("core")
    oc = []
    for i, (off, same) in enumerate(ftags):
        fc[i].wait()
        rows = pl.ds(i * COLS, COLS)
        grad_s[rows, :] = dot_tn(a_s[i], tot_s[...]).astype(BF16)
        rx = lax.rem(lax.rem(y + (off + YN), YN) + (XN - x), XN)
        first = (core if same else 1 - core) * (ZN // 2)
        for j in range(COLS // PIECE):
            at = pl.multiple_of(((first + j) * XN + rx) * PIECE, PIECE)
            src = grad_s.at[pl.ds(i * COLS + j * PIECE, PIECE), :]
            oc.append(pltpu.make_async_copy(src, parts_ref.at[pl.ds(at, PIECE), :], osem.at[i, j]))
            oc[-1].start()
    finish(oc)


def query_grad_kernel(ftags, *refs):
    nf = len(ftags)
    fr = refs[:nf]
    ins = refs[nf : nf + 7]
    state_ref, att_ref = refs[nf + 7 : nf + 9]
    outs = refs[nf + 9 : nf + 9 + XN]
    scratch = refs[nf + 9 + XN :]
    a_s, q_s, g_s, near0, near1, dq0, dq1, lam_s, att_s, tot_s, grad_s, fsem, isem, osem = scratch
    ic = plain_copies(ins, [q_s, g_s, near0, near1, dq0, dq1, lam_s], isem)
    fc = feature_copies(ftags, fr, a_s, fsem)
    begin(ic + fc)
    finish(ic)
    for h in range(HEADS_HERE):
        cols = pl.ds(h * HD, HD)
        q, g = q_s[:, cols], g_s[:, cols]
        out = (near0, near1)[h][...]
        total = (dq0, dq1)[h][...]
        for b in range(FAR):
            at = h * LEVELS + NEAR + b
            lam = lam_s[:, at : at + 1]
            state = state_ref[b, h]
            out = out + lam * dot(q, state)
            total = total + lam * dot_nt(g, state)
        att_s[:, cols] = out.astype(BF16)
        tot_s[:, cols] = total.astype(BF16)
    oc = [pltpu.make_async_copy(att_s, att_ref, osem.at[ZN])]
    begin(oc)
    finish(fc)
    x = lax.axis_index("x")
    part = WIDTH // XN
    for off in range(XN):
        xx = lax.rem(x + off, XN)
        for i in range(part // 256):
            cols = pl.ds(pl.multiple_of(xx * part + i * 256, 256), 256)
            rows = pl.ds(off * part + i * 256, 256)
            grad_s[rows, :] = dot_tn(a_s[:, cols], tot_s[...]).astype(BF16)
            to = outs[off].at[pl.ds(i * 256, 256), :]
            oc.append(pltpu.make_async_copy(grad_s.at[rows, :], to, osem.at[off * 2 + i]))
            oc[-1].start()
    finish(oc)


HBM = pl.BlockSpec(memory_space=pltpu.HBM)
VM = pl.BlockSpec(memory_space=pltpu.VMEM)


def struct(shape, dtype):
    return jax.ShapeDtypeStruct(shape, dtype)


def call(body, name, inputs, specs, outs, out_specs, scratch, flops, moved):
    return pl.pallas_call(
        body,
        name=name,
        in_specs=specs,
        out_specs=out_specs,
        out_shape=outs,
        scratch_shapes=scratch,
        compiler_params=pltpu.CompilerParams(vmem_limit_bytes=VMEM_LIMIT),
        cost_estimate=pl.CostEstimate(flops=flops, transcendentals=0, bytes_accessed=moved),
    )(*inputs)


def on_device(activations, w_query, w_key, w_value, level_table, table_rows, out_grad):
    x = lax.axis_index("x")
    z = lax.axis_index("z")
    pair = lax.shift_right_logical(z, 1)

    weights = jnp.concatenate([w_query, w_key, w_value], axis=1)
    along = [weights] + [shifted(weights, "x", -off) for off in (1, 2, 3)]
    weights = lax.all_gather(jnp.concatenate(along, axis=0), "z", axis=0)

    feats = features_of(activations)
    ftags = [(off, same) for off, same, _ in feats]
    fparts = [part for _, _, part in feats]
    nf = len(ftags)

    scale = 1.0 / math.sqrt(HD * TOK)
    table_size = level_table.shape[1]
    onehot = (table_rows[:, None] == jnp.arange(table_size, dtype=jnp.int32)[None, :]).astype(F32)
    flat = jnp.transpose(level_table, (1, 0, 2)).reshape(table_size, HEADS_HERE * LEVELS)
    lam = scale * jnp.dot(onehot, flat, precision=lax.Precision.HIGHEST)

    dma = pltpu.SemaphoreType.DMA
    wide = pltpu.VMEM((TOK, WIDTH), BF16)
    block = pltpu.VMEM((TOK, COLS), BF16)
    near_f32 = pltpu.VMEM((TOK, HD), F32)
    lam_held = pltpu.VMEM((TOK, HEADS_HERE * LEVELS), F32)
    state = (HEADS_HERE, HD, HD)

    queries, keys, values, local, s1, s2, s3, by_pair, by_one = call(
        functools.partial(projection_kernel, ftags),
        "projections",
        [*fparts, weights, out_grad, lam],
        [HBM] * (nf + 1) + [VM] * 2,
        [struct((TOK, COLS), BF16)] * 3
        + [struct(state, F32)]
        + [struct(state, BF16)] * 3
        + [struct((3, *state), F32), struct(state, F32)],
        [VM] * 9,
        [
            wide,
            pltpu.VMEM((WIDTH, 3 * COLS), BF16),
            dma((TOK // 256, nf)),
            dma((ZN, XN)),
        ],
        1 << 20,
        1 << 10,
    )

    after_one = [shifted(part, "x", -off) for off, part in zip((1, 2, 3), (s1, s2, s3))]
    pending = sum(part.astype(F32) for part in after_one)
    after_two = [
        shifted((pending + by_pair[i]).astype(BF16), "z", -2 * off) for i, off in enumerate((1, 2, 3))
    ]

    def near_of(h, gate):
        first, *_ = lax.optimization_barrier((queries, *gate))
        return call(
            functools.partial(near_kernel, h),
            "near",
            [first, keys, values, out_grad, lam],
            [HBM] * 5,
            [struct((TOK, HD), F32)] * 4,
            [HBM] * 4,
            [pltpu.VMEM((TOK, HD), BF16)] * 4
            + [pltpu.VMEM((TOK, HEADS_HERE * LEVELS), F32)]
            + [pltpu.VMEM((TOK, HD), F32)] * 4
            + [dma((5, 2)), dma((4, TOK // 128))],
            2 << 30,
            8 << 20,
        )

    near = [near_of(0, after_one)]
    *after_two, _ = lax.optimization_barrier((*after_two, near[0][0]))
    pending = pending + sum(part.astype(F32) for part in after_two)
    pending = pending + swapped((pending + by_one).astype(BF16), "z", 1).astype(F32)

    none = jnp.zeros(state, BF16)

    def among_four(value, index, axis, stride):
        sent = value.astype(BF16)
        got = {off: shifted(sent, axis, off * stride) for off in (1, 2, 3)}
        full = {off: part.astype(F32) for off, part in got.items()}
        first = jnp.where((index & 1) != 0, got[1], none)
        other = full[2] + jnp.where(index == 2, full[1], full[3])
        second = jnp.where(index >= 2, other.astype(BF16), none)
        return first, second, value + full[1] + full[2] + full[3]

    local, *_ = lax.optimization_barrier((local, *after_one))
    sibling = swapped(local, "z", 1)
    state0 = jnp.where((z & 1) != 0, sibling, 0.0).astype(BF16)
    total = local + sibling
    near.append(near_of(1, [*after_two, sibling]))
    near_out, query_near, key_near, value_near = (list(parts) for parts in zip(*near))

    total, pending = lax.optimization_barrier((total, pending))
    state1, state2, total = among_four(total, pair, "z", 2)
    state3, state4, total = among_four(total, x, "x", 1)
    states = jnp.stack([state0, state1, state2, state3, state4])

    (parts,) = call(
        functools.partial(key_value_grad_kernel, ftags),
        "key_value_grad",
        [*fparts, keys, values, *key_near, *value_near, pending],
        [HBM] * (nf + 6) + [VM],
        [struct((WIDTH, 2 * COLS), BF16)],
        [HBM],
        [
            pltpu.VMEM((nf, TOK, COLS), BF16),
            block,
            block,
            *[near_f32] * 4,
            pltpu.VMEM((TOK, 2 * COLS), BF16),
            pltpu.VMEM((WIDTH, 2 * COLS), BF16),
            dma((nf,)),
            dma((6,)),
            dma((nf, COLS // PIECE)),
        ],
        1 << 20,
        1 << 10,
    )
    kv_sum = lax.psum_scatter(parts, "z", scatter_dimension=0, tiled=True)

    query_near[0], _ = lax.optimization_barrier((query_near[0], parts))
    attended, *sums = call(
        functools.partial(query_grad_kernel, ftags),
        "query_grad",
        [*fparts, queries, out_grad, *near_out, *query_near, lam, states],
        [HBM] * (nf + 7) + [VM],
        [struct((TOK, COLS), BF16)] + [struct((WIDTH // XN, COLS), BF16)] * XN,
        [HBM] * (XN + 1),
        [
            wide,
            block,
            block,
            *[near_f32] * 4,
            lam_held,
            block,
            block,
            pltpu.VMEM((WIDTH, COLS), BF16),
            dma((nf,)),
            dma((7,)),
            dma((ZN + 1,)),
        ],
        8 << 30,
        8 << 20,
    )
    mine = sums[0].astype(F32)
    for off in (1, 2, 3):
        mine = mine + shifted(sums[off], "x", off).astype(F32)
    gathered = lax.all_to_all(mine.astype(BF16).reshape(ZN, PIECE, COLS), "z", 0, 0, tiled=True)
    grad_query = jnp.sum(gathered.astype(F32), axis=0)

    kv_sum = kv_sum.reshape(XN, PIECE, 2 * COLS)
    grad_kv = kv_sum[0].astype(F32)
    for off in (1, 2, 3):
        grad_kv = grad_kv + shifted(kv_sum[off], "x", off).astype(F32)
    return attended, grad_query, grad_kv[:, :COLS], grad_kv[:, COLS:]


def solution(mesh):
    finer = Mesh(mesh.devices.reshape(XN, ZN, YN, 2), ("x", "z", "y", "core"))
    rows, cols = ("x", "z"), ("y", "core")
    return jax.shard_map(
        on_device,
        mesh=finer,
        in_specs=(
            P(rows, cols),
            P(rows, cols),
            P(rows, cols),
            P(rows, cols),
            P(cols, None, None),
            P(rows),
            P(rows, cols),
        ),
        out_specs=(P(rows, cols), P(rows, cols), P(rows, cols), P(rows, cols)),
        check_vma=False,
    )
```

```python
import functools
import math

import jax
import jax.numpy as jnp
from jax import lax
from jax.experimental import pallas as pl
from jax.experimental.pallas import tpu as pltpu
from jax.sharding import Mesh
from jax.sharding import PartitionSpec as P

F32 = jnp.float32
BF16 = jnp.bfloat16
VMEM_LIMIT = 56 * 1024 * 1024

TOK = 1024
WIDTH = 2048
COLS = 256
HD = 128
HEADS_HERE = 2
LEVELS = 16
NEAR = 11
FAR = 5
XN, ZN, YN = 4, 8, 4
PIECE = WIDTH // (XN * ZN)


def shifted(value, axis, offset):
    count = lax.axis_size(axis)
    return lax.ppermute(value, axis, [(i, (i + offset) % count) for i in range(count)])


def swapped(value, axis, bit):
    count = lax.axis_size(axis)
    return lax.ppermute(value, axis, [(i, i ^ bit) for i in range(count)])


def features_of(block):
    mine = [(0, block)] + [(off, shifted(block, "y", -off)) for off in (1, -1, 2)]
    found = [(off, True, part) for off, part in mine]
    found += [(off, False, shifted(part, "core", 1)) for off, part in mine]
    return found


def dot(a, b):
    return lax.dot_general(a, b, (((1,), (0,)), ((), ())), preferred_element_type=F32)


def dot_nt(a, b):
    return lax.dot_general(a, b, (((1,), (1,)), ((), ())), preferred_element_type=F32)


def dot_tn(a, b):
    return lax.dot_general(a, b, (((0,), (0,)), ((), ())), preferred_element_type=F32)


def feature_copies(tags, refs, scratch, sem):
    y = lax.axis_index("y")
    core = lax.axis_index("core")
    copies = []
    for i, ((off, same), ref) in enumerate(zip(tags, refs)):
        block = lax.rem(y + (off + YN), YN) * 2 + (core if same else 1 - core)
        cols = pl.ds(pl.multiple_of(block * COLS, COLS), COLS)
        copies.append(pltpu.make_async_copy(ref, scratch.at[:, cols], sem.at[i]))
    return copies


def weight_copies(ref, scratch, sem):
    x = lax.axis_index("x")
    copies = []
    for z in range(ZN):
        for rx in range(XN):
            xx = lax.rem(x + rx, XN)
            rows = pl.ds(pl.multiple_of((xx * ZN + z) * PIECE, PIECE), PIECE)
            src = ref.at[z, pl.ds(rx * PIECE, PIECE), :]
            copies.append(pltpu.make_async_copy(src, scratch.at[rows, :], sem.at[z, rx]))
    return copies


def begin(copies):
    for copy in copies:
        copy.start()


def finish(copies):
    for copy in copies:
        copy.wait()


def projection_kernel(ftags, *refs):
    nf = len(ftags)
    fr = refs[:nf]
    w_ref, g_s, lam_s, q_s, k_s, v_s, local_ref = refs[nf : nf + 7]
    send_refs = refs[nf + 7 : nf + 10]
    pair_ref, one_ref = refs[nf + 10 : nf + 12]
    a_s, w_s, fsem, wsem = refs[nf + 12 :]
    fc = feature_copies(ftags, fr, a_s, fsem)
    wc = weight_copies(w_ref, w_s, wsem)
    begin(wc + fc)
    finish(wc + fc)
    step = 256
    for r in range(0, TOK, step):
        rows = pl.ds(r, step)
        both = dot(a_s[rows, :], w_s[...]).astype(BF16)
        for i, held in enumerate((q_s, k_s, v_s)):
            held[rows, :] = both[:, i * COLS : (i + 1) * COLS]
    x = lax.axis_index("x")
    pair = lax.div(lax.axis_index("z"), 2)
    low = lax.rem(lax.axis_index("z"), 2)
    for h in range(HEADS_HERE):
        cols = pl.ds(h * HD, HD)
        q = q_s[:, cols].astype(F32)
        g = g_s[:, cols]
        states = []
        for b in range(FAR):
            at = h * LEVELS + NEAR + b
            states.append(dot_tn((lam_s[:, at : at + 1] * q).astype(BF16), g))
        local_ref[h] = dot_tn(k_s[:, cols], v_s[:, cols])
        one_ref[h] = jnp.where(low == 1, states[0], 0.0)
        for i, off in enumerate((1, 2, 3)):
            to = lax.rem(pair + (4 - off), 4)
            sibling = lax.div(pair, 2) == lax.div(to, 2)
            pair_ref[i, h] = jnp.where(to < pair, jnp.where(sibling, states[1], states[2]), 0.0)
            to = lax.rem(x + (XN - off), XN)
            sibling = lax.div(x, 2) == lax.div(to, 2)
            level = jnp.where(to < x, jnp.where(sibling, states[3], states[4]), 0.0)
            send_refs[i][h] = level.astype(BF16)


def near_kernel(h, *refs):
    ins, lam_ref, outs = refs[:4], refs[4], refs[5:9]
    held = refs[9:13]
    lam_s, sums = refs[13], refs[14:18]
    isem, osem = refs[18:]
    q_s, k_s, v_s, g_s = held
    cols = pl.ds(h * HD, HD)
    half = TOK // 2
    copies = {}
    for name, i, part in (
        ("k0", 1, 0),
        ("v0", 2, 0),
        ("q1", 0, 1),
        ("g1", 3, 1),
        ("k1", 1, 1),
        ("v1", 2, 1),
        ("q0", 0, 0),
        ("g0", 3, 0),
    ):
        rows = pl.ds(part * half, half)
        copies[name] = pltpu.make_async_copy(ins[i].at[rows, cols], held[i].at[rows, :], isem.at[i, part])
    lam_copy = pltpu.make_async_copy(lam_ref, lam_s, isem.at[4, 0])
    early_ones = [copies[name] for name in ("k0", "v0", "q1", "g1")]
    late_ones = [copies[name] for name in ("k1", "v1", "q0", "g0")]
    begin([*early_ones[:2], lam_copy, *early_ones[2:], *late_ones])
    tile = 128
    t_at = lax.broadcasted_iota(jnp.int32, (tile, tile), 0)
    s_at = lax.broadcasted_iota(jnp.int32, (tile, tile), 1)
    apart = jnp.bitwise_xor(t_at, s_at)
    causal = t_at >= s_at
    begun = [set(), set(), set(), set()]

    def add(which, start, value):
        for i in range(value.shape[0] // tile):
            at = start + i * tile
            rows = pl.ds(at, tile)
            piece = value[i * tile : (i + 1) * tile, :]
            if at in begun[which]:
                piece = sums[which][rows, :] + piece
            begun[which].add(at)
            sums[which][rows, :] = piece

    finish([*early_ones, lam_copy])
    for level in reversed(range(8, NEAR)):
        size = tile << (level - 8)
        for at in range(0, TOK, 2 * size):
            early, late = pl.ds(at, size), pl.ds(at + size, size)
            k, v = k_s[early, :], v_s[early, :]
            q, g = q_s[late, :], g_s[late, :]
            lam = lam_s[late, h * LEVELS + level : h * LEVELS + level + 1]
            state = dot_tn(k, v).astype(BF16)
            back = dot_tn((lam * q.astype(F32)).astype(BF16), g).astype(BF16)
            add(0, at + size, lam * dot(q, state))
            add(1, at + size, lam * dot_nt(g, state))
            add(2, at, dot_nt(v, back))
            add(3, at, dot(k, back))
        if level == NEAR - 1:
            finish(late_ones)
    oc = []
    for i in range(TOK // tile):
        rows = pl.ds(i * tile, tile)
        q, k, v, g = q_s[rows, :], k_s[rows, :], v_s[rows, :], g_s[rows, :]
        lam = lam_s[rows, pl.ds(h * LEVELS, LEVELS)]
        mix = jnp.broadcast_to(lam[:, 0:1], (tile, tile))
        for level in range(1, 8):
            mix = jnp.where(apart >= 1 << (level - 1), lam[:, level : level + 1], mix)
        mix = jnp.where(causal, mix, 0.0)
        probs = (mix * dot_nt(q, k)).astype(BF16)
        mixed = (mix * dot_nt(g, v)).astype(BF16)
        add(0, i * tile, dot(probs, v))
        add(1, i * tile, dot(mixed, k))
        add(2, i * tile, dot_tn(mixed, q))
        add(3, i * tile, dot_tn(probs, g))
        for which in range(4):
            src, to = sums[which].at[rows, :], outs[which].at[rows, :]
            oc.append(pltpu.make_async_copy(src, to, osem.at[which, i]))
            oc[-1].start()
    finish(oc)


def key_value_grad_kernel(ftags, *refs):
    nf = len(ftags)
    fr = refs[:nf]
    k_s, v_s, dk0, dk1, dv0, dv1, back_ref, parts_ref = refs[nf : nf + 8]
    a_s, tot_s, grad_s, fsem, osem = refs[nf + 8 :]
    fc = feature_copies(ftags, fr, a_s, fsem)
    begin(fc)
    for h in range(HEADS_HERE):
        cols = pl.ds(h * HD, HD)
        back = back_ref[h].astype(BF16)
        tot_s[:, cols] = ((dk0, dk1)[h][...] + dot_nt(v_s[:, cols], back)).astype(BF16)
        tot_s[:, pl.ds(COLS + h * HD, HD)] = ((dv0, dv1)[h][...] + dot(k_s[:, cols], back)).astype(BF16)
    finish(fc)
    x = lax.axis_index("x")
    oc = []
    for r in range(0, WIDTH, 256):
        grad_s[pl.ds(r, 256), :] = dot_tn(a_s[:, pl.ds(r, 256)], tot_s[...]).astype(BF16)
        xx = r // (ZN * PIECE)
        rx = lax.rem(xx + (XN - x), XN)
        for i in range(256 // PIECE):
            z = r % (ZN * PIECE) // PIECE + i
            to = pl.ds(pl.multiple_of((z * XN + rx) * PIECE, PIECE), PIECE)
            src = grad_s.at[pl.ds(r + i * PIECE, PIECE), :]
            oc.append(pltpu.make_async_copy(src, parts_ref.at[to, :], osem.at[r // PIECE + i]))
            oc[-1].start()
    finish(oc)


def query_grad_kernel(ftags, *refs):
    nf = len(ftags)
    fr = refs[:nf]
    q_s, g_s, near0, near1, dq0, dq1, lam_s, state_ref, att_s = refs[nf : nf + 9]
    outs = refs[nf + 9 : nf + 9 + XN]
    a_s, tot_s, grad_s, fsem, osem = refs[nf + 9 + XN :]
    fc = feature_copies(ftags, fr, a_s, fsem)
    begin(fc)
    for h in range(HEADS_HERE):
        cols = pl.ds(h * HD, HD)
        q, g = q_s[:, cols], g_s[:, cols]
        out = (near0, near1)[h][...]
        total = (dq0, dq1)[h][...]
        for b in range(FAR):
            at = h * LEVELS + NEAR + b
            lam = lam_s[:, at : at + 1]
            state = state_ref[b, h]
            out = out + lam * dot(q, state)
            total = total + lam * dot_nt(g, state)
        att_s[:, cols] = out.astype(BF16)
        tot_s[:, cols] = total.astype(BF16)
    finish(fc)
    oc = []
    x = lax.axis_index("x")
    part = WIDTH // XN
    for off in range(XN):
        xx = lax.rem(x + off, XN)
        for i in range(part // 256):
            cols = pl.ds(pl.multiple_of(xx * part + i * 256, 256), 256)
            rows = pl.ds(off * part + i * 256, 256)
            grad_s[rows, :] = dot_tn(a_s[:, cols], tot_s[...]).astype(BF16)
            to = outs[off].at[pl.ds(i * 256, 256), :]
            oc.append(pltpu.make_async_copy(grad_s.at[rows, :], to, osem.at[off * 2 + i]))
            oc[-1].start()
    finish(oc)


HBM = pl.BlockSpec(memory_space=pltpu.HBM)
VM = pl.BlockSpec(memory_space=pltpu.VMEM)


def struct(shape, dtype):
    return jax.ShapeDtypeStruct(shape, dtype)


def call(body, name, inputs, specs, outs, out_specs, scratch, flops, moved):
    return pl.pallas_call(
        body,
        name=name,
        in_specs=specs,
        out_specs=out_specs,
        out_shape=outs,
        scratch_shapes=scratch,
        compiler_params=pltpu.CompilerParams(vmem_limit_bytes=VMEM_LIMIT),
        cost_estimate=pl.CostEstimate(flops=flops, transcendentals=0, bytes_accessed=moved),
    )(*inputs)


def on_device(activations, w_query, w_key, w_value, level_table, table_rows, out_grad):
    x = lax.axis_index("x")
    z = lax.axis_index("z")
    pair = lax.shift_right_logical(z, 1)

    low = jnp.array(-jnp.inf, BF16)
    weights = [
        lax.pad(w, low, ((0, 0, 0), (i * COLS, (2 - i) * COLS, 0)))
        for i, w in enumerate((w_query, w_key, w_value))
    ]
    weights = jnp.maximum(jnp.maximum(weights[0], weights[1]), weights[2])
    along = [weights] + [shifted(weights, "x", -off) for off in (1, 2, 3)]
    weights = lax.all_gather(jnp.concatenate(along, axis=0), "z", axis=0)

    feats = features_of(activations)
    ftags = [(off, same) for off, same, _ in feats]
    fparts = [part for _, _, part in feats]
    nf = len(ftags)

    scale = 1.0 / math.sqrt(HD * TOK)
    table_size = level_table.shape[1]
    onehot = (table_rows[:, None] == jnp.arange(table_size, dtype=jnp.int32)[None, :]).astype(F32)
    flat = jnp.transpose(level_table, (1, 0, 2)).reshape(table_size, HEADS_HERE * LEVELS)
    lam = scale * jnp.dot(onehot, flat, precision=lax.Precision.HIGHEST)

    dma = pltpu.SemaphoreType.DMA
    wide = pltpu.VMEM((TOK, WIDTH), BF16)
    block = pltpu.VMEM((TOK, COLS), BF16)
    state = (HEADS_HERE, HD, HD)

    queries, keys, values, local, s1, s2, s3, by_pair, by_one = call(
        functools.partial(projection_kernel, ftags),
        "projections",
        [*fparts, weights, out_grad, lam],
        [HBM] * (nf + 1) + [VM] * 2,
        [struct((TOK, COLS), BF16)] * 3
        + [struct(state, F32)]
        + [struct(state, BF16)] * 3
        + [struct((3, *state), F32), struct(state, F32)],
        [VM] * 9,
        [
            wide,
            pltpu.VMEM((WIDTH, 3 * COLS), BF16),
            dma((nf,)),
            dma((ZN, XN)),
        ],
        1 << 20,
        1 << 10,
    )

    def near_of(h, gate):
        first, *_ = lax.optimization_barrier((queries, *gate))
        return call(
            functools.partial(near_kernel, h),
            "near",
            [first, keys, values, out_grad, lam],
            [HBM] * 5,
            [struct((TOK, HD), F32)] * 4,
            [HBM] * 4,
            [pltpu.VMEM((TOK, HD), BF16)] * 4
            + [pltpu.VMEM((TOK, HEADS_HERE * LEVELS), F32)]
            + [pltpu.VMEM((TOK, HD), F32)] * 4
            + [dma((5, 2)), dma((4, TOK // 128))],
            2 << 30,
            8 << 20,
        )

    after_one = [shifted(part, "x", -off) for off, part in zip((1, 2, 3), (s1, s2, s3))]
    near = [near_of(0, [])]
    *after_one, _ = lax.optimization_barrier((*after_one, near[0][0]))
    pending = sum(part.astype(F32) for part in after_one)
    after_two = [
        shifted((pending + by_pair[i]).astype(BF16), "z", -2 * off) for i, off in enumerate((1, 2, 3))
    ]
    near.append(near_of(1, after_one))
    *after_two, _ = lax.optimization_barrier((*after_two, near[1][0]))
    pending = pending + sum(part.astype(F32) for part in after_two)
    pending = pending + swapped((pending + by_one).astype(BF16), "z", 1).astype(F32)

    none = jnp.zeros(state, BF16)

    def among_four(value, index, axis, stride):
        sent = value.astype(BF16)
        got = {off: shifted(sent, axis, off * stride) for off in (1, 2, 3)}
        full = {off: part.astype(F32) for off, part in got.items()}
        first = jnp.where((index & 1) != 0, got[1], none)
        other = full[2] + jnp.where(index == 2, full[1], full[3])
        second = jnp.where(index >= 2, other.astype(BF16), none)
        return first, second, value + full[1] + full[2] + full[3]

    local, *_ = lax.optimization_barrier((local, *after_one))
    sibling = swapped(local, "z", 1)
    state0 = jnp.where((z & 1) != 0, sibling, 0.0).astype(BF16)
    total = local + sibling
    near_out, query_near, key_near, value_near = (list(parts) for parts in zip(*near))

    total, *_ = lax.optimization_barrier((total, *after_two))
    state1, state2, total = among_four(total, pair, "z", 2)
    (parts,) = call(
        functools.partial(key_value_grad_kernel, ftags),
        "key_value_grad",
        [*fparts, keys, values, *key_near, *value_near, pending],
        [HBM] * nf + [VM] * 7,
        [struct((WIDTH, 2 * COLS), BF16)],
        [HBM],
        [
            wide,
            pltpu.VMEM((TOK, 2 * COLS), BF16),
            pltpu.VMEM((WIDTH, 2 * COLS), BF16),
            dma((nf,)),
            dma((WIDTH // PIECE,)),
        ],
        8 << 30,
        8 << 20,
    )
    parts, total = lax.optimization_barrier((parts, total))
    state3, state4, total = among_four(total, x, "x", 1)
    states = jnp.stack([state0, state1, state2, state3, state4])
    kv_sum = lax.psum_scatter(parts, "z", scatter_dimension=0, tiled=True)

    query_near[0], _ = lax.optimization_barrier((query_near[0], parts))
    attended, *sums = call(
        functools.partial(query_grad_kernel, ftags),
        "query_grad",
        [*fparts, queries, out_grad, *near_out, *query_near, lam, states],
        [HBM] * nf + [VM] * 8,
        [struct((TOK, COLS), BF16)] + [struct((WIDTH // XN, COLS), BF16)] * XN,
        [VM] + [HBM] * XN,
        [
            wide,
            block,
            pltpu.VMEM((WIDTH, COLS), BF16),
            dma((nf,)),
            dma((ZN,)),
        ],
        8 << 30,
        8 << 20,
    )
    mine = sums[0].astype(F32)
    for off in (1, 2, 3):
        mine = mine + shifted(sums[off], "x", off).astype(F32)
    gathered = lax.all_to_all(mine.astype(BF16).reshape(ZN, PIECE, COLS), "z", 0, 0, tiled=True)
    grad_query = jnp.sum(gathered.astype(F32), axis=0)

    kv_sum = kv_sum.reshape(XN, PIECE, 2 * COLS)
    grad_kv = kv_sum[0].astype(F32)
    for off in (1, 2, 3):
        grad_kv = grad_kv + shifted(kv_sum[off], "x", off).astype(F32)
    return attended, grad_query, grad_kv[:, :COLS], grad_kv[:, COLS:]


def solution(mesh):
    finer = Mesh(mesh.devices.reshape(XN, ZN, YN, 2), ("x", "z", "y", "core"))
    rows, cols = ("x", "z"), ("y", "core")
    return jax.shard_map(
        on_device,
        mesh=finer,
        in_specs=(
            P(rows, cols),
            P(rows, cols),
            P(rows, cols),
            P(rows, cols),
            P(cols, None, None),
            P(rows),
            P(rows, cols),
        ),
        out_specs=(P(rows, cols), P(rows, cols), P(rows, cols), P(rows, cols)),
        check_vma=False,
    )
```

```python
import functools
import math

import jax
import jax.numpy as jnp
from jax import lax
from jax.experimental import pallas as pl
from jax.experimental.pallas import tpu as pltpu
from jax.sharding import Mesh
from jax.sharding import PartitionSpec as P

F32 = jnp.float32
BF16 = jnp.bfloat16
VMEM_LIMIT = 56 * 1024 * 1024

TOK = 1024
WIDTH = 2048
COLS = 256
HD = 128
HEADS_HERE = 2
LEVELS = 16
NEAR = 11
FAR = 5
XN, ZN, YN = 4, 8, 4
PIECE = WIDTH // (XN * ZN)


def shifted(value, axis, offset):
    count = lax.axis_size(axis)
    return lax.ppermute(value, axis, [(i, (i + offset) % count) for i in range(count)])


def swapped(value, axis, bit):
    count = lax.axis_size(axis)
    return lax.ppermute(value, axis, [(i, i ^ bit) for i in range(count)])


def features_of(block):
    mine = [(0, block)] + [(off, shifted(block, "y", -off)) for off in (1, -1, 2)]
    found = [(off, True, part) for off, part in mine]
    found += [(off, False, shifted(part, "core", 1)) for off, part in mine]
    return found


def dot(a, b):
    return lax.dot_general(a, b, (((1,), (0,)), ((), ())), preferred_element_type=F32)


def dot_nt(a, b):
    return lax.dot_general(a, b, (((1,), (1,)), ((), ())), preferred_element_type=F32)


def dot_tn(a, b):
    return lax.dot_general(a, b, (((0,), (0,)), ((), ())), preferred_element_type=F32)


def feature_copies(tags, refs, scratch, sem):
    y = lax.axis_index("y")
    core = lax.axis_index("core")
    copies = []
    for i, ((off, same), ref) in enumerate(zip(tags, refs)):
        block = lax.rem(y + (off + YN), YN) * 2 + (core if same else 1 - core)
        cols = pl.ds(pl.multiple_of(block * COLS, COLS), COLS)
        copies.append(pltpu.make_async_copy(ref, scratch.at[:, cols], sem.at[i]))
    return copies


def weight_copies(ref, scratch, sem):
    x = lax.axis_index("x")
    copies = []
    for z in range(ZN):
        for rx in range(XN):
            xx = lax.rem(x + rx, XN)
            rows = pl.ds(pl.multiple_of((xx * ZN + z) * PIECE, PIECE), PIECE)
            src = ref.at[z, pl.ds(rx * PIECE, PIECE), :]
            copies.append(pltpu.make_async_copy(src, scratch.at[rows, :], sem.at[z, rx]))
    return copies


def begin(copies):
    for copy in copies:
        copy.start()


def finish(copies):
    for copy in copies:
        copy.wait()


def projection_kernel(ftags, *refs):
    nf = len(ftags)
    fr = refs[:nf]
    w_ref, g_s, lam_s, q_s, k_s, v_s, local_ref = refs[nf : nf + 7]
    send_refs = refs[nf + 7 : nf + 10]
    pair_ref, one_ref = refs[nf + 10 : nf + 12]
    a_s, w_s, fsem, wsem = refs[nf + 12 :]
    fc = feature_copies(ftags, fr, a_s, fsem)
    wc = weight_copies(w_ref, w_s, wsem)
    begin(wc + fc)
    finish(wc + fc)
    step = 256
    for r in range(0, TOK, step):
        rows = pl.ds(r, step)
        both = dot(a_s[rows, :], w_s[...]).astype(BF16)
        for i, held in enumerate((q_s, k_s, v_s)):
            held[rows, :] = both[:, i * COLS : (i + 1) * COLS]
    x = lax.axis_index("x")
    pair = lax.div(lax.axis_index("z"), 2)
    low = lax.rem(lax.axis_index("z"), 2)
    for h in range(HEADS_HERE):
        cols = pl.ds(h * HD, HD)
        q = q_s[:, cols].astype(F32)
        g = g_s[:, cols]
        states = []
        for b in range(FAR):
            at = h * LEVELS + NEAR + b
            states.append(dot_tn((lam_s[:, at : at + 1] * q).astype(BF16), g))
        local_ref[h] = dot_tn(k_s[:, cols], v_s[:, cols])
        one_ref[h] = jnp.where(low == 1, states[0], 0.0)
        for i, off in enumerate((1, 2, 3)):
            to = lax.rem(pair + (4 - off), 4)
            sibling = lax.div(pair, 2) == lax.div(to, 2)
            pair_ref[i, h] = jnp.where(to < pair, jnp.where(sibling, states[1], states[2]), 0.0)
            to = lax.rem(x + (XN - off), XN)
            sibling = lax.div(x, 2) == lax.div(to, 2)
            level = jnp.where(to < x, jnp.where(sibling, states[3], states[4]), 0.0)
            send_refs[i][h] = level.astype(BF16)


def near_kernel(h, *refs):
    ins, lam_ref, outs = refs[:4], refs[4], refs[5:9]
    held = refs[9:13]
    lam_s, sums = refs[13], refs[14:18]
    isem, osem = refs[18:]
    q_s, k_s, v_s, g_s = held
    cols = pl.ds(h * HD, HD)
    half = TOK // 2
    copies = {}
    for name, i, part in (
        ("k0", 1, 0),
        ("v0", 2, 0),
        ("q1", 0, 1),
        ("g1", 3, 1),
        ("k1", 1, 1),
        ("v1", 2, 1),
        ("q0", 0, 0),
        ("g0", 3, 0),
    ):
        rows = pl.ds(part * half, half)
        copies[name] = pltpu.make_async_copy(ins[i].at[rows, cols], held[i].at[rows, :], isem.at[i, part])
    lam_copy = pltpu.make_async_copy(lam_ref, lam_s, isem.at[4, 0])
    early_ones = [copies[name] for name in ("k0", "v0", "q1", "g1")]
    late_ones = [copies[name] for name in ("k1", "v1", "q0", "g0")]
    begin([*early_ones[:2], lam_copy, *early_ones[2:], *late_ones])
    tile = 128
    t_at = lax.broadcasted_iota(jnp.int32, (tile, tile), 0)
    s_at = lax.broadcasted_iota(jnp.int32, (tile, tile), 1)
    apart = jnp.bitwise_xor(t_at, s_at)
    causal = t_at >= s_at
    begun = [set(), set(), set(), set()]

    def add(which, start, value):
        for i in range(value.shape[0] // tile):
            at = start + i * tile
            rows = pl.ds(at, tile)
            piece = value[i * tile : (i + 1) * tile, :]
            if at in begun[which]:
                piece = sums[which][rows, :] + piece
            begun[which].add(at)
            sums[which][rows, :] = piece

    finish([*early_ones, lam_copy])
    for level in reversed(range(8, NEAR)):
        size = tile << (level - 8)
        for at in range(0, TOK, 2 * size):
            early, late = pl.ds(at, size), pl.ds(at + size, size)
            k, v = k_s[early, :], v_s[early, :]
            q, g = q_s[late, :], g_s[late, :]
            lam = lam_s[late, h * LEVELS + level : h * LEVELS + level + 1]
            state = dot_tn(k, v).astype(BF16)
            back = dot_tn((lam * q.astype(F32)).astype(BF16), g).astype(BF16)
            add(0, at + size, lam * dot(q, state))
            add(1, at + size, lam * dot_nt(g, state))
            add(2, at, dot_nt(v, back))
            add(3, at, dot(k, back))
        if level == NEAR - 1:
            finish(late_ones)
    oc = []
    for i in range(TOK // tile):
        rows = pl.ds(i * tile, tile)
        q, k, v, g = q_s[rows, :], k_s[rows, :], v_s[rows, :], g_s[rows, :]
        lam = lam_s[rows, pl.ds(h * LEVELS, LEVELS)]
        mix = jnp.broadcast_to(lam[:, 0:1], (tile, tile))
        for level in range(1, 8):
            mix = jnp.where(apart >= 1 << (level - 1), lam[:, level : level + 1], mix)
        mix = jnp.where(causal, mix, 0.0)
        probs = (mix * dot_nt(q, k)).astype(BF16)
        mixed = (mix * dot_nt(g, v)).astype(BF16)
        add(0, i * tile, dot(probs, v))
        add(1, i * tile, dot(mixed, k))
        add(2, i * tile, dot_tn(mixed, q))
        add(3, i * tile, dot_tn(probs, g))
        for which in range(4):
            src, to = sums[which].at[rows, :], outs[which].at[rows, :]
            oc.append(pltpu.make_async_copy(src, to, osem.at[which, i]))
            oc[-1].start()
    finish(oc)


def key_value_grad_kernel(ftags, *refs):
    nf = len(ftags)
    fr = refs[:nf]
    k_s, v_s, dk0, dk1, dv0, dv1, back_ref, parts_ref = refs[nf : nf + 8]
    a_s, tot_s, grad_s, fsem, osem = refs[nf + 8 :]
    fc = feature_copies(ftags, fr, a_s, fsem)
    begin(fc)
    for h in range(HEADS_HERE):
        cols = pl.ds(h * HD, HD)
        back = back_ref[h].astype(BF16)
        tot_s[:, cols] = ((dk0, dk1)[h][...] + dot_nt(v_s[:, cols], back)).astype(BF16)
        tot_s[:, pl.ds(COLS + h * HD, HD)] = ((dv0, dv1)[h][...] + dot(k_s[:, cols], back)).astype(BF16)
    finish(fc)
    x = lax.axis_index("x")
    oc = []
    for r in range(0, WIDTH, 256):
        grad_s[pl.ds(r, 256), :] = dot_tn(a_s[:, pl.ds(r, 256)], tot_s[...]).astype(BF16)
        xx = r // (ZN * PIECE)
        rx = lax.rem(xx + (XN - x), XN)
        for i in range(256 // PIECE):
            z = r % (ZN * PIECE) // PIECE + i
            to = pl.ds(pl.multiple_of((z * XN + rx) * PIECE, PIECE), PIECE)
            src = grad_s.at[pl.ds(r + i * PIECE, PIECE), :]
            oc.append(pltpu.make_async_copy(src, parts_ref.at[to, :], osem.at[r // PIECE + i]))
            oc[-1].start()
    finish(oc)


def query_grad_kernel(ftags, *refs):
    nf = len(ftags)
    fr = refs[:nf]
    q_s, g_s, near0, near1, dq0, dq1, lam_s = refs[nf : nf + 7]
    state_refs = refs[nf + 7 : nf + 7 + FAR]
    att_s, *outs = refs[nf + 7 + FAR : nf + 8 + FAR + XN]
    a_s, tot_s, grad_s, fsem, osem = refs[nf + 8 + FAR + XN :]
    fc = feature_copies(ftags, fr, a_s, fsem)
    begin(fc)
    for h in range(HEADS_HERE):
        cols = pl.ds(h * HD, HD)
        q, g = q_s[:, cols], g_s[:, cols]
        out = (near0, near1)[h][...]
        total = (dq0, dq1)[h][...]
        for b in range(FAR):
            at = h * LEVELS + NEAR + b
            lam = lam_s[:, at : at + 1]
            state = state_refs[b][h]
            out = out + lam * dot(q, state)
            total = total + lam * dot_nt(g, state)
        att_s[:, cols] = out.astype(BF16)
        tot_s[:, cols] = total.astype(BF16)
    finish(fc)
    oc = []
    x = lax.axis_index("x")
    part = WIDTH // XN
    for off in range(XN):
        xx = lax.rem(x + off, XN)
        for i in range(part // 256):
            cols = pl.ds(pl.multiple_of(xx * part + i * 256, 256), 256)
            rows = pl.ds(off * part + i * 256, 256)
            grad_s[rows, :] = dot_tn(a_s[:, cols], tot_s[...]).astype(BF16)
            to = outs[off].at[pl.ds(i * 256, 256), :]
            oc.append(pltpu.make_async_copy(grad_s.at[rows, :], to, osem.at[off * 2 + i]))
            oc[-1].start()
    finish(oc)


HBM = pl.BlockSpec(memory_space=pltpu.HBM)
VM = pl.BlockSpec(memory_space=pltpu.VMEM)


def struct(shape, dtype):
    return jax.ShapeDtypeStruct(shape, dtype)


def call(body, name, inputs, specs, outs, out_specs, scratch, flops, moved):
    return pl.pallas_call(
        body,
        name=name,
        in_specs=specs,
        out_specs=out_specs,
        out_shape=outs,
        scratch_shapes=scratch,
        compiler_params=pltpu.CompilerParams(vmem_limit_bytes=VMEM_LIMIT),
        cost_estimate=pl.CostEstimate(flops=flops, transcendentals=0, bytes_accessed=moved),
    )(*inputs)


def on_device(activations, w_query, w_key, w_value, level_table, table_rows, out_grad):
    x = lax.axis_index("x")
    z = lax.axis_index("z")

    low = jnp.array(-jnp.inf, BF16)
    weights = [
        lax.pad(w, low, ((0, 0, 0), (i * COLS, (2 - i) * COLS, 0)))
        for i, w in enumerate((w_query, w_key, w_value))
    ]
    weights = jnp.maximum(jnp.maximum(weights[0], weights[1]), weights[2])
    along = [weights] + [shifted(weights, "x", -off) for off in (1, 2, 3)]
    weights = lax.all_gather(jnp.concatenate(along, axis=0), "z", axis=0)

    feats = features_of(activations)
    ftags = [(off, same) for off, same, _ in feats]
    fparts = [part for _, _, part in feats]
    nf = len(ftags)

    scale = 1.0 / math.sqrt(HD * TOK)
    table_size = level_table.shape[1]
    onehot = (table_rows[:, None] == jnp.arange(table_size, dtype=jnp.int32)[None, :]).astype(F32)
    flat = jnp.transpose(level_table, (1, 0, 2)).reshape(table_size, HEADS_HERE * LEVELS)
    lam = scale * jnp.dot(onehot, flat, precision=lax.Precision.HIGHEST)

    dma = pltpu.SemaphoreType.DMA
    wide = pltpu.VMEM((TOK, WIDTH), BF16)
    block = pltpu.VMEM((TOK, COLS), BF16)
    state = (HEADS_HERE, HD, HD)

    queries, keys, values, local, s1, s2, s3, by_pair, by_one = call(
        functools.partial(projection_kernel, ftags),
        "projections",
        [*fparts, weights, out_grad, lam],
        [HBM] * (nf + 1) + [VM] * 2,
        [struct((TOK, COLS), BF16)] * 3
        + [struct(state, F32)]
        + [struct(state, BF16)] * 3
        + [struct((3, *state), F32), struct(state, F32)],
        [VM] * 9,
        [
            wide,
            pltpu.VMEM((WIDTH, 3 * COLS), BF16),
            dma((nf,)),
            dma((ZN, XN)),
        ],
        1 << 20,
        1 << 10,
    )

    def near_of(h, gate):
        first, *_ = lax.optimization_barrier((queries, *gate))
        return call(
            functools.partial(near_kernel, h),
            "near",
            [first, keys, values, out_grad, lam],
            [HBM] * 5,
            [struct((TOK, HD), F32)] * 4,
            [HBM] * 4,
            [pltpu.VMEM((TOK, HD), BF16)] * 4
            + [pltpu.VMEM((TOK, HEADS_HERE * LEVELS), F32)]
            + [pltpu.VMEM((TOK, HD), F32)] * 4
            + [dma((5, 2)), dma((4, TOK // 128))],
            2 << 30,
            8 << 20,
        )

    after_one = [shifted(part, "x", -off) for off, part in zip((1, 2, 3), (s1, s2, s3))]
    near = [near_of(0, [])]
    *after_one, _ = lax.optimization_barrier((*after_one, near[0][0]))
    pending = sum(part.astype(F32) for part in after_one)
    after_two = [
        shifted((pending + by_pair[i]).astype(BF16), "z", -2 * off) for i, off in enumerate((1, 2, 3))
    ]
    near.append(near_of(1, after_one))
    *after_two, _ = lax.optimization_barrier((*after_two, near[1][0]))
    pending = pending + sum(part.astype(F32) for part in after_two)
    pending = pending + swapped((pending + by_one).astype(BF16), "z", 1).astype(F32)

    none = jnp.zeros(state, BF16)

    def among_four(value, index, axis, stride):
        sent = value.astype(BF16)
        got = {off: shifted(sent, axis, off * stride) for off in (1, 2, 3)}
        full = {off: part.astype(F32) for off, part in got.items()}
        first = jnp.where((index & 1) != 0, got[1], none)
        other = full[2] + jnp.where(index == 2, full[1], full[3])
        second = jnp.where(index >= 2, other.astype(BF16), none)
        return first, second, value + full[1] + full[2] + full[3]

    local, *_ = lax.optimization_barrier((local, *after_one))
    sibling = swapped(local, "z", 1)
    state0 = jnp.where((z & 1) != 0, sibling, 0.0).astype(BF16)
    total = local + sibling
    near_out, query_near, key_near, value_near = (list(parts) for parts in zip(*near))

    total, *_ = lax.optimization_barrier((total, *after_two))
    sibling = swapped(total.astype(BF16), "z", 2)
    state1 = jnp.where((z & 2) != 0, sibling, none)
    total = total + sibling.astype(F32)
    (parts,) = call(
        functools.partial(key_value_grad_kernel, ftags),
        "key_value_grad",
        [*fparts, keys, values, *key_near, *value_near, pending],
        [HBM] * nf + [VM] * 7,
        [struct((WIDTH, 2 * COLS), BF16)],
        [HBM],
        [
            wide,
            pltpu.VMEM((TOK, 2 * COLS), BF16),
            pltpu.VMEM((WIDTH, 2 * COLS), BF16),
            dma((nf,)),
            dma((WIDTH // PIECE,)),
        ],
        8 << 30,
        8 << 20,
    )
    parts, total = lax.optimization_barrier((parts, total))
    sibling = swapped(total.astype(BF16), "z", 4)
    state2 = jnp.where((z & 4) != 0, sibling, none)
    total = total + sibling.astype(F32)
    state3, state4, total = among_four(total, x, "x", 1)
    states = [state0, state1, state2, state3, state4]
    kv_sum = lax.psum_scatter(parts, "z", scatter_dimension=0, tiled=True)

    query_near[0], _ = lax.optimization_barrier((query_near[0], parts))
    attended, *sums = call(
        functools.partial(query_grad_kernel, ftags),
        "query_grad",
        [*fparts, queries, out_grad, *near_out, *query_near, lam, *states],
        [HBM] * nf + [VM] * (7 + FAR),
        [struct((TOK, COLS), BF16)] + [struct((WIDTH // XN, COLS), BF16)] * XN,
        [VM] + [HBM] * XN,
        [
            wide,
            block,
            pltpu.VMEM((WIDTH, COLS), BF16),
            dma((nf,)),
            dma((ZN,)),
        ],
        8 << 30,
        8 << 20,
    )
    mine = sums[0].astype(F32)
    for off in (1, 2, 3):
        mine = mine + shifted(sums[off], "x", off).astype(F32)
    gathered = lax.all_to_all(mine.astype(BF16).reshape(ZN, PIECE, COLS), "z", 0, 0, tiled=True)
    grad_query = jnp.sum(gathered.astype(F32), axis=0)

    kv_sum = kv_sum.reshape(XN, PIECE, 2 * COLS)
    grad_kv = kv_sum[0].astype(F32)
    for off in (1, 2, 3):
        grad_kv = grad_kv + shifted(kv_sum[off], "x", off).astype(F32)
    return attended, grad_query, grad_kv[:, :COLS], grad_kv[:, COLS:]


def solution(mesh):
    finer = Mesh(mesh.devices.reshape(XN, ZN, YN, 2), ("x", "z", "y", "core"))
    rows, cols = ("x", "z"), ("y", "core")
    return jax.shard_map(
        on_device,
        mesh=finer,
        in_specs=(
            P(rows, cols),
            P(rows, cols),
            P(rows, cols),
            P(rows, cols),
            P(cols, None, None),
            P(rows),
            P(rows, cols),
        ),
        out_specs=(P(rows, cols), P(rows, cols), P(rows, cols), P(rows, cols)),
        check_vma=False,
    )
```

```python
import functools
import math

import jax
import jax.numpy as jnp
from jax import lax
from jax.experimental import pallas as pl
from jax.experimental.pallas import tpu as pltpu
from jax.sharding import Mesh
from jax.sharding import PartitionSpec as P

F32 = jnp.float32
BF16 = jnp.bfloat16
VMEM_LIMIT = 56 * 1024 * 1024

TOK = 1024
WIDTH = 2048
COLS = 256
HD = 128
HEADS_HERE = 2
LEVELS = 16
NEAR = 11
FAR = 5
XN, ZN, YN = 4, 8, 4
PIECE = WIDTH // (XN * ZN)


def shifted(value, axis, offset):
    count = lax.axis_size(axis)
    return lax.ppermute(value, axis, [(i, (i + offset) % count) for i in range(count)])


def swapped(value, axis, bit):
    count = lax.axis_size(axis)
    return lax.ppermute(value, axis, [(i, i ^ bit) for i in range(count)])


def features_of(block):
    mine = [(0, block)] + [(off, shifted(block, "y", -off)) for off in (1, -1, 2)]
    found = [(off, True, part) for off, part in mine]
    found += [(off, False, shifted(part, "core", 1)) for off, part in mine]
    return found


def dot(a, b):
    return lax.dot_general(a, b, (((1,), (0,)), ((), ())), preferred_element_type=F32)


def dot_nt(a, b):
    return lax.dot_general(a, b, (((1,), (1,)), ((), ())), preferred_element_type=F32)


def dot_tn(a, b):
    return lax.dot_general(a, b, (((0,), (0,)), ((), ())), preferred_element_type=F32)


def feature_copies(tags, refs, scratch, sem):
    y = lax.axis_index("y")
    core = lax.axis_index("core")
    copies = []
    for i, ((off, same), ref) in enumerate(zip(tags, refs)):
        block = lax.rem(y + (off + YN), YN) * 2 + (core if same else 1 - core)
        cols = pl.ds(pl.multiple_of(block * COLS, COLS), COLS)
        copies.append(pltpu.make_async_copy(ref, scratch.at[:, cols], sem.at[i]))
    return copies


def weight_copies(ref, scratch, sem):
    x = lax.axis_index("x")
    copies = []
    for z in range(ZN):
        for rx in range(XN):
            xx = lax.rem(x + rx, XN)
            rows = pl.ds(pl.multiple_of((xx * ZN + z) * PIECE, PIECE), PIECE)
            src = ref.at[z, pl.ds(rx * PIECE, PIECE), :]
            copies.append(pltpu.make_async_copy(src, scratch.at[rows, :], sem.at[z, rx]))
    return copies


def begin(copies):
    for copy in copies:
        copy.start()


def finish(copies):
    for copy in copies:
        copy.wait()


def projection_kernel(ftags, *refs):
    nf = len(ftags)
    fr = refs[:nf]
    w_ref, g_s, lam_s, q_s, k_s, v_s, local_ref = refs[nf : nf + 7]
    send_refs = refs[nf + 7 : nf + 10]
    pair_ref, one_ref = refs[nf + 10 : nf + 12]
    a_s, w_s, fsem, wsem = refs[nf + 12 :]
    fc = feature_copies(ftags, fr, a_s, fsem)
    wc = weight_copies(w_ref, w_s, wsem)
    begin(wc + fc)
    finish(wc + fc)
    step = 256
    for r in range(0, TOK, step):
        rows = pl.ds(r, step)
        both = dot(a_s[rows, :], w_s[...]).astype(BF16)
        for i, held in enumerate((q_s, k_s, v_s)):
            held[rows, :] = both[:, i * COLS : (i + 1) * COLS]
    x = lax.axis_index("x")
    pair = lax.div(lax.axis_index("z"), 2)
    low = lax.rem(lax.axis_index("z"), 2)
    for h in range(HEADS_HERE):
        cols = pl.ds(h * HD, HD)
        q = q_s[:, cols].astype(F32)
        g = g_s[:, cols]
        states = []
        for b in range(FAR):
            at = h * LEVELS + NEAR + b
            states.append(dot_tn((lam_s[:, at : at + 1] * q).astype(BF16), g))
        local_ref[h] = dot_tn(k_s[:, cols], v_s[:, cols])
        one_ref[h] = jnp.where(low == 1, states[0], 0.0)
        for i, off in enumerate((1, 2, 3)):
            to = lax.rem(pair + (4 - off), 4)
            sibling = lax.div(pair, 2) == lax.div(to, 2)
            pair_ref[i, h] = jnp.where(to < pair, jnp.where(sibling, states[1], states[2]), 0.0)
            to = lax.rem(x + (XN - off), XN)
            sibling = lax.div(x, 2) == lax.div(to, 2)
            level = jnp.where(to < x, jnp.where(sibling, states[3], states[4]), 0.0)
            send_refs[i][h] = level.astype(BF16)


def near_kernel(h, *refs):
    ins, lam_ref, outs = refs[:4], refs[4], refs[5:9]
    held = refs[9:13]
    lam_s, sums = refs[13], refs[14:18]
    isem, osem = refs[18:]
    q_s, k_s, v_s, g_s = held
    cols = pl.ds(h * HD, HD)
    half = TOK // 2
    copies = {}
    for name, i, part in (
        ("k0", 1, 0),
        ("v0", 2, 0),
        ("q1", 0, 1),
        ("g1", 3, 1),
        ("k1", 1, 1),
        ("v1", 2, 1),
        ("q0", 0, 0),
        ("g0", 3, 0),
    ):
        rows = pl.ds(part * half, half)
        copies[name] = pltpu.make_async_copy(ins[i].at[rows, cols], held[i].at[rows, :], isem.at[i, part])
    lam_copy = pltpu.make_async_copy(lam_ref, lam_s, isem.at[4, 0])
    early_ones = [copies[name] for name in ("k0", "v0", "q1", "g1")]
    late_ones = [copies[name] for name in ("k1", "v1", "q0", "g0")]
    begin([*early_ones[:2], lam_copy, *early_ones[2:], *late_ones])
    tile = 128
    t_at = lax.broadcasted_iota(jnp.int32, (tile, tile), 0)
    s_at = lax.broadcasted_iota(jnp.int32, (tile, tile), 1)
    apart = jnp.bitwise_xor(t_at, s_at)
    causal = t_at >= s_at
    begun = [set(), set(), set(), set()]

    def add(which, start, value):
        for i in range(value.shape[0] // tile):
            at = start + i * tile
            rows = pl.ds(at, tile)
            piece = value[i * tile : (i + 1) * tile, :]
            if at in begun[which]:
                piece = sums[which][rows, :] + piece
            begun[which].add(at)
            sums[which][rows, :] = piece

    finish([*early_ones, lam_copy])
    for level in reversed(range(8, NEAR)):
        size = tile << (level - 8)
        for at in range(0, TOK, 2 * size):
            early, late = pl.ds(at, size), pl.ds(at + size, size)
            k, v = k_s[early, :], v_s[early, :]
            q, g = q_s[late, :], g_s[late, :]
            lam = lam_s[late, h * LEVELS + level : h * LEVELS + level + 1]
            state = dot_tn(k, v).astype(BF16)
            back = dot_tn((lam * q.astype(F32)).astype(BF16), g).astype(BF16)
            add(0, at + size, lam * dot(q, state))
            add(1, at + size, lam * dot_nt(g, state))
            add(2, at, dot_nt(v, back))
            add(3, at, dot(k, back))
        if level == NEAR - 1:
            finish(late_ones)
    oc = []
    for i in range(TOK // tile):
        rows = pl.ds(i * tile, tile)
        q, k, v, g = q_s[rows, :], k_s[rows, :], v_s[rows, :], g_s[rows, :]
        lam = lam_s[rows, pl.ds(h * LEVELS, LEVELS)]
        mix = jnp.broadcast_to(lam[:, 0:1], (tile, tile))
        for level in range(1, 8):
            mix = jnp.where(apart >= 1 << (level - 1), lam[:, level : level + 1], mix)
        mix = jnp.where(causal, mix, 0.0)
        probs = (mix * dot_nt(q, k)).astype(BF16)
        mixed = (mix * dot_nt(g, v)).astype(BF16)
        add(0, i * tile, dot(probs, v))
        add(1, i * tile, dot(mixed, k))
        add(2, i * tile, dot_tn(mixed, q))
        add(3, i * tile, dot_tn(probs, g))
        for which in range(4):
            src, to = sums[which].at[rows, :], outs[which].at[rows, :]
            oc.append(pltpu.make_async_copy(src, to, osem.at[which, i]))
            oc[-1].start()
    finish(oc)


def key_value_grad_kernel(ftags, *refs):
    nf = len(ftags)
    fr = refs[:nf]
    k_s, v_s, dk0, dk1, dv0, dv1, back_ref, parts_ref = refs[nf : nf + 8]
    a_s, tot_s, grad_s, fsem, osem = refs[nf + 8 :]
    fc = feature_copies(ftags, fr, a_s, fsem)
    begin(fc)
    for h in range(HEADS_HERE):
        cols = pl.ds(h * HD, HD)
        back = back_ref[h].astype(BF16)
        tot_s[:, cols] = ((dk0, dk1)[h][...] + dot_nt(v_s[:, cols], back)).astype(BF16)
        tot_s[:, pl.ds(COLS + h * HD, HD)] = ((dv0, dv1)[h][...] + dot(k_s[:, cols], back)).astype(BF16)
    finish(fc)
    x = lax.axis_index("x")
    oc = []
    for r in range(0, WIDTH, 256):
        grad_s[pl.ds(r, 256), :] = dot_tn(a_s[:, pl.ds(r, 256)], tot_s[...]).astype(BF16)
        xx = r // (ZN * PIECE)
        rx = lax.rem(xx + (XN - x), XN)
        for i in range(256 // PIECE):
            z = r % (ZN * PIECE) // PIECE + i
            to = pl.ds(pl.multiple_of((z * XN + rx) * PIECE, PIECE), PIECE)
            src = grad_s.at[pl.ds(r + i * PIECE, PIECE), :]
            oc.append(pltpu.make_async_copy(src, parts_ref.at[to, :], osem.at[r // PIECE + i]))
            oc[-1].start()
    finish(oc)


def attended_kernel(q_s, near0, near1, lam_s, *refs):
    state_refs, att_ref = refs[:FAR], refs[FAR]
    for h in range(HEADS_HERE):
        cols = pl.ds(h * HD, HD)
        q = q_s[:, cols]
        out = (near0, near1)[h][...]
        for b in range(FAR):
            at = h * LEVELS + NEAR + b
            out = out + lam_s[:, at : at + 1] * dot(q, state_refs[b][h])
        att_ref[:, cols] = out.astype(BF16)


def query_grad_kernel(ftags, *refs):
    nf = len(ftags)
    fr = refs[:nf]
    g_s, dq0, dq1, lam_s = refs[nf : nf + 4]
    state_refs = refs[nf + 4 : nf + 4 + FAR]
    outs = refs[nf + 4 + FAR : nf + 4 + FAR + XN]
    a_s, tot_s, grad_s, fsem, osem = refs[nf + 4 + FAR + XN :]
    fc = feature_copies(ftags, fr, a_s, fsem)
    begin(fc)
    for h in range(HEADS_HERE):
        cols = pl.ds(h * HD, HD)
        g = g_s[:, cols]
        total = (dq0, dq1)[h][...]
        for b in range(FAR):
            at = h * LEVELS + NEAR + b
            lam = lam_s[:, at : at + 1]
            total = total + lam * dot_nt(g, state_refs[b][h])
        tot_s[:, cols] = total.astype(BF16)
    finish(fc)
    oc = []
    x = lax.axis_index("x")
    part = WIDTH // XN
    for off in range(XN):
        xx = lax.rem(x + off, XN)
        for i in range(part // 256):
            cols = pl.ds(pl.multiple_of(xx * part + i * 256, 256), 256)
            rows = pl.ds(off * part + i * 256, 256)
            grad_s[rows, :] = dot_tn(a_s[:, cols], tot_s[...]).astype(BF16)
            to = outs[off].at[pl.ds(i * 256, 256), :]
            oc.append(pltpu.make_async_copy(grad_s.at[rows, :], to, osem.at[off * 2 + i]))
            oc[-1].start()
    finish(oc)


HBM = pl.BlockSpec(memory_space=pltpu.HBM)
VM = pl.BlockSpec(memory_space=pltpu.VMEM)


def struct(shape, dtype):
    return jax.ShapeDtypeStruct(shape, dtype)


def call(body, name, inputs, specs, outs, out_specs, scratch, flops, moved):
    return pl.pallas_call(
        body,
        name=name,
        in_specs=specs,
        out_specs=out_specs,
        out_shape=outs,
        scratch_shapes=scratch,
        compiler_params=pltpu.CompilerParams(vmem_limit_bytes=VMEM_LIMIT),
        cost_estimate=pl.CostEstimate(flops=flops, transcendentals=0, bytes_accessed=moved),
    )(*inputs)


def on_device(activations, w_query, w_key, w_value, level_table, table_rows, out_grad):
    x = lax.axis_index("x")
    z = lax.axis_index("z")

    low = jnp.array(-jnp.inf, BF16)
    weights = [
        lax.pad(w, low, ((0, 0, 0), (i * COLS, (2 - i) * COLS, 0)))
        for i, w in enumerate((w_query, w_key, w_value))
    ]
    weights = jnp.maximum(jnp.maximum(weights[0], weights[1]), weights[2])
    along = [weights] + [shifted(weights, "x", -off) for off in (1, 2, 3)]
    weights = lax.all_gather(jnp.concatenate(along, axis=0), "z", axis=0)

    feats = features_of(activations)
    ftags = [(off, same) for off, same, _ in feats]
    fparts = [part for _, _, part in feats]
    nf = len(ftags)

    scale = 1.0 / math.sqrt(HD * TOK)
    table_size = level_table.shape[1]
    onehot = (table_rows[:, None] == jnp.arange(table_size, dtype=jnp.int32)[None, :]).astype(F32)
    flat = jnp.transpose(level_table, (1, 0, 2)).reshape(table_size, HEADS_HERE * LEVELS)
    lam = scale * jnp.dot(onehot, flat, precision=lax.Precision.HIGHEST)

    dma = pltpu.SemaphoreType.DMA
    wide = pltpu.VMEM((TOK, WIDTH), BF16)
    block = pltpu.VMEM((TOK, COLS), BF16)
    state = (HEADS_HERE, HD, HD)

    queries, keys, values, local, s1, s2, s3, by_pair, by_one = call(
        functools.partial(projection_kernel, ftags),
        "projections",
        [*fparts, weights, out_grad, lam],
        [HBM] * (nf + 1) + [VM] * 2,
        [struct((TOK, COLS), BF16)] * 3
        + [struct(state, F32)]
        + [struct(state, BF16)] * 3
        + [struct((3, *state), F32), struct(state, F32)],
        [VM] * 9,
        [
            wide,
            pltpu.VMEM((WIDTH, 3 * COLS), BF16),
            dma((nf,)),
            dma((ZN, XN)),
        ],
        1 << 20,
        1 << 10,
    )

    def near_of(h, gate):
        first, *_ = lax.optimization_barrier((queries, *gate))
        return call(
            functools.partial(near_kernel, h),
            "near",
            [first, keys, values, out_grad, lam],
            [HBM] * 5,
            [struct((TOK, HD), F32)] * 4,
            [HBM] * 4,
            [pltpu.VMEM((TOK, HD), BF16)] * 4
            + [pltpu.VMEM((TOK, HEADS_HERE * LEVELS), F32)]
            + [pltpu.VMEM((TOK, HD), F32)] * 4
            + [dma((5, 2)), dma((4, TOK // 128))],
            2 << 30,
            8 << 20,
        )

    after_one = [shifted(part, "x", -off) for off, part in zip((1, 2, 3), (s1, s2, s3))]
    near = [near_of(0, [])]
    *after_one, _ = lax.optimization_barrier((*after_one, near[0][0]))
    pending = sum(part.astype(F32) for part in after_one)
    after_two = [
        shifted((pending + by_pair[i]).astype(BF16), "z", -2 * off) for i, off in enumerate((1, 2, 3))
    ]
    near.append(near_of(1, after_one))
    *after_two, _ = lax.optimization_barrier((*after_two, near[1][0]))
    pending = pending + sum(part.astype(F32) for part in after_two)
    pending = pending + swapped((pending + by_one).astype(BF16), "z", 1).astype(F32)

    none = jnp.zeros(state, BF16)

    def among_four(value, index, axis, stride):
        sent = value.astype(BF16)
        got = {off: shifted(sent, axis, off * stride) for off in (1, 2, 3)}
        full = {off: part.astype(F32) for off, part in got.items()}
        first = jnp.where((index & 1) != 0, got[1], none)
        other = full[2] + jnp.where(index == 2, full[1], full[3])
        second = jnp.where(index >= 2, other.astype(BF16), none)
        return first, second, value + full[1] + full[2] + full[3]

    local, *_ = lax.optimization_barrier((local, *after_one))
    sibling = swapped(local, "z", 1)
    state0 = jnp.where((z & 1) != 0, sibling, 0.0).astype(BF16)
    total = local + sibling
    near_out, query_near, key_near, value_near = (list(parts) for parts in zip(*near))

    total, *_ = lax.optimization_barrier((total, *after_two))
    sibling = swapped(total.astype(BF16), "z", 2)
    state1 = jnp.where((z & 2) != 0, sibling, none)
    total = total + sibling.astype(F32)
    (parts,) = call(
        functools.partial(key_value_grad_kernel, ftags),
        "key_value_grad",
        [*fparts, keys, values, *key_near, *value_near, pending],
        [HBM] * nf + [VM] * 7,
        [struct((WIDTH, 2 * COLS), BF16)],
        [HBM],
        [
            wide,
            pltpu.VMEM((TOK, 2 * COLS), BF16),
            pltpu.VMEM((WIDTH, 2 * COLS), BF16),
            dma((nf,)),
            dma((WIDTH // PIECE,)),
        ],
        8 << 30,
        8 << 20,
    )
    parts, total = lax.optimization_barrier((parts, total))
    sibling = swapped(total.astype(BF16), "z", 4)
    state2 = jnp.where((z & 4) != 0, sibling, none)
    total = total + sibling.astype(F32)
    state3, state4, total = among_four(total, x, "x", 1)
    states = [state0, state1, state2, state3, state4]
    kv_sum = lax.psum_scatter(parts, "z", scatter_dimension=0, tiled=True)

    query_near[0], _ = lax.optimization_barrier((query_near[0], parts))
    sums = call(
        functools.partial(query_grad_kernel, ftags),
        "query_grad",
        [*fparts, out_grad, *query_near, lam, *states],
        [HBM] * nf + [VM] * (4 + FAR),
        [struct((WIDTH // XN, COLS), BF16)] * XN,
        [HBM] * XN,
        [
            wide,
            block,
            pltpu.VMEM((WIDTH, COLS), BF16),
            dma((nf,)),
            dma((ZN,)),
        ],
        8 << 30,
        8 << 20,
    )
    first, *_ = lax.optimization_barrier((queries, sums[0]))
    (attended,) = call(
        attended_kernel,
        "attended",
        [first, *near_out, lam, *states],
        [VM] * (4 + FAR),
        [struct((TOK, COLS), BF16)],
        [VM],
        [],
        2 << 30,
        8 << 20,
    )
    mine = sums[0].astype(F32)
    for off in (1, 2, 3):
        mine = mine + shifted(sums[off], "x", off).astype(F32)
    gathered = lax.all_to_all(mine.astype(BF16).reshape(ZN, PIECE, COLS), "z", 0, 0, tiled=True)
    grad_query = jnp.sum(gathered.astype(F32), axis=0)

    kv_sum = kv_sum.reshape(XN, PIECE, 2 * COLS)
    grad_kv = kv_sum[0].astype(F32)
    for off in (1, 2, 3):
        grad_kv = grad_kv + shifted(kv_sum[off], "x", off).astype(F32)
    return attended, grad_query, grad_kv[:, :COLS], grad_kv[:, COLS:]


def solution(mesh):
    finer = Mesh(mesh.devices.reshape(XN, ZN, YN, 2), ("x", "z", "y", "core"))
    rows, cols = ("x", "z"), ("y", "core")
    return jax.shard_map(
        on_device,
        mesh=finer,
        in_specs=(
            P(rows, cols),
            P(rows, cols),
            P(rows, cols),
            P(rows, cols),
            P(cols, None, None),
            P(rows),
            P(rows, cols),
        ),
        out_specs=(P(rows, cols), P(rows, cols), P(rows, cols), P(rows, cols)),
        check_vma=False,
    )
```
